512 devices in a mesh: rep: 8 (over z_hi, core), ty: 16 (over z_lo, y), tx: 4 (over x).
Axes of the slice: x: 4, y: 8, z: 8 (z_hi: 4, z_lo: 2; z = z_hi * 2 + z_lo), core: 2. Of those that a mesh axis runs over, the one named last changes fastest.
Arguments:
- tokens: bfloat16 [8, 1024, 16, 512], P('rep', 'ty', 'tx'), may hold values from -160 to 160
- qkv_weight: bfloat16 [512, 1536], replicated, may hold values from -16 to 16
- cotangent: bfloat16 [8, 1024, 16, 512], P('rep', 'ty', 'tx'), may hold values from -6 to 6
Outputs:
- token_grad: bfloat16 [8, 1024, 16, 512], P('rep', 'ty', 'tx')
- weight_grad: float32 [512, 1536], P(('ty', 'tx'))
The draws below stay inside these ranges and needn't reach their ends.
All inputs are finite; a program needn't handle non-finite values.
Results may differ from the reference program's by a relative error of at most 0.024.
Values may be sent and summed in bfloat16 or wider, within the bound.
A program may use at most 64 MiB of HBM per device.

```python
import math
import jax
import jax.numpy as jnp
from jax import lax

D = 512
HEADS = 16
HEAD_DIM = 32
GRID = 8
TH = 64
TW = 4
REPS = 8
HEIGHT = 1024
WIDTH = 16
N_REP = 8
N_TY = 16
N_TX = 4


def draw_tokens(key, part):
    key_list = jax.random.split(key, 4)
    full_shape = (REPS, HEIGHT, WIDTH, D)
    base_draw = jax.random.truncated_normal(key_list[0], -4.0, 4.0, full_shape, jnp.float32)
    log_low = math.log(0.3)
    log_high = math.log(3.0)
    pixel_scale = jnp.exp(jax.random.uniform(key_list[1], (REPS, HEIGHT, WIDTH, 1), jnp.float32, log_low, log_high))
    channel_scale = jnp.exp(jax.random.uniform(key_list[2], (1, 1, 1, D), jnp.float32, log_low, log_high))
    tile_total = HEIGHT // TH * (WIDTH // TW)
    tile_ids = (jnp.arange(HEIGHT) // TH)[:, None] * (WIDTH // TW) + (jnp.arange(WIDTH) // TW)[None, :]
    orders = jax.vmap(lambda subkey: jax.random.permutation(subkey, tile_total))(jax.random.split(key_list[3], REPS))
    targets = orders[:, tile_ids]
    blocks = jnp.arange(D) // (D // tile_total)
    boost_factor = jnp.where(targets[..., None] == blocks, 4.0, 1.0)
    values = base_draw * pixel_scale * channel_scale * boost_factor
    return values.astype(jnp.bfloat16)


def draw_qkv_weight(key, part):
    key_list = jax.random.split(key, 1)
    return (jax.random.truncated_normal(key_list[0], -3.0, 3.0, (D, 3 * D), jnp.float32) * D ** (-0.5)).astype(jnp.bfloat16)


def block_levels(key, dims, pieces, low, top_value):
    loudness = 1.0
    for dim, blocks in pieces:
        steps = jax.random.uniform(jax.random.fold_in(jax.random.fold_in(key, 6), dim), (blocks,), jnp.float32, low / len(pieces), top_value / len(pieces))
        loudness = loudness * jnp.repeat(jnp.exp(steps), dims[dim] // blocks).reshape((-1,) + (1,) * (len(dims) - 1 - dim))
    return loudness


def scatter_about(rng, extent, width, bound, cuts=(), dtype=jnp.bfloat16):
    values = jax.random.normal(rng, extent, jnp.float32) * width
    if len(cuts) > 0:
        values = block_levels(rng, extent, cuts, -0.22, 0.18) * values
    return jnp.clip(values, min=-bound, max=bound).astype(dtype)


def setup_inputs(seed: int = 0) -> dict:
    arg_keys = jax.random.split(jax.random.key(seed), 4)
    return {
        "tokens": draw_tokens(jax.random.fold_in(arg_keys[3], 71), 0),
        "qkv_weight": draw_qkv_weight(jax.random.fold_in(arg_keys[3], 71), 0),
        "cotangent": scatter_about(arg_keys[2], (REPS, HEIGHT, WIDTH, D), 1.0, 6.0, ((0, 8), (1, 16), (2, 4))),
    }


eps_norm = 1e-05

def normalize(values):
    center = values - lax.optimization_barrier(jnp.mean(values, axis=-1, keepdims=True))
    inv_std = lax.rsqrt(lax.optimization_barrier(jnp.mean(center * center, axis=-1, keepdims=True)) + eps_norm)
    return (center * inv_std, inv_std)

def window_grads(window_x, window_g, qkv_weight):
    win_count, win_tokens, channels = window_x.shape
    standard, inv_std = normalize(window_x.astype(jnp.float32))
    normed = standard.astype(jnp.bfloat16).reshape(win_count * win_tokens, channels)
    projection = jnp.dot(normed, qkv_weight, preferred_element_type=jnp.float32)
    head_shape = (win_count, win_tokens, HEADS, HEAD_DIM)
    query_heads = (projection[:, :channels] * HEAD_DIM ** (-0.5)).astype(jnp.bfloat16).reshape(head_shape)
    key_heads = projection[:, channels:2 * channels].astype(jnp.bfloat16).reshape(head_shape)
    value_heads = projection[:, 2 * channels:].astype(jnp.bfloat16).reshape(head_shape)
    query_wide = query_heads.astype(jnp.float32)
    key_wide = key_heads.astype(jnp.float32)
    value_wide = value_heads.astype(jnp.float32)
    scores = jnp.einsum('wqne,wkne->wnqk', query_wide, key_wide)
    peak_score = lax.optimization_barrier(jnp.max(scores, axis=-1, keepdims=True))
    exponent = jnp.exp(scores - peak_score)
    attn_probs = exponent / lax.optimization_barrier(jnp.sum(exponent, axis=-1, keepdims=True))
    probs_low = attn_probs.astype(jnp.bfloat16)
    grad_heads = window_g.astype(jnp.float32).reshape(head_shape)
    attn_grad = jnp.einsum('wqne,wkne->wnqk', grad_heads, value_wide)
    value_grad = jnp.einsum('wnqk,wqne->wkne', probs_low.astype(jnp.float32), grad_heads).astype(jnp.bfloat16)
    score_grad = (attn_probs * (attn_grad - lax.optimization_barrier(jnp.sum(attn_probs * attn_grad, axis=-1, keepdims=True)))).astype(jnp.bfloat16)
    score_wide = score_grad.astype(jnp.float32)
    query_grad = (jnp.einsum('wnqk,wkne->wqne', score_wide, key_wide) * HEAD_DIM ** (-0.5)).astype(jnp.bfloat16)
    key_grad = jnp.einsum('wnqk,wqne->wkne', score_wide, query_wide).astype(jnp.bfloat16)
    flat_shape = (win_count * win_tokens, channels)
    proj_grad = jnp.concatenate([query_grad.reshape(flat_shape), key_grad.reshape(flat_shape), value_grad.reshape(flat_shape)], axis=1)
    normed_grad = lax.dot_general(proj_grad, qkv_weight, (((1,), (1,)), ((), ())), preferred_element_type=jnp.float32)
    normed_grad = normed_grad.reshape(win_count, win_tokens, channels)
    weight_term = lax.dot_general(normed, proj_grad, (((0,), (0,)), ((), ())), preferred_element_type=jnp.float32)
    inner_term = normed_grad - lax.optimization_barrier(jnp.mean(normed_grad, axis=-1, keepdims=True)) - standard * lax.optimization_barrier(jnp.mean(normed_grad * standard, axis=-1, keepdims=True))
    token_grad = (window_g.astype(jnp.float32) + inv_std * inner_term).astype(jnp.bfloat16)
    return (token_grad, weight_term)

def reference(tokens, qkv_weight, cotangent):
    stride_rows = HEIGHT // GRID
    stride_cols = WIDTH // GRID

    def to_windows(values):
        return values.reshape(GRID, stride_rows, GRID, stride_cols, D).transpose(1, 3, 0, 2, 4).reshape(stride_rows * stride_cols, GRID * GRID, D)

    def from_windows(values):
        return values.reshape(stride_rows, stride_cols, GRID, GRID, D).transpose(2, 0, 3, 1, 4).reshape(HEIGHT, WIDTH, D)

    def one_sample(sample):
        sample_x, sample_g = sample
        grad_windows, weight_term = window_grads(to_windows(sample_x), to_windows(sample_g), qkv_weight)
        return (from_windows(grad_windows), weight_term)
    token_grad, weight_terms = lax.map(one_sample, (tokens, cotangent))
    weight_grad = lax.optimization_barrier(jnp.sum(weight_terms, axis=0)) / (N_REP * N_TY * N_TX)
    return (token_grad, weight_grad)
```

```python
import jax
import jax.numpy as jnp
from jax import lax
from jax.sharding import PartitionSpec as P

HEADS = 16
HEAD_DIM = 32
GRID = 8


eps_norm = 1e-05


def normalize(values):
    center = values - jnp.mean(values, axis=-1, keepdims=True)
    inv_std = lax.rsqrt(jnp.mean(center * center, axis=-1, keepdims=True) + eps_norm)
    return (center * inv_std, inv_std)


def window_grads(window_x, window_g, qkv_weight):
    win_count, win_tokens, channels = window_x.shape
    standard, inv_std = normalize(window_x.astype(jnp.float32))
    normed = standard.astype(jnp.bfloat16).reshape(win_count * win_tokens, channels)
    projection = jnp.dot(normed, qkv_weight, preferred_element_type=jnp.float32)
    head_shape = (win_count, win_tokens, HEADS, HEAD_DIM)
    query_heads = (
        (projection[:, :channels] * HEAD_DIM ** (-0.5)).astype(jnp.bfloat16).reshape(head_shape)
    )
    key_heads = projection[:, channels : 2 * channels].astype(jnp.bfloat16).reshape(head_shape)
    value_heads = projection[:, 2 * channels :].astype(jnp.bfloat16).reshape(head_shape)
    scores = jnp.einsum(
        "wqne,wkne->wnqk", query_heads, key_heads, preferred_element_type=jnp.float32
    )
    peak_score = jnp.max(scores, axis=-1, keepdims=True)
    exponent = jnp.exp(scores - peak_score)
    attn_probs = exponent / jnp.sum(exponent, axis=-1, keepdims=True)
    probs_low = attn_probs.astype(jnp.bfloat16)
    grad_heads = window_g.reshape(head_shape)
    attn_grad = jnp.einsum(
        "wqne,wkne->wnqk", grad_heads, value_heads, preferred_element_type=jnp.float32
    )
    value_grad = jnp.einsum(
        "wnqk,wqne->wkne", probs_low, grad_heads, preferred_element_type=jnp.float32
    ).astype(jnp.bfloat16)
    score_grad = (
        attn_probs * (attn_grad - jnp.sum(attn_probs * attn_grad, axis=-1, keepdims=True))
    ).astype(jnp.bfloat16)
    query_grad = (
        jnp.einsum("wnqk,wkne->wqne", score_grad, key_heads, preferred_element_type=jnp.float32)
        * HEAD_DIM ** (-0.5)
    ).astype(jnp.bfloat16)
    key_grad = jnp.einsum(
        "wnqk,wqne->wkne", score_grad, query_heads, preferred_element_type=jnp.float32
    ).astype(jnp.bfloat16)
    flat_shape = (win_count * win_tokens, channels)
    proj_grad = jnp.concatenate(
        [
            query_grad.reshape(flat_shape),
            key_grad.reshape(flat_shape),
            value_grad.reshape(flat_shape),
        ],
        axis=1,
    )
    normed_grad = lax.dot_general(
        proj_grad, qkv_weight, (((1,), (1,)), ((), ())), preferred_element_type=jnp.float32
    )
    normed_grad = normed_grad.reshape(win_count, win_tokens, channels)
    weight_term = lax.dot_general(
        normed, proj_grad, (((0,), (0,)), ((), ())), preferred_element_type=jnp.float32
    )
    inner_term = (
        normed_grad
        - jnp.mean(normed_grad, axis=-1, keepdims=True)
        - standard * jnp.mean(normed_grad * standard, axis=-1, keepdims=True)
    )
    token_grad = (window_g.astype(jnp.float32) + inv_std * inner_term).astype(jnp.bfloat16)
    return (token_grad, weight_term)


def shards(tokens, qkv_weight, cotangent):
    rep_count = lax.axis_size("rep")
    row_tiles = lax.axis_size("ty")
    col_tiles = lax.axis_size("tx")
    tile_count = row_tiles * col_tiles
    tile_height = tokens.shape[1]
    tile_width = tokens.shape[2]
    channels = tokens.shape[3]
    stride_rows = row_tiles * tile_height // GRID
    stride_cols = col_tiles * tile_width // GRID
    block_rows = min(tile_height, stride_rows)
    fold_rows = stride_rows // block_rows
    col_groups = tile_width // stride_cols
    outer_rows = tile_height // block_rows
    inner_rows = block_rows // tile_count
    split_shape = (outer_rows, tile_count, inner_rows, tile_width, channels)
    grid_x, grid_g = (
        lax.all_to_all(
            tokens.reshape(split_shape), ("ty", "tx"), split_axis=1, concat_axis=1, tiled=True
        ),
        lax.all_to_all(
            cotangent.reshape(split_shape), ("ty", "tx"), split_axis=1, concat_axis=1, tiled=True
        ),
    )
    token_shape = (
        outer_rows,
        row_tiles // fold_rows,
        fold_rows,
        col_tiles,
        inner_rows,
        col_groups,
        stride_cols,
        channels,
    )
    win_count = fold_rows * inner_rows * stride_cols

    def to_windows(values):
        return (
            values.reshape(token_shape)
            .transpose(2, 4, 6, 1, 0, 3, 5, 7)
            .reshape(win_count, GRID * GRID, channels)
        )

    grad_windows, weight_term = window_grads(to_windows(grid_x), to_windows(grid_g), qkv_weight)
    back_shape = (
        fold_rows,
        inner_rows,
        stride_cols,
        row_tiles // fold_rows,
        outer_rows,
        col_tiles,
        col_groups,
        channels,
    )
    spread = grad_windows.reshape(back_shape).transpose(4, 3, 0, 5, 1, 6, 2, 7).reshape(split_shape)
    returned = lax.all_to_all(spread, ("ty", "tx"), split_axis=1, concat_axis=1, tiled=True)
    token_grad = returned.reshape(1, tile_height, tile_width, channels)
    row_blocks = weight_term.reshape(tile_count, channels // tile_count, weight_term.shape[1])
    gathered = lax.all_to_all(
        row_blocks.astype(jnp.bfloat16), ("ty", "tx"), 0, 0, tiled=True
    )
    partial_rows = jnp.sum(gathered.astype(jnp.float32), axis=0)
    weight_grad = lax.psum(partial_rows, "rep")
    weight_grad = weight_grad / (rep_count * tile_count)
    return (token_grad, weight_grad)


def solution(mesh):
    placed = (P("rep", "ty", "tx", None), P(), P("rep", "ty", "tx", None))
    return jax.shard_map(
        shards,
        mesh=mesh,
        in_specs=placed,
        out_specs=(P("rep", "ty", "tx", None), P(("ty", "tx"), None)),
        check_vma=False,
    )
```

```python
import functools

import jax
import jax.numpy as jnp
from jax import lax
from jax.experimental import pallas as pl
from jax.experimental.pallas import tpu as pltpu
from jax.sharding import PartitionSpec as P

HEADS = 16
HEAD_DIM = 32
GRID = 8


eps_norm = 1e-05


def normalize(values):
    center = values - jnp.mean(values, axis=-1, keepdims=True)
    inv_std = lax.rsqrt(jnp.mean(center * center, axis=-1, keepdims=True) + eps_norm)
    return (center * inv_std, inv_std)


def window_grads(window_x, window_g, qkv_weight):
    win_count, win_tokens, channels = window_x.shape
    standard, inv_std = normalize(window_x.astype(jnp.float32))
    normed = standard.astype(jnp.bfloat16).reshape(win_count * win_tokens, channels)
    projection = jnp.dot(normed, qkv_weight, preferred_element_type=jnp.float32)
    head_shape = (win_count, win_tokens, HEADS, HEAD_DIM)
    query_heads = (
        (projection[:, :channels] * HEAD_DIM ** (-0.5)).astype(jnp.bfloat16).reshape(head_shape)
    )
    key_heads = projection[:, channels : 2 * channels].astype(jnp.bfloat16).reshape(head_shape)
    value_heads = projection[:, 2 * channels :].astype(jnp.bfloat16).reshape(head_shape)
    scores = jnp.einsum(
        "wqne,wkne->wnqk", query_heads, key_heads, preferred_element_type=jnp.float32
    )
    peak_score = jnp.max(scores, axis=-1, keepdims=True)
    exponent = jnp.exp(scores - peak_score)
    attn_probs = exponent / jnp.sum(exponent, axis=-1, keepdims=True)
    probs_low = attn_probs.astype(jnp.bfloat16)
    grad_heads = window_g.reshape(head_shape)
    attn_grad = jnp.einsum(
        "wqne,wkne->wnqk", grad_heads, value_heads, preferred_element_type=jnp.float32
    )
    value_grad = jnp.einsum(
        "wnqk,wqne->wkne", probs_low, grad_heads, preferred_element_type=jnp.float32
    ).astype(jnp.bfloat16)
    score_grad = (
        attn_probs * (attn_grad - jnp.sum(attn_probs * attn_grad, axis=-1, keepdims=True))
    ).astype(jnp.bfloat16)
    query_grad = (
        jnp.einsum("wnqk,wkne->wqne", score_grad, key_heads, preferred_element_type=jnp.float32)
        * HEAD_DIM ** (-0.5)
    ).astype(jnp.bfloat16)
    key_grad = jnp.einsum(
        "wnqk,wqne->wkne", score_grad, query_heads, preferred_element_type=jnp.float32
    ).astype(jnp.bfloat16)
    flat_shape = (win_count * win_tokens, channels)
    proj_grad = jnp.concatenate(
        [
            query_grad.reshape(flat_shape),
            key_grad.reshape(flat_shape),
            value_grad.reshape(flat_shape),
        ],
        axis=1,
    )
    normed_grad = lax.dot_general(
        proj_grad, qkv_weight, (((1,), (1,)), ((), ())), preferred_element_type=jnp.float32
    )
    normed_grad = normed_grad.reshape(win_count, win_tokens, channels)
    weight_term = lax.dot_general(
        normed, proj_grad, (((0,), (0,)), ((), ())), preferred_element_type=jnp.float32
    )
    inner_term = (
        normed_grad
        - jnp.mean(normed_grad, axis=-1, keepdims=True)
        - standard * jnp.mean(normed_grad * standard, axis=-1, keepdims=True)
    )
    token_grad = (window_g.astype(jnp.float32) + inv_std * inner_term).astype(jnp.bfloat16)
    return (token_grad, weight_term)


def rep_sum_kernel(rep_count, part_ref, out_ref, held, copy_sems, send_sems, recv_sems):
    me = lax.axis_index("rep")
    row = lax.axis_index("ty")
    col = lax.axis_index("tx")
    barrier = pltpu.get_barrier_semaphore()
    for step in range(1, rep_count):
        peer = lax.rem(me + step, rep_count)
        pl.semaphore_signal(
            barrier, inc=1, device_id=(peer, row, col), device_id_type=pl.DeviceIdType.MESH
        )
    pl.semaphore_wait(barrier, rep_count - 1)
    own = pltpu.make_async_copy(part_ref, held.at[me], copy_sems.at[0])
    own.start()
    copies = []
    for step in range(1, rep_count):
        peer = lax.rem(me + step, rep_count)
        copy = pltpu.make_async_remote_copy(
            src_ref=part_ref,
            dst_ref=held.at[me],
            send_sem=send_sems.at[step],
            recv_sem=recv_sems.at[step],
            device_id=(peer, row, col),
            device_id_type=pl.DeviceIdType.MESH,
        )
        copy.start()
        copies.append(copy)
    own.wait()
    for copy in copies:
        copy.wait()
    total = held[0]
    for source in range(1, rep_count):
        total = total + held[source]
    out_ref[...] = total


def rep_sum(partial_rows):
    rep_count = lax.axis_size("rep")
    return pl.pallas_call(
        functools.partial(rep_sum_kernel, rep_count),
        out_shape=jax.ShapeDtypeStruct(partial_rows.shape, partial_rows.dtype),
        in_specs=[pl.BlockSpec(memory_space=pltpu.VMEM)],
        out_specs=pl.BlockSpec(memory_space=pltpu.VMEM),
        scratch_shapes=[
            pltpu.VMEM((rep_count,) + partial_rows.shape, partial_rows.dtype),
            pltpu.SemaphoreType.DMA((1,)),
            pltpu.SemaphoreType.DMA((rep_count,)),
            pltpu.SemaphoreType.DMA((rep_count,)),
        ],
        compiler_params=pltpu.CompilerParams(collective_id=0, has_side_effects=True),
    )(partial_rows)


def shards(tokens, qkv_weight, cotangent):
    rep_count = lax.axis_size("rep")
    row_tiles = lax.axis_size("ty")
    col_tiles = lax.axis_size("tx")
    tile_count = row_tiles * col_tiles
    tile_height = tokens.shape[1]
    tile_width = tokens.shape[2]
    channels = tokens.shape[3]
    stride_rows = row_tiles * tile_height // GRID
    stride_cols = col_tiles * tile_width // GRID
    block_rows = min(tile_height, stride_rows)
    fold_rows = stride_rows // block_rows
    col_groups = tile_width // stride_cols
    outer_rows = tile_height // block_rows
    inner_rows = block_rows // tile_count
    split_shape = (outer_rows, tile_count, inner_rows, tile_width, channels)
    grid_x, grid_g = (
        lax.all_to_all(
            tokens.reshape(split_shape), ("ty", "tx"), split_axis=1, concat_axis=1, tiled=True
        ),
        lax.all_to_all(
            cotangent.reshape(split_shape), ("ty", "tx"), split_axis=1, concat_axis=1, tiled=True
        ),
    )
    token_shape = (
        outer_rows,
        row_tiles // fold_rows,
        fold_rows,
        col_tiles,
        inner_rows,
        col_groups,
        stride_cols,
        channels,
    )
    win_count = fold_rows * inner_rows * stride_cols

    def to_windows(values):
        return (
            values.reshape(token_shape)
            .transpose(2, 4, 6, 1, 0, 3, 5, 7)
            .reshape(win_count, GRID * GRID, channels)
        )

    grad_windows, weight_term = window_grads(to_windows(grid_x), to_windows(grid_g), qkv_weight)
    back_shape = (
        fold_rows,
        inner_rows,
        stride_cols,
        row_tiles // fold_rows,
        outer_rows,
        col_tiles,
        col_groups,
        channels,
    )
    spread = grad_windows.reshape(back_shape).transpose(4, 3, 0, 5, 1, 6, 2, 7).reshape(split_shape)
    returned = lax.all_to_all(spread, ("ty", "tx"), split_axis=1, concat_axis=1, tiled=True)
    token_grad = returned.reshape(1, tile_height, tile_width, channels)
    row_blocks = weight_term.reshape(tile_count, channels // tile_count, weight_term.shape[1])
    gathered = lax.all_to_all(
        row_blocks.astype(jnp.bfloat16), ("ty", "tx"), 0, 0, tiled=True
    )
    partial_rows = jnp.sum(gathered.astype(jnp.float32), axis=0)
    weight_grad = rep_sum(partial_rows)
    weight_grad = weight_grad / (rep_count * tile_count)
    return (token_grad, weight_grad)


def solution(mesh):
    placed = (P("rep", "ty", "tx", None), P(), P("rep", "ty", "tx", None))
    return jax.shard_map(
        shards,
        mesh=mesh,
        in_specs=placed,
        out_specs=(P("rep", "ty", "tx", None), P(("ty", "tx"), None)),
        check_vma=False,
    )
```

```python
import functools

import jax
import jax.numpy as jnp
from jax import lax
from jax.experimental import pallas as pl
from jax.experimental.pallas import tpu as pltpu
from jax.sharding import PartitionSpec as P

HEADS = 16
HEAD_DIM = 32
GRID = 8


eps_norm = 1e-05


def normalize(values):
    center = values - jnp.mean(values, axis=-1, keepdims=True)
    inv_std = lax.rsqrt(jnp.mean(center * center, axis=-1, keepdims=True) + eps_norm)
    return (center * inv_std, inv_std)


def window_grads(window_x, window_g, qkv_weight):
    win_count, win_tokens, channels = window_x.shape
    standard, inv_std = normalize(window_x.astype(jnp.float32))
    normed = standard.astype(jnp.bfloat16).reshape(win_count * win_tokens, channels)
    projection = jnp.dot(normed, qkv_weight, preferred_element_type=jnp.float32)
    head_shape = (win_count, win_tokens, HEADS, HEAD_DIM)
    query_heads = (
        (projection[:, :channels] * HEAD_DIM ** (-0.5)).astype(jnp.bfloat16).reshape(head_shape)
    )
    key_heads = projection[:, channels : 2 * channels].astype(jnp.bfloat16).reshape(head_shape)
    value_heads = projection[:, 2 * channels :].astype(jnp.bfloat16).reshape(head_shape)
    scores = jnp.einsum(
        "wqne,wkne->wnqk", query_heads, key_heads, preferred_element_type=jnp.float32
    )
    peak_score = jnp.max(scores, axis=-1, keepdims=True)
    exponent = jnp.exp(scores - peak_score)
    attn_probs = exponent / jnp.sum(exponent, axis=-1, keepdims=True)
    probs_low = attn_probs.astype(jnp.bfloat16)
    grad_heads = window_g.reshape(head_shape)
    attn_grad = jnp.einsum(
        "wqne,wkne->wnqk", grad_heads, value_heads, preferred_element_type=jnp.float32
    )
    value_grad = jnp.einsum(
        "wnqk,wqne->wkne", probs_low, grad_heads, preferred_element_type=jnp.float32
    ).astype(jnp.bfloat16)
    score_grad = (
        attn_probs * (attn_grad - jnp.sum(attn_probs * attn_grad, axis=-1, keepdims=True))
    ).astype(jnp.bfloat16)
    query_grad = (
        jnp.einsum("wnqk,wkne->wqne", score_grad, key_heads, preferred_element_type=jnp.float32)
        * HEAD_DIM ** (-0.5)
    ).astype(jnp.bfloat16)
    key_grad = jnp.einsum(
        "wnqk,wqne->wkne", score_grad, query_heads, preferred_element_type=jnp.float32
    ).astype(jnp.bfloat16)
    flat_shape = (win_count * win_tokens, channels)
    proj_grad = jnp.concatenate(
        [
            query_grad.reshape(flat_shape),
            key_grad.reshape(flat_shape),
            value_grad.reshape(flat_shape),
        ],
        axis=1,
    )
    normed_grad = lax.dot_general(
        proj_grad, qkv_weight, (((1,), (1,)), ((), ())), preferred_element_type=jnp.float32
    )
    normed_grad = normed_grad.reshape(win_count, win_tokens, channels)
    weight_term = lax.dot_general(
        normed, proj_grad, (((0,), (0,)), ((), ())), preferred_element_type=jnp.float32
    )
    inner_term = (
        normed_grad
        - jnp.mean(normed_grad, axis=-1, keepdims=True)
        - standard * jnp.mean(normed_grad * standard, axis=-1, keepdims=True)
    )
    token_grad = (window_g.astype(jnp.float32) + inv_std * inner_term).astype(jnp.bfloat16)
    return (token_grad, weight_term)


def weight_sum_kernel(rep_count, tile_count, col_tiles, blocks_ref, out_ref, arrived,
                      partial, held, send_sems, recv_sems, rep_send_sems, rep_recv_sems):
    me = lax.axis_index("rep")
    row = lax.axis_index("ty")
    col = lax.axis_index("tx")
    tile = row * col_tiles + col
    barrier = pltpu.get_barrier_semaphore()

    def tile_peer(step):
        peer = lax.rem(tile + step, tile_count)
        return (me, peer // col_tiles, lax.rem(peer, col_tiles))

    def rep_peer(step):
        return (lax.rem(me + step, rep_count), row, col)

    @pl.loop(1, tile_count)
    def _(step):
        pl.semaphore_signal(barrier, inc=1, device_id=tile_peer(step),
                            device_id_type=pl.DeviceIdType.MESH)

    @pl.loop(1, rep_count)
    def _(step):
        pl.semaphore_signal(barrier, inc=1, device_id=rep_peer(step),
                            device_id_type=pl.DeviceIdType.MESH)

    pl.semaphore_wait(barrier, tile_count + rep_count - 2)

    def tile_copy(step):
        peer = lax.rem(tile + step, tile_count)
        return pltpu.make_async_remote_copy(
            src_ref=blocks_ref.at[peer],
            dst_ref=arrived.at[tile],
            send_sem=send_sems.at[step],
            recv_sem=recv_sems.at[step],
            device_id=tile_peer(step),
            device_id_type=pl.DeviceIdType.MESH,
        )

    own = pltpu.make_async_copy(blocks_ref.at[tile], arrived.at[tile], send_sems.at[0])
    own.start()

    @pl.loop(1, tile_count)
    def _(step):
        tile_copy(step).start()

    own.wait()

    @pl.loop(1, tile_count)
    def _(step):
        tile_copy(step).wait()

    def add_source(source, total):
        return total + arrived[source].astype(jnp.float32)

    partial[...] = lax.fori_loop(
        0, tile_count, add_source, jnp.zeros(partial.shape, jnp.float32)
    )
    held[me] = partial[...]

    def rep_copy(step):
        return pltpu.make_async_remote_copy(
            src_ref=partial,
            dst_ref=held.at[me],
            send_sem=rep_send_sems.at[step],
            recv_sem=rep_recv_sems.at[step],
            device_id=rep_peer(step),
            device_id_type=pl.DeviceIdType.MESH,
        )

    @pl.loop(1, rep_count)
    def _(step):
        rep_copy(step).start()

    @pl.loop(1, rep_count)
    def _(step):
        rep_copy(step).wait()

    total = held[0]
    for source in range(1, rep_count):
        total = total + held[source]
    out_ref[...] = total


def weight_sum(row_blocks):
    rep_count = lax.axis_size("rep")
    col_tiles = lax.axis_size("tx")
    tile_count = row_blocks.shape[0]
    block_shape = row_blocks.shape[1:]
    return pl.pallas_call(
        functools.partial(weight_sum_kernel, rep_count, tile_count, col_tiles),
        out_shape=jax.ShapeDtypeStruct(block_shape, jnp.float32),
        in_specs=[pl.BlockSpec(memory_space=pltpu.VMEM)],
        out_specs=pl.BlockSpec(memory_space=pltpu.VMEM),
        scratch_shapes=[
            pltpu.VMEM(row_blocks.shape, row_blocks.dtype),
            pltpu.VMEM(block_shape, jnp.float32),
            pltpu.VMEM((rep_count,) + block_shape, jnp.float32),
            pltpu.SemaphoreType.DMA((tile_count,)),
            pltpu.SemaphoreType.DMA((tile_count,)),
            pltpu.SemaphoreType.DMA((rep_count,)),
            pltpu.SemaphoreType.DMA((rep_count,)),
        ],
        compiler_params=pltpu.CompilerParams(collective_id=0, has_side_effects=True),
    )(row_blocks)


def shards(tokens, qkv_weight, cotangent):
    rep_count = lax.axis_size("rep")
    row_tiles = lax.axis_size("ty")
    col_tiles = lax.axis_size("tx")
    tile_count = row_tiles * col_tiles
    tile_height = tokens.shape[1]
    tile_width = tokens.shape[2]
    channels = tokens.shape[3]
    stride_rows = row_tiles * tile_height // GRID
    stride_cols = col_tiles * tile_width // GRID
    block_rows = min(tile_height, stride_rows)
    fold_rows = stride_rows // block_rows
    col_groups = tile_width // stride_cols
    outer_rows = tile_height // block_rows
    inner_rows = block_rows // tile_count
    split_shape = (outer_rows, tile_count, inner_rows, tile_width, channels)
    grid_x, grid_g = (
        lax.all_to_all(
            tokens.reshape(split_shape), ("ty", "tx"), split_axis=1, concat_axis=1, tiled=True
        ),
        lax.all_to_all(
            cotangent.reshape(split_shape), ("ty", "tx"), split_axis=1, concat_axis=1, tiled=True
        ),
    )
    token_shape = (
        outer_rows,
        row_tiles // fold_rows,
        fold_rows,
        col_tiles,
        inner_rows,
        col_groups,
        stride_cols,
        channels,
    )
    win_count = fold_rows * inner_rows * stride_cols

    def to_windows(values):
        return (
            values.reshape(token_shape)
            .transpose(2, 4, 6, 1, 0, 3, 5, 7)
            .reshape(win_count, GRID * GRID, channels)
        )

    grad_windows, weight_term = window_grads(to_windows(grid_x), to_windows(grid_g), qkv_weight)
    back_shape = (
        fold_rows,
        inner_rows,
        stride_cols,
        row_tiles // fold_rows,
        outer_rows,
        col_tiles,
        col_groups,
        channels,
    )
    spread = grad_windows.reshape(back_shape).transpose(4, 3, 0, 5, 1, 6, 2, 7).reshape(split_shape)
    returned = lax.all_to_all(spread, ("ty", "tx"), split_axis=1, concat_axis=1, tiled=True)
    token_grad = returned.reshape(1, tile_height, tile_width, channels)
    row_blocks = weight_term.reshape(tile_count, channels // tile_count, weight_term.shape[1])
    weight_grad = weight_sum(row_blocks.astype(jnp.bfloat16))
    weight_grad = weight_grad / (rep_count * tile_count)
    return (token_grad, weight_grad)


def solution(mesh):
    placed = (P("rep", "ty", "tx", None), P(), P("rep", "ty", "tx", None))
    return jax.shard_map(
        shards,
        mesh=mesh,
        in_specs=placed,
        out_specs=(P("rep", "ty", "tx", None), P(("ty", "tx"), None)),
        check_vma=False,
    )
```

```python
import functools

import jax
import jax.numpy as jnp
from jax import lax
from jax.experimental import pallas as pl
from jax.experimental.pallas import tpu as pltpu
from jax.sharding import PartitionSpec as P

HEADS = 16
HEAD_DIM = 32
GRID = 8


eps_norm = 1e-05


def normalize(values):
    center = values - jnp.mean(values, axis=-1, keepdims=True)
    inv_std = lax.rsqrt(jnp.mean(center * center, axis=-1, keepdims=True) + eps_norm)
    return (center * inv_std, inv_std)


def window_grads(window_x, window_g, qkv_weight):
    win_count, win_tokens, channels = window_x.shape
    standard, inv_std = normalize(window_x.astype(jnp.float32))
    normed = standard.astype(jnp.bfloat16).reshape(win_count * win_tokens, channels)
    projection = jnp.dot(normed, qkv_weight, preferred_element_type=jnp.float32)
    flat_shape = (win_count, win_tokens, channels)
    query = (projection[:, :channels] * HEAD_DIM ** (-0.5)).astype(jnp.bfloat16).reshape(flat_shape)
    key = projection[:, channels : 2 * channels].astype(jnp.bfloat16).reshape(flat_shape)
    value = projection[:, 2 * channels :].astype(jnp.bfloat16).reshape(flat_shape)
    grad = window_g.astype(jnp.bfloat16)
    head_mask = (
        lax.broadcasted_iota(jnp.int32, (HEADS, channels), 1) // HEAD_DIM
        == lax.broadcasted_iota(jnp.int32, (HEADS, channels), 0)
    ).astype(jnp.bfloat16)

    def spread(values):
        return values[:, None, :, :] * head_mask[None, :, None, :]

    query_spread = spread(query)
    grad_spread = spread(grad)
    scores = jnp.einsum("wnqc,wkc->wnqk", query_spread, key, preferred_element_type=jnp.float32)
    peak_score = jnp.max(scores, axis=-1, keepdims=True)
    exponent = jnp.exp(scores - peak_score)
    attn_probs = exponent / jnp.sum(exponent, axis=-1, keepdims=True)
    probs_low = attn_probs.astype(jnp.bfloat16)
    attn_grad = jnp.einsum("wnqc,wkc->wnqk", grad_spread, value, preferred_element_type=jnp.float32)
    value_grad = jnp.einsum(
        "wnqk,wnqc->wkc", probs_low, grad_spread, preferred_element_type=jnp.float32
    ).astype(jnp.bfloat16)
    score_grad = (
        attn_probs * (attn_grad - jnp.sum(attn_probs * attn_grad, axis=-1, keepdims=True))
    ).astype(jnp.bfloat16)
    key_grad = jnp.einsum(
        "wnqk,wnqc->wkc", score_grad, query_spread, preferred_element_type=jnp.float32
    ).astype(jnp.bfloat16)
    query_full = jnp.einsum("wnqk,wkc->wnqc", score_grad, key, preferred_element_type=jnp.float32)
    query_grad = (
        jnp.sum(query_full * head_mask[None, :, None, :].astype(jnp.float32), axis=1)
        * HEAD_DIM ** (-0.5)
    ).astype(jnp.bfloat16)
    flat_shape = (win_count * win_tokens, channels)
    proj_grad = jnp.concatenate(
        [
            query_grad.reshape(flat_shape),
            key_grad.reshape(flat_shape),
            value_grad.reshape(flat_shape),
        ],
        axis=1,
    )
    normed_grad = lax.dot_general(
        proj_grad, qkv_weight, (((1,), (1,)), ((), ())), preferred_element_type=jnp.float32
    )
    normed_grad = normed_grad.reshape(win_count, win_tokens, channels)
    weight_term = lax.dot_general(
        normed, proj_grad, (((0,), (0,)), ((), ())), preferred_element_type=jnp.float32
    )
    inner_term = (
        normed_grad
        - jnp.mean(normed_grad, axis=-1, keepdims=True)
        - standard * jnp.mean(normed_grad * standard, axis=-1, keepdims=True)
    )
    token_grad = (window_g.astype(jnp.float32) + inv_std * inner_term).astype(jnp.bfloat16)
    return (token_grad, weight_term)


def weight_sum_kernel(rep_count, tile_count, col_tiles, blocks_ref, out_ref, arrived,
                      partial, held, send_sems, recv_sems, rep_send_sems, rep_recv_sems):
    me = lax.axis_index("rep")
    row = lax.axis_index("ty")
    col = lax.axis_index("tx")
    tile = row * col_tiles + col
    barrier = pltpu.get_barrier_semaphore()

    def tile_peer(step):
        peer = lax.rem(tile + step, tile_count)
        return (me, peer // col_tiles, lax.rem(peer, col_tiles))

    def rep_peer(step):
        return (lax.rem(me + step, rep_count), row, col)

    @pl.loop(1, tile_count)
    def _(step):
        pl.semaphore_signal(barrier, inc=1, device_id=tile_peer(step),
                            device_id_type=pl.DeviceIdType.MESH)

    @pl.loop(1, rep_count)
    def _(step):
        pl.semaphore_signal(barrier, inc=1, device_id=rep_peer(step),
                            device_id_type=pl.DeviceIdType.MESH)

    pl.semaphore_wait(barrier, tile_count + rep_count - 2)

    def tile_copy(step):
        peer = lax.rem(tile + step, tile_count)
        return pltpu.make_async_remote_copy(
            src_ref=blocks_ref.at[peer],
            dst_ref=arrived.at[tile],
            send_sem=send_sems.at[step],
            recv_sem=recv_sems.at[step],
            device_id=tile_peer(step),
            device_id_type=pl.DeviceIdType.MESH,
        )

    own = pltpu.make_async_copy(blocks_ref.at[tile], arrived.at[tile], send_sems.at[0])
    own.start()

    @pl.loop(1, tile_count)
    def _(step):
        tile_copy(step).start()

    own.wait()

    @pl.loop(1, tile_count)
    def _(step):
        tile_copy(step).wait()

    def add_source(source, total):
        return total + arrived[source].astype(jnp.float32)

    partial[...] = lax.fori_loop(
        0, tile_count, add_source, jnp.zeros(partial.shape, jnp.float32)
    )
    held[me] = partial[...]

    def rep_copy(step):
        return pltpu.make_async_remote_copy(
            src_ref=partial,
            dst_ref=held.at[me],
            send_sem=rep_send_sems.at[step],
            recv_sem=rep_recv_sems.at[step],
            device_id=rep_peer(step),
            device_id_type=pl.DeviceIdType.MESH,
        )

    @pl.loop(1, rep_count)
    def _(step):
        rep_copy(step).start()

    @pl.loop(1, rep_count)
    def _(step):
        rep_copy(step).wait()

    total = held[0]
    for source in range(1, rep_count):
        total = total + held[source]
    out_ref[...] = total


def weight_sum(row_blocks):
    rep_count = lax.axis_size("rep")
    col_tiles = lax.axis_size("tx")
    tile_count = row_blocks.shape[0]
    block_shape = row_blocks.shape[1:]
    return pl.pallas_call(
        functools.partial(weight_sum_kernel, rep_count, tile_count, col_tiles),
        out_shape=jax.ShapeDtypeStruct(block_shape, jnp.float32),
        in_specs=[pl.BlockSpec(memory_space=pltpu.VMEM)],
        out_specs=pl.BlockSpec(memory_space=pltpu.VMEM),
        scratch_shapes=[
            pltpu.VMEM(row_blocks.shape, row_blocks.dtype),
            pltpu.VMEM(block_shape, jnp.float32),
            pltpu.VMEM((rep_count,) + block_shape, jnp.float32),
            pltpu.SemaphoreType.DMA((tile_count,)),
            pltpu.SemaphoreType.DMA((tile_count,)),
            pltpu.SemaphoreType.DMA((rep_count,)),
            pltpu.SemaphoreType.DMA((rep_count,)),
        ],
        compiler_params=pltpu.CompilerParams(collective_id=0, has_side_effects=True),
    )(row_blocks)


def shards(tokens, qkv_weight, cotangent):
    rep_count = lax.axis_size("rep")
    row_tiles = lax.axis_size("ty")
    col_tiles = lax.axis_size("tx")
    tile_count = row_tiles * col_tiles
    tile_height = tokens.shape[1]
    tile_width = tokens.shape[2]
    channels = tokens.shape[3]
    stride_rows = row_tiles * tile_height // GRID
    stride_cols = col_tiles * tile_width // GRID
    block_rows = min(tile_height, stride_rows)
    fold_rows = stride_rows // block_rows
    col_groups = tile_width // stride_cols
    outer_rows = tile_height // block_rows
    inner_rows = block_rows // tile_count
    split_shape = (outer_rows, tile_count, inner_rows, tile_width, channels)
    grid_x, grid_g = (
        lax.all_to_all(
            tokens.reshape(split_shape), ("ty", "tx"), split_axis=1, concat_axis=1, tiled=True
        ),
        lax.all_to_all(
            cotangent.reshape(split_shape), ("ty", "tx"), split_axis=1, concat_axis=1, tiled=True
        ),
    )
    token_shape = (
        outer_rows,
        row_tiles // fold_rows,
        fold_rows,
        col_tiles,
        inner_rows,
        col_groups,
        stride_cols,
        channels,
    )
    win_count = fold_rows * inner_rows * stride_cols

    def to_windows(values):
        return (
            values.reshape(token_shape)
            .transpose(2, 4, 6, 1, 0, 3, 5, 7)
            .reshape(win_count, GRID * GRID, channels)
        )

    grad_windows, weight_term = window_grads(to_windows(grid_x), to_windows(grid_g), qkv_weight)
    back_shape = (
        fold_rows,
        inner_rows,
        stride_cols,
        row_tiles // fold_rows,
        outer_rows,
        col_tiles,
        col_groups,
        channels,
    )
    spread = grad_windows.reshape(back_shape).transpose(4, 3, 0, 5, 1, 6, 2, 7).reshape(split_shape)
    returned = lax.all_to_all(spread, ("ty", "tx"), split_axis=1, concat_axis=1, tiled=True)
    token_grad = returned.reshape(1, tile_height, tile_width, channels)
    row_blocks = weight_term.reshape(tile_count, channels // tile_count, weight_term.shape[1])
    weight_grad = weight_sum(row_blocks.astype(jnp.bfloat16))
    weight_grad = weight_grad / (rep_count * tile_count)
    return (token_grad, weight_grad)


def solution(mesh):
    placed = (P("rep", "ty", "tx", None), P(), P("rep", "ty", "tx", None))
    return jax.shard_map(
        shards,
        mesh=mesh,
        in_specs=placed,
        out_specs=(P("rep", "ty", "tx", None), P(("ty", "tx"), None)),
        check_vma=False,
    )
```

```python
import functools

import jax
import jax.numpy as jnp
from jax import lax
from jax.experimental import pallas as pl
from jax.experimental.pallas import tpu as pltpu
from jax.sharding import PartitionSpec as P

HEADS = 16
HEAD_DIM = 32
GRID = 8


eps_norm = 1e-05


def normalize(values):
    center = values - jnp.mean(values, axis=-1, keepdims=True)
    inv_std = lax.rsqrt(jnp.mean(center * center, axis=-1, keepdims=True) + eps_norm)
    return (center * inv_std, inv_std)


def window_grads(window_x, window_g, qkv_weight):
    win_count, win_tokens, channels = window_x.shape
    standard, inv_std = normalize(window_x.astype(jnp.float32))
    normed = standard.astype(jnp.bfloat16).reshape(win_count * win_tokens, channels)
    projection = jnp.dot(normed, qkv_weight, preferred_element_type=jnp.float32)
    flat_shape = (win_count, win_tokens, channels)
    query = (projection[:, :channels] * HEAD_DIM ** (-0.5)).astype(jnp.bfloat16).reshape(flat_shape)
    key = projection[:, channels : 2 * channels].astype(jnp.bfloat16).reshape(flat_shape)
    value = projection[:, 2 * channels :].astype(jnp.bfloat16).reshape(flat_shape)
    grad = window_g.astype(jnp.bfloat16)
    head_mask = (
        lax.broadcasted_iota(jnp.int32, (HEADS, channels), 1) // HEAD_DIM
        == lax.broadcasted_iota(jnp.int32, (HEADS, channels), 0)
    ).astype(jnp.bfloat16)

    def spread(values):
        return values[:, None, :, :] * head_mask[None, :, None, :]

    query_spread = spread(query)
    grad_spread = spread(grad)
    scores = jnp.einsum("wnqc,wkc->wnqk", query_spread, key, preferred_element_type=jnp.float32)
    peak_score = jnp.max(scores, axis=-1, keepdims=True)
    exponent = jnp.exp(scores - peak_score)
    attn_probs = exponent / jnp.sum(exponent, axis=-1, keepdims=True)
    probs_low = attn_probs.astype(jnp.bfloat16)
    attn_grad = jnp.einsum("wnqc,wkc->wnqk", grad_spread, value, preferred_element_type=jnp.float32)
    value_grad = jnp.einsum(
        "wnqk,wnqc->wkc", probs_low, grad_spread, preferred_element_type=jnp.float32
    ).astype(jnp.bfloat16)
    score_grad = (
        attn_probs * (attn_grad - jnp.sum(attn_probs * attn_grad, axis=-1, keepdims=True))
    ).astype(jnp.bfloat16)
    key_grad = jnp.einsum(
        "wnqk,wnqc->wkc", score_grad, query_spread, preferred_element_type=jnp.float32
    ).astype(jnp.bfloat16)
    query_full = jnp.einsum("wnqk,wkc->wnqc", score_grad, key, preferred_element_type=jnp.float32)
    query_grad = (
        jnp.sum(query_full * head_mask[None, :, None, :].astype(jnp.float32), axis=1)
        * HEAD_DIM ** (-0.5)
    ).astype(jnp.bfloat16)
    flat_shape = (win_count * win_tokens, channels)
    proj_grad = jnp.concatenate(
        [
            query_grad.reshape(flat_shape),
            key_grad.reshape(flat_shape),
            value_grad.reshape(flat_shape),
        ],
        axis=1,
    )
    normed_grad = lax.dot_general(
        proj_grad, qkv_weight, (((1,), (1,)), ((), ())), preferred_element_type=jnp.float32
    )
    normed_grad = normed_grad.reshape(win_count, win_tokens, channels)
    weight_term = lax.dot_general(
        normed, proj_grad, (((0,), (0,)), ((), ())), preferred_element_type=jnp.float32
    )
    inner_term = (
        normed_grad
        - jnp.mean(normed_grad, axis=-1, keepdims=True)
        - standard * jnp.mean(normed_grad * standard, axis=-1, keepdims=True)
    )
    token_grad = (window_g.astype(jnp.float32) + inv_std * inner_term).astype(jnp.bfloat16)
    return (token_grad, weight_term)


def weight_sum_kernel(rep_count, tile_count, col_tiles, blocks_ref, out_ref, arrived,
                      partial, held, send_sems, recv_sems, rep_send_sems, rep_recv_sems):
    me = lax.axis_index("rep")
    row = lax.axis_index("ty")
    col = lax.axis_index("tx")
    tile = row * col_tiles + col
    barrier = pltpu.get_barrier_semaphore()

    def tile_peer(step):
        peer = lax.rem(tile + step, tile_count)
        return (me, peer // col_tiles, lax.rem(peer, col_tiles))

    def rep_peer(step):
        return (lax.rem(me + step, rep_count), row, col)

    @pl.loop(1, tile_count)
    def _(step):
        pl.semaphore_signal(barrier, inc=1, device_id=tile_peer(step),
                            device_id_type=pl.DeviceIdType.MESH)

    @pl.loop(1, rep_count)
    def _(step):
        pl.semaphore_signal(barrier, inc=1, device_id=rep_peer(step),
                            device_id_type=pl.DeviceIdType.MESH)

    pl.semaphore_wait(barrier, tile_count + rep_count - 2)

    def tile_copy(step):
        peer = lax.rem(tile + step, tile_count)
        return pltpu.make_async_remote_copy(
            src_ref=blocks_ref.at[peer],
            dst_ref=arrived.at[tile],
            send_sem=send_sems.at[step],
            recv_sem=recv_sems.at[step],
            device_id=tile_peer(step),
            device_id_type=pl.DeviceIdType.MESH,
        )

    own = pltpu.make_async_copy(blocks_ref.at[tile], arrived.at[tile], send_sems.at[0])
    own.start()

    @pl.loop(1, tile_count)
    def _(step):
        tile_copy(step).start()

    own.wait()

    @pl.loop(1, tile_count)
    def _(step):
        tile_copy(step).wait()

    def add_source(source, total):
        return total + arrived[source].astype(jnp.float32)

    partial[...] = lax.fori_loop(
        0, tile_count, add_source, jnp.zeros(partial.shape, jnp.float32)
    )
    held[me] = partial[...]

    def rep_copy(step):
        return pltpu.make_async_remote_copy(
            src_ref=partial,
            dst_ref=held.at[me],
            send_sem=rep_send_sems.at[step],
            recv_sem=rep_recv_sems.at[step],
            device_id=rep_peer(step),
            device_id_type=pl.DeviceIdType.MESH,
        )

    @pl.loop(1, rep_count)
    def _(step):
        rep_copy(step).start()

    @pl.loop(1, rep_count)
    def _(step):
        rep_copy(step).wait()

    total = held[0]
    for source in range(1, rep_count):
        total = total + held[source]
    out_ref[...] = total


def weight_sum(row_blocks):
    rep_count = lax.axis_size("rep")
    col_tiles = lax.axis_size("tx")
    tile_count = row_blocks.shape[0]
    block_shape = row_blocks.shape[1:]
    return pl.pallas_call(
        functools.partial(weight_sum_kernel, rep_count, tile_count, col_tiles),
        out_shape=jax.ShapeDtypeStruct(block_shape, jnp.float32),
        in_specs=[pl.BlockSpec(memory_space=pltpu.VMEM)],
        out_specs=pl.BlockSpec(memory_space=pltpu.VMEM),
        scratch_shapes=[
            pltpu.VMEM(row_blocks.shape, row_blocks.dtype),
            pltpu.VMEM(block_shape, jnp.float32),
            pltpu.VMEM((rep_count,) + block_shape, jnp.float32),
            pltpu.SemaphoreType.DMA((tile_count,)),
            pltpu.SemaphoreType.DMA((tile_count,)),
            pltpu.SemaphoreType.DMA((rep_count,)),
            pltpu.SemaphoreType.DMA((rep_count,)),
        ],
        compiler_params=pltpu.CompilerParams(collective_id=0, has_side_effects=True),
    )(row_blocks)


def exchange_kernel(tile_count, col_tiles, tokens_ref, cot_ref, tokens_out, cot_out,
                    tokens_held, cot_held, send_sems, recv_sems, own_sems):
    me = lax.axis_index("rep")
    row = lax.axis_index("ty")
    col = lax.axis_index("tx")
    tile = row * col_tiles + col
    barrier = pltpu.get_barrier_semaphore()

    def tile_peer(step):
        peer = lax.rem(tile + step, tile_count)
        return (me, peer // col_tiles, lax.rem(peer, col_tiles))

    @pl.loop(1, tile_count)
    def _(step):
        pl.semaphore_signal(barrier, inc=1, device_id=tile_peer(step),
                            device_id_type=pl.DeviceIdType.MESH)

    pl.semaphore_wait(barrier, tile_count - 1)

    def tile_copies(step):
        peer = lax.rem(tile + step, tile_count)
        return [
            pltpu.make_async_remote_copy(
                src_ref=source.at[0, peer],
                dst_ref=held.at[tile],
                send_sem=send_sems.at[step, index],
                recv_sem=recv_sems.at[step, index],
                device_id=tile_peer(step),
                device_id_type=pl.DeviceIdType.MESH,
            )
            for index, (source, held) in enumerate(((tokens_ref, tokens_held), (cot_ref, cot_held)))
        ]

    own = [
        pltpu.make_async_copy(tokens_ref.at[0, tile], tokens_held.at[tile], own_sems.at[0]),
        pltpu.make_async_copy(cot_ref.at[0, tile], cot_held.at[tile], own_sems.at[1]),
    ]
    for copy in own:
        copy.start()

    @pl.loop(1, tile_count)
    def _(step):
        for copy in tile_copies(step):
            copy.start()

    for copy in own:
        copy.wait()

    @pl.loop(1, tile_count)
    def _(step):
        for copy in tile_copies(step):
            copy.wait()

    tokens_out[...] = tokens_held[...]
    cot_out[...] = cot_held[...]


def exchange(tokens, cotangent):
    col_tiles = lax.axis_size("tx")
    tile_count = lax.axis_size("ty") * col_tiles
    held_shape = (tile_count,) + tokens.shape[2:]
    return pl.pallas_call(
        functools.partial(exchange_kernel, tile_count, col_tiles),
        out_shape=[jax.ShapeDtypeStruct(held_shape, tokens.dtype)] * 2,
        in_specs=[pl.BlockSpec(memory_space=pltpu.VMEM)] * 2,
        out_specs=[pl.BlockSpec(memory_space=pltpu.VMEM)] * 2,
        scratch_shapes=[
            pltpu.VMEM(held_shape, tokens.dtype),
            pltpu.VMEM(held_shape, tokens.dtype),
            pltpu.SemaphoreType.DMA((tile_count, 2)),
            pltpu.SemaphoreType.DMA((tile_count, 2)),
            pltpu.SemaphoreType.DMA((2,)),
        ],
        compiler_params=pltpu.CompilerParams(collective_id=1, has_side_effects=True),
    )(tokens, cotangent)


def shards(tokens, qkv_weight, cotangent):
    rep_count = lax.axis_size("rep")
    row_tiles = lax.axis_size("ty")
    col_tiles = lax.axis_size("tx")
    tile_count = row_tiles * col_tiles
    tile_height = tokens.shape[1]
    tile_width = tokens.shape[2]
    channels = tokens.shape[3]
    stride_rows = row_tiles * tile_height // GRID
    stride_cols = col_tiles * tile_width // GRID
    block_rows = min(tile_height, stride_rows)
    fold_rows = stride_rows // block_rows
    col_groups = tile_width // stride_cols
    outer_rows = tile_height // block_rows
    inner_rows = block_rows // tile_count
    split_shape = (outer_rows, tile_count, inner_rows, tile_width, channels)
    if tile_height == tile_count and outer_rows == 1 and inner_rows == 1:
        grid_x, grid_g = (
            values.reshape(split_shape) for values in exchange(tokens, cotangent)
        )
    else:
        grid_x, grid_g = (
            lax.all_to_all(
                values.reshape(split_shape), ("ty", "tx"), split_axis=1, concat_axis=1, tiled=True
            )
            for values in (tokens, cotangent)
        )
    token_shape = (
        outer_rows,
        row_tiles // fold_rows,
        fold_rows,
        col_tiles,
        inner_rows,
        col_groups,
        stride_cols,
        channels,
    )
    win_count = fold_rows * inner_rows * stride_cols

    def to_windows(values):
        return (
            values.reshape(token_shape)
            .transpose(2, 4, 6, 1, 0, 3, 5, 7)
            .reshape(win_count, GRID * GRID, channels)
        )

    grad_windows, weight_term = window_grads(to_windows(grid_x), to_windows(grid_g), qkv_weight)
    back_shape = (
        fold_rows,
        inner_rows,
        stride_cols,
        row_tiles // fold_rows,
        outer_rows,
        col_tiles,
        col_groups,
        channels,
    )
    spread = grad_windows.reshape(back_shape).transpose(4, 3, 0, 5, 1, 6, 2, 7).reshape(split_shape)
    returned = lax.all_to_all(spread, ("ty", "tx"), split_axis=1, concat_axis=1, tiled=True)
    token_grad = returned.reshape(1, tile_height, tile_width, channels)
    row_blocks = weight_term.reshape(tile_count, channels // tile_count, weight_term.shape[1])
    weight_grad = weight_sum(row_blocks.astype(jnp.bfloat16))
    weight_grad = weight_grad / (rep_count * tile_count)
    return (token_grad, weight_grad)


def solution(mesh):
    placed = (P("rep", "ty", "tx", None), P(), P("rep", "ty", "tx", None))
    return jax.shard_map(
        shards,
        mesh=mesh,
        in_specs=placed,
        out_specs=(P("rep", "ty", "tx", None), P(("ty", "tx"), None)),
        check_vma=False,
    )
```

```python
import functools

import jax
import jax.numpy as jnp
from jax import lax
from jax.experimental import pallas as pl
from jax.experimental.pallas import tpu as pltpu
from jax.sharding import PartitionSpec as P

HEADS = 16
HEAD_DIM = 32
GRID = 8


eps_norm = 1e-05


def normalize(values):
    center = values - jnp.mean(values, axis=-1, keepdims=True)
    inv_std = lax.rsqrt(jnp.mean(center * center, axis=-1, keepdims=True) + eps_norm)
    return (center * inv_std, inv_std)


def window_grads(window_x, window_g, qkv_weight):
    win_count, win_tokens, channels = window_x.shape
    standard, inv_std = normalize(window_x.astype(jnp.float32))
    normed = standard.astype(jnp.bfloat16).reshape(win_count * win_tokens, channels)
    projection = jnp.dot(normed, qkv_weight, preferred_element_type=jnp.float32)
    flat_shape = (win_count, win_tokens, channels)
    query = (projection[:, :channels] * HEAD_DIM ** (-0.5)).astype(jnp.bfloat16).reshape(flat_shape)
    key = projection[:, channels : 2 * channels].astype(jnp.bfloat16).reshape(flat_shape)
    value = projection[:, 2 * channels :].astype(jnp.bfloat16).reshape(flat_shape)
    grad = window_g.astype(jnp.bfloat16)
    head_mask = (
        lax.broadcasted_iota(jnp.int32, (HEADS, channels), 1) // HEAD_DIM
        == lax.broadcasted_iota(jnp.int32, (HEADS, channels), 0)
    ).astype(jnp.bfloat16)

    def spread(values):
        return values[:, None, :, :] * head_mask[None, :, None, :]

    query_spread = spread(query)
    grad_spread = spread(grad)
    scores = jnp.einsum("wnqc,wkc->wnqk", query_spread, key, preferred_element_type=jnp.float32)
    peak_score = jnp.max(scores, axis=-1, keepdims=True)
    exponent = jnp.exp(scores - peak_score)
    attn_probs = exponent / jnp.sum(exponent, axis=-1, keepdims=True)
    probs_low = attn_probs.astype(jnp.bfloat16)
    attn_grad = jnp.einsum("wnqc,wkc->wnqk", grad_spread, value, preferred_element_type=jnp.float32)
    value_grad = jnp.einsum(
        "wnqk,wnqc->wkc", probs_low, grad_spread, preferred_element_type=jnp.float32
    ).astype(jnp.bfloat16)
    score_grad = (
        attn_probs * (attn_grad - jnp.sum(attn_probs * attn_grad, axis=-1, keepdims=True))
    ).astype(jnp.bfloat16)
    key_grad = jnp.einsum(
        "wnqk,wnqc->wkc", score_grad, query_spread, preferred_element_type=jnp.float32
    ).astype(jnp.bfloat16)
    query_full = jnp.einsum("wnqk,wkc->wnqc", score_grad, key, preferred_element_type=jnp.float32)
    query_grad = (
        jnp.sum(query_full * head_mask[None, :, None, :].astype(jnp.float32), axis=1)
        * HEAD_DIM ** (-0.5)
    ).astype(jnp.bfloat16)
    flat_shape = (win_count * win_tokens, channels)
    proj_grad = jnp.concatenate(
        [
            query_grad.reshape(flat_shape),
            key_grad.reshape(flat_shape),
            value_grad.reshape(flat_shape),
        ],
        axis=1,
    )
    normed_grad = lax.dot_general(
        proj_grad, qkv_weight, (((1,), (1,)), ((), ())), preferred_element_type=jnp.float32
    )
    normed_grad = normed_grad.reshape(win_count, win_tokens, channels)
    weight_term = lax.dot_general(
        normed, proj_grad, (((0,), (0,)), ((), ())), preferred_element_type=jnp.float32
    )
    inner_term = (
        normed_grad
        - jnp.mean(normed_grad, axis=-1, keepdims=True)
        - standard * jnp.mean(normed_grad * standard, axis=-1, keepdims=True)
    )
    token_grad = (window_g.astype(jnp.float32) + inv_std * inner_term).astype(jnp.bfloat16)
    return (token_grad, weight_term)


def weight_sum_kernel(rep_count, tile_count, col_tiles, blocks_ref, spread_ref, out_ref,
                      returned_ref, arrived, partial, held, returned_held, send_sems, recv_sems,
                      rep_send_sems, rep_recv_sems, back_send_sems, back_recv_sems, back_own_sem):
    me = lax.axis_index("rep")
    row = lax.axis_index("ty")
    col = lax.axis_index("tx")
    tile = row * col_tiles + col
    barrier = pltpu.get_barrier_semaphore()

    def tile_peer(step):
        peer = lax.rem(tile + step, tile_count)
        return (me, peer // col_tiles, lax.rem(peer, col_tiles))

    def rep_peer(step):
        return (lax.rem(me + step, rep_count), row, col)

    @pl.loop(1, tile_count)
    def _(step):
        pl.semaphore_signal(barrier, inc=1, device_id=tile_peer(step),
                            device_id_type=pl.DeviceIdType.MESH)

    @pl.loop(1, rep_count)
    def _(step):
        pl.semaphore_signal(barrier, inc=1, device_id=rep_peer(step),
                            device_id_type=pl.DeviceIdType.MESH)

    pl.semaphore_wait(barrier, tile_count + rep_count - 2)

    def back_copy(step):
        peer = lax.rem(tile + step, tile_count)
        return pltpu.make_async_remote_copy(
            src_ref=spread_ref.at[peer],
            dst_ref=returned_held.at[tile],
            send_sem=back_send_sems.at[step],
            recv_sem=back_recv_sems.at[step],
            device_id=tile_peer(step),
            device_id_type=pl.DeviceIdType.MESH,
        )

    back_own = pltpu.make_async_copy(spread_ref.at[tile], returned_held.at[tile], back_own_sem.at[0])
    back_own.start()

    @pl.loop(1, tile_count)
    def _(step):
        back_copy(step).start()

    def tile_copy(step):
        peer = lax.rem(tile + step, tile_count)
        return pltpu.make_async_remote_copy(
            src_ref=blocks_ref.at[peer],
            dst_ref=arrived.at[tile],
            send_sem=send_sems.at[step],
            recv_sem=recv_sems.at[step],
            device_id=tile_peer(step),
            device_id_type=pl.DeviceIdType.MESH,
        )

    own = pltpu.make_async_copy(blocks_ref.at[tile], arrived.at[tile], send_sems.at[0])
    own.start()

    @pl.loop(1, tile_count)
    def _(step):
        tile_copy(step).start()

    own.wait()

    @pl.loop(1, tile_count)
    def _(step):
        tile_copy(step).wait()

    def add_source(source, total):
        return total + arrived[source].astype(jnp.float32)

    partial[...] = lax.fori_loop(
        0, tile_count, add_source, jnp.zeros(partial.shape, jnp.float32)
    )
    held[me] = partial[...]

    def rep_copy(step):
        return pltpu.make_async_remote_copy(
            src_ref=partial,
            dst_ref=held.at[me],
            send_sem=rep_send_sems.at[step],
            recv_sem=rep_recv_sems.at[step],
            device_id=rep_peer(step),
            device_id_type=pl.DeviceIdType.MESH,
        )

    @pl.loop(1, rep_count)
    def _(step):
        rep_copy(step).start()

    @pl.loop(1, rep_count)
    def _(step):
        rep_copy(step).wait()

    back_own.wait()

    @pl.loop(1, tile_count)
    def _(step):
        back_copy(step).wait()

    returned_ref[...] = returned_held[...]
    total = held[0]
    for source in range(1, rep_count):
        total = total + held[source]
    out_ref[...] = total


def weight_sum(row_blocks, spread):
    rep_count = lax.axis_size("rep")
    col_tiles = lax.axis_size("tx")
    tile_count = row_blocks.shape[0]
    block_shape = row_blocks.shape[1:]
    return pl.pallas_call(
        functools.partial(weight_sum_kernel, rep_count, tile_count, col_tiles),
        out_shape=[
            jax.ShapeDtypeStruct(block_shape, jnp.float32),
            jax.ShapeDtypeStruct(spread.shape, spread.dtype),
        ],
        in_specs=[pl.BlockSpec(memory_space=pltpu.VMEM)] * 2,
        out_specs=[pl.BlockSpec(memory_space=pltpu.VMEM)] * 2,
        scratch_shapes=[
            pltpu.VMEM(row_blocks.shape, row_blocks.dtype),
            pltpu.VMEM(block_shape, jnp.float32),
            pltpu.VMEM((rep_count,) + block_shape, jnp.float32),
            pltpu.VMEM(spread.shape, spread.dtype),
            pltpu.SemaphoreType.DMA((tile_count,)),
            pltpu.SemaphoreType.DMA((tile_count,)),
            pltpu.SemaphoreType.DMA((rep_count,)),
            pltpu.SemaphoreType.DMA((rep_count,)),
            pltpu.SemaphoreType.DMA((tile_count,)),
            pltpu.SemaphoreType.DMA((tile_count,)),
            pltpu.SemaphoreType.DMA((1,)),
        ],
        compiler_params=pltpu.CompilerParams(collective_id=0, has_side_effects=True),
    )(row_blocks, spread)


def exchange_kernel(tile_count, col_tiles, tokens_ref, cot_ref, tokens_out, cot_out,
                    tokens_held, cot_held, send_sems, recv_sems, own_sems):
    me = lax.axis_index("rep")
    row = lax.axis_index("ty")
    col = lax.axis_index("tx")
    tile = row * col_tiles + col
    barrier = pltpu.get_barrier_semaphore()

    def tile_peer(step):
        peer = lax.rem(tile + step, tile_count)
        return (me, peer // col_tiles, lax.rem(peer, col_tiles))

    @pl.loop(1, tile_count)
    def _(step):
        pl.semaphore_signal(barrier, inc=1, device_id=tile_peer(step),
                            device_id_type=pl.DeviceIdType.MESH)

    pl.semaphore_wait(barrier, tile_count - 1)

    def tile_copies(step):
        peer = lax.rem(tile + step, tile_count)
        return [
            pltpu.make_async_remote_copy(
                src_ref=source.at[0, peer],
                dst_ref=held.at[tile],
                send_sem=send_sems.at[step, index],
                recv_sem=recv_sems.at[step, index],
                device_id=tile_peer(step),
                device_id_type=pl.DeviceIdType.MESH,
            )
            for index, (source, held) in enumerate(((tokens_ref, tokens_held), (cot_ref, cot_held)))
        ]

    own = [
        pltpu.make_async_copy(tokens_ref.at[0, tile], tokens_held.at[tile], own_sems.at[0]),
        pltpu.make_async_copy(cot_ref.at[0, tile], cot_held.at[tile], own_sems.at[1]),
    ]
    for copy in own:
        copy.start()

    @pl.loop(1, tile_count)
    def _(step):
        for copy in tile_copies(step):
            copy.start()

    for copy in own:
        copy.wait()

    @pl.loop(1, tile_count)
    def _(step):
        for copy in tile_copies(step):
            copy.wait()

    tokens_out[...] = tokens_held[...]
    cot_out[...] = cot_held[...]


def exchange(tokens, cotangent):
    col_tiles = lax.axis_size("tx")
    tile_count = lax.axis_size("ty") * col_tiles
    held_shape = (tile_count,) + tokens.shape[2:]
    return pl.pallas_call(
        functools.partial(exchange_kernel, tile_count, col_tiles),
        out_shape=[jax.ShapeDtypeStruct(held_shape, tokens.dtype)] * 2,
        in_specs=[pl.BlockSpec(memory_space=pltpu.VMEM)] * 2,
        out_specs=[pl.BlockSpec(memory_space=pltpu.VMEM)] * 2,
        scratch_shapes=[
            pltpu.VMEM(held_shape, tokens.dtype),
            pltpu.VMEM(held_shape, tokens.dtype),
            pltpu.SemaphoreType.DMA((tile_count, 2)),
            pltpu.SemaphoreType.DMA((tile_count, 2)),
            pltpu.SemaphoreType.DMA((2,)),
        ],
        compiler_params=pltpu.CompilerParams(collective_id=1, has_side_effects=True),
    )(tokens, cotangent)


def shards(tokens, qkv_weight, cotangent):
    rep_count = lax.axis_size("rep")
    row_tiles = lax.axis_size("ty")
    col_tiles = lax.axis_size("tx")
    tile_count = row_tiles * col_tiles
    tile_height = tokens.shape[1]
    tile_width = tokens.shape[2]
    channels = tokens.shape[3]
    stride_rows = row_tiles * tile_height // GRID
    stride_cols = col_tiles * tile_width // GRID
    block_rows = min(tile_height, stride_rows)
    fold_rows = stride_rows // block_rows
    col_groups = tile_width // stride_cols
    outer_rows = tile_height // block_rows
    inner_rows = block_rows // tile_count
    split_shape = (outer_rows, tile_count, inner_rows, tile_width, channels)
    if tile_height == tile_count and outer_rows == 1 and inner_rows == 1:
        grid_x, grid_g = (
            values.reshape(split_shape) for values in exchange(tokens, cotangent)
        )
    else:
        grid_x, grid_g = (
            lax.all_to_all(
                values.reshape(split_shape), ("ty", "tx"), split_axis=1, concat_axis=1, tiled=True
            )
            for values in (tokens, cotangent)
        )
    token_shape = (
        outer_rows,
        row_tiles // fold_rows,
        fold_rows,
        col_tiles,
        inner_rows,
        col_groups,
        stride_cols,
        channels,
    )
    win_count = fold_rows * inner_rows * stride_cols

    def to_windows(values):
        return (
            values.reshape(token_shape)
            .transpose(2, 4, 6, 1, 0, 3, 5, 7)
            .reshape(win_count, GRID * GRID, channels)
        )

    grad_windows, weight_term = window_grads(to_windows(grid_x), to_windows(grid_g), qkv_weight)
    back_shape = (
        fold_rows,
        inner_rows,
        stride_cols,
        row_tiles // fold_rows,
        outer_rows,
        col_tiles,
        col_groups,
        channels,
    )
    spread = grad_windows.reshape(back_shape).transpose(4, 3, 0, 5, 1, 6, 2, 7).reshape(split_shape)
    row_blocks = weight_term.reshape(tile_count, channels // tile_count, weight_term.shape[1])
    if tile_height == tile_count and outer_rows == 1 and inner_rows == 1:
        weight_grad, returned = weight_sum(
            row_blocks.astype(jnp.bfloat16), spread.reshape((tile_count,) + tokens.shape[2:])
        )
    else:
        returned = lax.all_to_all(spread, ("ty", "tx"), split_axis=1, concat_axis=1, tiled=True)
        gathered = lax.all_to_all(row_blocks.astype(jnp.bfloat16), ("ty", "tx"), 0, 0, tiled=True)
        weight_grad = lax.psum(jnp.sum(gathered.astype(jnp.float32), axis=0), "rep")
    token_grad = returned.reshape(1, tile_height, tile_width, channels)
    weight_grad = weight_grad / (rep_count * tile_count)
    return (token_grad, weight_grad)


def solution(mesh):
    placed = (P("rep", "ty", "tx", None), P(), P("rep", "ty", "tx", None))
    return jax.shard_map(
        shards,
        mesh=mesh,
        in_specs=placed,
        out_specs=(P("rep", "ty", "tx", None), P(("ty", "tx"), None)),
        check_vma=False,
    )
```

```python
import functools

import jax
import jax.numpy as jnp
from jax import lax
from jax.experimental import pallas as pl
from jax.experimental.pallas import tpu as pltpu
from jax.sharding import PartitionSpec as P

HEADS = 16
HEAD_DIM = 32
GRID = 8


eps_norm = 1e-05


def normalize(values):
    center = values - jnp.mean(values, axis=-1, keepdims=True)
    inv_std = lax.rsqrt(jnp.mean(center * center, axis=-1, keepdims=True) + eps_norm)
    return (center * inv_std, inv_std)


def window_grads(window_x, window_g, qkv_weight):
    win_count, win_tokens, channels = window_x.shape
    standard, inv_std = normalize(window_x.astype(jnp.float32))
    normed = standard.astype(jnp.bfloat16).reshape(win_count * win_tokens, channels)
    projection = jnp.dot(normed, qkv_weight, preferred_element_type=jnp.float32)
    flat_shape = (win_count, win_tokens, channels)
    query = (projection[:, :channels] * HEAD_DIM ** (-0.5)).astype(jnp.bfloat16).reshape(flat_shape)
    key = projection[:, channels : 2 * channels].astype(jnp.bfloat16).reshape(flat_shape)
    value = projection[:, 2 * channels :].astype(jnp.bfloat16).reshape(flat_shape)
    grad = window_g.astype(jnp.bfloat16)
    head_mask = (
        lax.broadcasted_iota(jnp.int32, (HEADS, channels), 1) // HEAD_DIM
        == lax.broadcasted_iota(jnp.int32, (HEADS, channels), 0)
    ).astype(jnp.bfloat16)

    def spread(values):
        return values[:, None, :, :] * head_mask[None, :, None, :]

    query_spread = spread(query)
    grad_spread = spread(grad)
    scores = jnp.einsum("wnqc,wkc->wnqk", query_spread, key, preferred_element_type=jnp.float32)
    peak_score = jnp.max(scores, axis=-1, keepdims=True)
    exponent = jnp.exp(scores - peak_score)
    attn_probs = exponent / jnp.sum(exponent, axis=-1, keepdims=True)
    probs_low = attn_probs.astype(jnp.bfloat16)
    attn_grad = jnp.einsum("wnqc,wkc->wnqk", grad_spread, value, preferred_element_type=jnp.float32)
    value_grad = jnp.einsum(
        "wnqk,wnqc->wkc", probs_low, grad_spread, preferred_element_type=jnp.float32
    ).astype(jnp.bfloat16)
    score_grad = (
        attn_probs * (attn_grad - jnp.sum(attn_probs * attn_grad, axis=-1, keepdims=True))
    ).astype(jnp.bfloat16)
    key_grad = jnp.einsum(
        "wnqk,wnqc->wkc", score_grad, query_spread, preferred_element_type=jnp.float32
    ).astype(jnp.bfloat16)
    query_full = jnp.einsum("wnqk,wkc->wnqc", score_grad, key, preferred_element_type=jnp.float32)
    query_grad = (
        jnp.sum(query_full * head_mask[None, :, None, :].astype(jnp.float32), axis=1)
        * HEAD_DIM ** (-0.5)
    ).astype(jnp.bfloat16)
    flat_shape = (win_count * win_tokens, channels)
    proj_grad = jnp.concatenate(
        [
            query_grad.reshape(flat_shape),
            key_grad.reshape(flat_shape),
            value_grad.reshape(flat_shape),
        ],
        axis=1,
    )
    normed_grad = lax.dot_general(
        proj_grad, qkv_weight, (((1,), (1,)), ((), ())), preferred_element_type=jnp.float32
    )
    normed_grad = normed_grad.reshape(win_count, win_tokens, channels)
    weight_term = lax.dot_general(
        normed, proj_grad, (((0,), (0,)), ((), ())), preferred_element_type=jnp.float32
    )
    inner_term = (
        normed_grad
        - jnp.mean(normed_grad, axis=-1, keepdims=True)
        - standard * jnp.mean(normed_grad * standard, axis=-1, keepdims=True)
    )
    token_grad = (window_g.astype(jnp.float32) + inv_std * inner_term).astype(jnp.bfloat16)
    return (token_grad, weight_term)


def weight_sum_kernel(rep_count, tile_count, col_tiles, blocks_ref, spread_ref, out_ref,
                      returned_ref, arrived, partial, held, returned_held, send_sems, recv_sems,
                      rep_send_sems, rep_recv_sems, back_send_sems, back_recv_sems, back_own_sem):
    me = lax.axis_index("rep")
    row = lax.axis_index("ty")
    col = lax.axis_index("tx")
    tile = row * col_tiles + col
    barrier = pltpu.get_barrier_semaphore()

    def tile_peer(step):
        peer = lax.rem(tile + step, tile_count)
        return (me, peer // col_tiles, lax.rem(peer, col_tiles))

    def rep_peer(step):
        return (lax.rem(me + step, rep_count), row, col)

    @pl.loop(1, tile_count)
    def _(step):
        pl.semaphore_signal(barrier, inc=1, device_id=tile_peer(step),
                            device_id_type=pl.DeviceIdType.MESH)

    @pl.loop(1, rep_count)
    def _(step):
        pl.semaphore_signal(barrier, inc=1, device_id=rep_peer(step),
                            device_id_type=pl.DeviceIdType.MESH)

    pl.semaphore_wait(barrier, tile_count + rep_count - 2)

    def back_copy(step):
        peer = lax.rem(tile + step, tile_count)
        return pltpu.make_async_remote_copy(
            src_ref=spread_ref.at[peer],
            dst_ref=returned_held.at[tile],
            send_sem=back_send_sems.at[step],
            recv_sem=back_recv_sems.at[step],
            device_id=tile_peer(step),
            device_id_type=pl.DeviceIdType.MESH,
        )

    back_own = pltpu.make_async_copy(spread_ref.at[tile], returned_held.at[tile], back_own_sem.at[0])
    back_own.start()

    @pl.loop(1, tile_count)
    def _(step):
        back_copy(step).start()

    def tile_copy(step):
        peer = lax.rem(tile + step, tile_count)
        return pltpu.make_async_remote_copy(
            src_ref=blocks_ref.at[peer],
            dst_ref=arrived.at[tile],
            send_sem=send_sems.at[step],
            recv_sem=recv_sems.at[step],
            device_id=tile_peer(step),
            device_id_type=pl.DeviceIdType.MESH,
        )

    own = pltpu.make_async_copy(blocks_ref.at[tile], arrived.at[tile], send_sems.at[0])
    own.start()

    @pl.loop(1, tile_count)
    def _(step):
        tile_copy(step).start()

    own.wait()

    @pl.loop(1, tile_count)
    def _(step):
        tile_copy(step).wait()

    def add_source(source, total):
        return total + arrived[source].astype(jnp.float32)

    partial[...] = lax.fori_loop(
        0, tile_count, add_source, jnp.zeros(partial.shape, jnp.float32)
    )
    held[me] = partial[...]

    def rep_copy(step):
        return pltpu.make_async_remote_copy(
            src_ref=partial,
            dst_ref=held.at[me],
            send_sem=rep_send_sems.at[step],
            recv_sem=rep_recv_sems.at[step],
            device_id=rep_peer(step),
            device_id_type=pl.DeviceIdType.MESH,
        )

    @pl.loop(1, rep_count)
    def _(step):
        rep_copy(step).start()

    @pl.loop(1, rep_count)
    def _(step):
        rep_copy(step).wait()

    back_own.wait()

    @pl.loop(1, tile_count)
    def _(step):
        back_copy(step).wait()

    returned_ref[...] = returned_held[...]
    total = held[0]
    for source in range(1, rep_count):
        total = total + held[source]
    out_ref[...] = total


def weight_sum(row_blocks, spread):
    rep_count = lax.axis_size("rep")
    col_tiles = lax.axis_size("tx")
    tile_count = row_blocks.shape[0]
    block_shape = row_blocks.shape[1:]
    return pl.pallas_call(
        functools.partial(weight_sum_kernel, rep_count, tile_count, col_tiles),
        out_shape=[
            jax.ShapeDtypeStruct(block_shape, jnp.float32),
            jax.ShapeDtypeStruct(spread.shape, spread.dtype),
        ],
        in_specs=[pl.BlockSpec(memory_space=pltpu.VMEM)] * 2,
        out_specs=[pl.BlockSpec(memory_space=pltpu.VMEM)] * 2,
        scratch_shapes=[
            pltpu.VMEM(row_blocks.shape, row_blocks.dtype),
            pltpu.VMEM(block_shape, jnp.float32),
            pltpu.VMEM((rep_count,) + block_shape, jnp.float32),
            pltpu.VMEM(spread.shape, spread.dtype),
            pltpu.SemaphoreType.DMA((tile_count,)),
            pltpu.SemaphoreType.DMA((tile_count,)),
            pltpu.SemaphoreType.DMA((rep_count,)),
            pltpu.SemaphoreType.DMA((rep_count,)),
            pltpu.SemaphoreType.DMA((tile_count,)),
            pltpu.SemaphoreType.DMA((tile_count,)),
            pltpu.SemaphoreType.DMA((1,)),
        ],
        compiler_params=pltpu.CompilerParams(collective_id=0, has_side_effects=True),
    )(row_blocks, spread)


def paired_sum_kernel(rep_count, tile_count, col_tiles, blocks_ref, spread_ref, out_ref,
                      returned_ref, pair_held, pair_sum, arrived, partial, held, final,
                      returned_held, pair_sems, tile_send_sems, tile_recv_sems, zh_send_sems,
                      zh_recv_sems, final_sems, back_send_sems, back_recv_sems, own_sems):
    me = lax.axis_index("rep")
    row = lax.axis_index("ty")
    col = lax.axis_index("tx")
    tile = row * col_tiles + col
    core = lax.rem(me, 2)
    plane = me // 2
    planes = rep_count // 2
    partner = me + 1 - 2 * core
    half = tile_count // 2
    mine_start = core * half
    receiver = tile // half == core
    barrier = pltpu.get_barrier_semaphore()

    def tile_device(peer):
        return (me, peer // col_tiles, lax.rem(peer, col_tiles))

    def tile_peer(step):
        return tile_device(lax.rem(tile + step, tile_count))

    def plane_peer(step):
        return (2 * lax.rem(plane + step, planes) + core, row, col)

    mesh_id = pl.DeviceIdType.MESH
    pl.semaphore_signal(barrier, inc=1, device_id=(partner, row, col), device_id_type=mesh_id)

    @pl.loop(1, tile_count)
    def _(step):
        pl.semaphore_signal(barrier, inc=1, device_id=tile_peer(step), device_id_type=mesh_id)

    @pl.when(receiver)
    def _():
        @pl.loop(1, planes)
        def _(step):
            pl.semaphore_signal(barrier, inc=1, device_id=plane_peer(step), device_id_type=mesh_id)

    pl.semaphore_wait(barrier, tile_count + (planes - 1) * receiver.astype(jnp.int32))

    pair_copy = pltpu.make_async_remote_copy(
        src_ref=blocks_ref.at[pl.ds((1 - core) * half, half)],
        dst_ref=pair_held,
        send_sem=pair_sems.at[0],
        recv_sem=pair_sems.at[1],
        device_id=(partner, row, col),
        device_id_type=mesh_id,
    )
    pair_copy.start()

    def back_copy(step):
        peer = lax.rem(tile + step, tile_count)
        return pltpu.make_async_remote_copy(
            src_ref=spread_ref.at[peer],
            dst_ref=returned_held.at[tile],
            send_sem=back_send_sems.at[step],
            recv_sem=back_recv_sems.at[step],
            device_id=tile_peer(step),
            device_id_type=mesh_id,
        )

    back_own = pltpu.make_async_copy(spread_ref.at[tile], returned_held.at[tile], own_sems.at[0])
    back_own.start()

    @pl.loop(1, tile_count)
    def _(step):
        back_copy(step).start()

    pair_copy.wait()

    @pl.loop(0, half)
    def _(index):
        pair_sum[index] = (
            blocks_ref[mine_start + index].astype(jnp.float32)
            + pair_held[index].astype(jnp.float32)
        ).astype(pair_sum.dtype)

    def sum_copy(index):
        target = mine_start + index
        step = lax.rem(target - tile + tile_count, tile_count)
        return pltpu.make_async_remote_copy(
            src_ref=pair_sum.at[index],
            dst_ref=arrived.at[tile],
            send_sem=tile_send_sems.at[step],
            recv_sem=tile_recv_sems.at[step],
            device_id=tile_device(target),
            device_id_type=mesh_id,
        )

    @pl.loop(0, half)
    def _(index):
        @pl.when(mine_start + index != tile)
        def _():
            sum_copy(index).start()

    def final_copy():
        return pltpu.make_async_remote_copy(
            src_ref=final,
            dst_ref=final,
            send_sem=final_sems.at[0],
            recv_sem=final_sems.at[1],
            device_id=(partner, row, col),
            device_id_type=mesh_id,
        )

    @pl.when(receiver)
    def _():
        own = pltpu.make_async_copy(
            pair_sum.at[tile - mine_start], arrived.at[tile], own_sems.at[1]
        )
        own.start()
        own.wait()

        @pl.loop(1, tile_count)
        def _(step):
            pltpu.make_async_remote_copy(
                src_ref=pair_sum.at[0],
                dst_ref=arrived.at[tile],
                send_sem=tile_send_sems.at[step],
                recv_sem=tile_recv_sems.at[step],
                device_id=tile_peer(step),
                device_id_type=mesh_id,
            ).wait_recv()

        def add_source(source, total):
            return total + arrived[source].astype(jnp.float32)

        partial[...] = lax.fori_loop(
            0, tile_count, add_source, jnp.zeros(partial.shape, jnp.float32)
        )
        held[plane] = partial[...]

        def plane_copy(step):
            return pltpu.make_async_remote_copy(
                src_ref=partial,
                dst_ref=held.at[plane],
                send_sem=zh_send_sems.at[step],
                recv_sem=zh_recv_sems.at[step],
                device_id=plane_peer(step),
                device_id_type=mesh_id,
            )

        @pl.loop(1, planes)
        def _(step):
            plane_copy(step).start()

        @pl.loop(1, planes)
        def _(step):
            plane_copy(step).wait()

        total = held[0]
        for source in range(1, planes):
            total = total + held[source]
        final[...] = total
        copy = final_copy()
        copy.start()
        copy.wait_send()

    @pl.when(jnp.logical_not(receiver))
    def _():
        final_copy().wait_recv()

    @pl.loop(0, half)
    def _(index):
        @pl.when(mine_start + index != tile)
        def _():
            sum_copy(index).wait_send()

    back_own.wait()

    @pl.loop(1, tile_count)
    def _(step):
        back_copy(step).wait()

    returned_ref[...] = returned_held[...]
    out_ref[...] = final[...]


def paired_sum(row_blocks, spread):
    rep_count = lax.axis_size("rep")
    col_tiles = lax.axis_size("tx")
    tile_count = row_blocks.shape[0]
    block_shape = row_blocks.shape[1:]
    half_shape = (tile_count // 2,) + block_shape
    return pl.pallas_call(
        functools.partial(paired_sum_kernel, rep_count, tile_count, col_tiles),
        out_shape=[
            jax.ShapeDtypeStruct(block_shape, jnp.float32),
            jax.ShapeDtypeStruct(spread.shape, spread.dtype),
        ],
        in_specs=[pl.BlockSpec(memory_space=pltpu.VMEM)] * 2,
        out_specs=[pl.BlockSpec(memory_space=pltpu.VMEM)] * 2,
        scratch_shapes=[
            pltpu.VMEM(half_shape, row_blocks.dtype),
            pltpu.VMEM(half_shape, row_blocks.dtype),
            pltpu.VMEM(row_blocks.shape, row_blocks.dtype),
            pltpu.VMEM(block_shape, jnp.float32),
            pltpu.VMEM((rep_count // 2,) + block_shape, jnp.float32),
            pltpu.VMEM(block_shape, jnp.float32),
            pltpu.VMEM(spread.shape, spread.dtype),
            pltpu.SemaphoreType.DMA((2,)),
            pltpu.SemaphoreType.DMA((tile_count,)),
            pltpu.SemaphoreType.DMA((tile_count,)),
            pltpu.SemaphoreType.DMA((rep_count // 2,)),
            pltpu.SemaphoreType.DMA((rep_count // 2,)),
            pltpu.SemaphoreType.DMA((2,)),
            pltpu.SemaphoreType.DMA((tile_count,)),
            pltpu.SemaphoreType.DMA((tile_count,)),
            pltpu.SemaphoreType.DMA((2,)),
        ],
        compiler_params=pltpu.CompilerParams(collective_id=2, has_side_effects=True),
    )(row_blocks, spread)


def exchange_kernel(tile_count, col_tiles, tokens_ref, cot_ref, tokens_out, cot_out,
                    tokens_held, cot_held, send_sems, recv_sems, own_sems):
    me = lax.axis_index("rep")
    row = lax.axis_index("ty")
    col = lax.axis_index("tx")
    tile = row * col_tiles + col
    barrier = pltpu.get_barrier_semaphore()

    def tile_peer(step):
        peer = lax.rem(tile + step, tile_count)
        return (me, peer // col_tiles, lax.rem(peer, col_tiles))

    @pl.loop(1, tile_count)
    def _(step):
        pl.semaphore_signal(barrier, inc=1, device_id=tile_peer(step),
                            device_id_type=pl.DeviceIdType.MESH)

    pl.semaphore_wait(barrier, tile_count - 1)

    def tile_copies(step):
        peer = lax.rem(tile + step, tile_count)
        return [
            pltpu.make_async_remote_copy(
                src_ref=source.at[0, peer],
                dst_ref=held.at[tile],
                send_sem=send_sems.at[step, index],
                recv_sem=recv_sems.at[step, index],
                device_id=tile_peer(step),
                device_id_type=pl.DeviceIdType.MESH,
            )
            for index, (source, held) in enumerate(((tokens_ref, tokens_held), (cot_ref, cot_held)))
        ]

    own = [
        pltpu.make_async_copy(tokens_ref.at[0, tile], tokens_held.at[tile], own_sems.at[0]),
        pltpu.make_async_copy(cot_ref.at[0, tile], cot_held.at[tile], own_sems.at[1]),
    ]
    for copy in own:
        copy.start()

    @pl.loop(1, tile_count)
    def _(step):
        for copy in tile_copies(step):
            copy.start()

    for copy in own:
        copy.wait()

    @pl.loop(1, tile_count)
    def _(step):
        for copy in tile_copies(step):
            copy.wait()

    tokens_out[...] = tokens_held[...]
    cot_out[...] = cot_held[...]


def exchange(tokens, cotangent):
    col_tiles = lax.axis_size("tx")
    tile_count = lax.axis_size("ty") * col_tiles
    held_shape = (tile_count,) + tokens.shape[2:]
    return pl.pallas_call(
        functools.partial(exchange_kernel, tile_count, col_tiles),
        out_shape=[jax.ShapeDtypeStruct(held_shape, tokens.dtype)] * 2,
        in_specs=[pl.BlockSpec(memory_space=pltpu.VMEM)] * 2,
        out_specs=[pl.BlockSpec(memory_space=pltpu.VMEM)] * 2,
        scratch_shapes=[
            pltpu.VMEM(held_shape, tokens.dtype),
            pltpu.VMEM(held_shape, tokens.dtype),
            pltpu.SemaphoreType.DMA((tile_count, 2)),
            pltpu.SemaphoreType.DMA((tile_count, 2)),
            pltpu.SemaphoreType.DMA((2,)),
        ],
        compiler_params=pltpu.CompilerParams(collective_id=1, has_side_effects=True),
    )(tokens, cotangent)


def shards(tokens, qkv_weight, cotangent):
    rep_count = lax.axis_size("rep")
    row_tiles = lax.axis_size("ty")
    col_tiles = lax.axis_size("tx")
    tile_count = row_tiles * col_tiles
    tile_height = tokens.shape[1]
    tile_width = tokens.shape[2]
    channels = tokens.shape[3]
    stride_rows = row_tiles * tile_height // GRID
    stride_cols = col_tiles * tile_width // GRID
    block_rows = min(tile_height, stride_rows)
    fold_rows = stride_rows // block_rows
    col_groups = tile_width // stride_cols
    outer_rows = tile_height // block_rows
    inner_rows = block_rows // tile_count
    split_shape = (outer_rows, tile_count, inner_rows, tile_width, channels)
    if tile_height == tile_count and outer_rows == 1 and inner_rows == 1:
        grid_x, grid_g = (
            values.reshape(split_shape) for values in exchange(tokens, cotangent)
        )
    else:
        grid_x, grid_g = (
            lax.all_to_all(
                values.reshape(split_shape), ("ty", "tx"), split_axis=1, concat_axis=1, tiled=True
            )
            for values in (tokens, cotangent)
        )
    token_shape = (
        outer_rows,
        row_tiles // fold_rows,
        fold_rows,
        col_tiles,
        inner_rows,
        col_groups,
        stride_cols,
        channels,
    )
    win_count = fold_rows * inner_rows * stride_cols

    def to_windows(values):
        return (
            values.reshape(token_shape)
            .transpose(2, 4, 6, 1, 0, 3, 5, 7)
            .reshape(win_count, GRID * GRID, channels)
        )

    grad_windows, weight_term = window_grads(to_windows(grid_x), to_windows(grid_g), qkv_weight)
    back_shape = (
        fold_rows,
        inner_rows,
        stride_cols,
        row_tiles // fold_rows,
        outer_rows,
        col_tiles,
        col_groups,
        channels,
    )
    spread = grad_windows.reshape(back_shape).transpose(4, 3, 0, 5, 1, 6, 2, 7).reshape(split_shape)
    row_blocks = weight_term.reshape(tile_count, channels // tile_count, weight_term.shape[1])
    if tile_height == tile_count and outer_rows == 1 and inner_rows == 1:
        weight_grad, returned = paired_sum(
            row_blocks.astype(jnp.bfloat16), spread.reshape((tile_count,) + tokens.shape[2:])
        )
    else:
        returned = lax.all_to_all(spread, ("ty", "tx"), split_axis=1, concat_axis=1, tiled=True)
        gathered = lax.all_to_all(row_blocks.astype(jnp.bfloat16), ("ty", "tx"), 0, 0, tiled=True)
        weight_grad = lax.psum(jnp.sum(gathered.astype(jnp.float32), axis=0), "rep")
    token_grad = returned.reshape(1, tile_height, tile_width, channels)
    weight_grad = weight_grad / (rep_count * tile_count)
    return (token_grad, weight_grad)


def solution(mesh):
    placed = (P("rep", "ty", "tx", None), P(), P("rep", "ty", "tx", None))
    return jax.shard_map(
        shards,
        mesh=mesh,
        in_specs=placed,
        out_specs=(P("rep", "ty", "tx", None), P(("ty", "tx"), None)),
        check_vma=False,
    )
```

```python
import functools

import jax
import jax.numpy as jnp
from jax import lax
from jax.experimental import pallas as pl
from jax.experimental.pallas import tpu as pltpu
from jax.sharding import PartitionSpec as P

HEADS = 16
HEAD_DIM = 32
GRID = 8


eps_norm = 1e-05


def normalize(values):
    center = values - jnp.mean(values, axis=-1, keepdims=True)
    inv_std = lax.rsqrt(jnp.mean(center * center, axis=-1, keepdims=True) + eps_norm)
    return (center * inv_std, inv_std)


def window_grads(window_x, window_g, qkv_weight):
    win_count, win_tokens, channels = window_x.shape
    standard, inv_std = normalize(window_x.astype(jnp.float32))
    normed = standard.astype(jnp.bfloat16).reshape(win_count * win_tokens, channels)
    projection = jnp.dot(normed, qkv_weight, preferred_element_type=jnp.float32)
    flat_shape = (win_count, win_tokens, channels)
    query = (projection[:, :channels] * HEAD_DIM ** (-0.5)).astype(jnp.bfloat16).reshape(flat_shape)
    key = projection[:, channels : 2 * channels].astype(jnp.bfloat16).reshape(flat_shape)
    value = projection[:, 2 * channels :].astype(jnp.bfloat16).reshape(flat_shape)
    grad = window_g.astype(jnp.bfloat16)
    head_mask = (
        lax.broadcasted_iota(jnp.int32, (HEADS, channels), 1) // HEAD_DIM
        == lax.broadcasted_iota(jnp.int32, (HEADS, channels), 0)
    ).astype(jnp.bfloat16)

    def spread(values):
        return values[:, None, :, :] * head_mask[None, :, None, :]

    query_spread = spread(query)
    grad_spread = spread(grad)
    scores = jnp.einsum("wnqc,wkc->wnqk", query_spread, key, preferred_element_type=jnp.float32)
    peak_score = jnp.max(scores, axis=-1, keepdims=True)
    exponent = jnp.exp(scores - peak_score)
    attn_probs = exponent / jnp.sum(exponent, axis=-1, keepdims=True)
    probs_low = attn_probs.astype(jnp.bfloat16)
    attn_grad = jnp.einsum("wnqc,wkc->wnqk", grad_spread, value, preferred_element_type=jnp.float32)
    value_grad = jnp.einsum(
        "wnqk,wnqc->wkc", probs_low, grad_spread, preferred_element_type=jnp.float32
    ).astype(jnp.bfloat16)
    score_grad = (
        attn_probs * (attn_grad - jnp.sum(attn_probs * attn_grad, axis=-1, keepdims=True))
    ).astype(jnp.bfloat16)
    key_grad = jnp.einsum(
        "wnqk,wnqc->wkc", score_grad, query_spread, preferred_element_type=jnp.float32
    ).astype(jnp.bfloat16)
    query_full = jnp.einsum("wnqk,wkc->wnqc", score_grad, key, preferred_element_type=jnp.float32)
    query_grad = (
        jnp.sum(query_full * head_mask[None, :, None, :].astype(jnp.float32), axis=1)
        * HEAD_DIM ** (-0.5)
    ).astype(jnp.bfloat16)
    flat_shape = (win_count * win_tokens, channels)
    proj_grad = jnp.concatenate(
        [
            query_grad.reshape(flat_shape),
            key_grad.reshape(flat_shape),
            value_grad.reshape(flat_shape),
        ],
        axis=1,
    )
    normed_grad = lax.dot_general(
        proj_grad, qkv_weight, (((1,), (1,)), ((), ())), preferred_element_type=jnp.float32
    )
    normed_grad = normed_grad.reshape(win_count, win_tokens, channels)
    weight_term = lax.dot_general(
        normed, proj_grad, (((0,), (0,)), ((), ())), preferred_element_type=jnp.float32
    )
    inner_term = (
        normed_grad
        - jnp.mean(normed_grad, axis=-1, keepdims=True)
        - standard * jnp.mean(normed_grad * standard, axis=-1, keepdims=True)
    )
    token_grad = (window_g.astype(jnp.float32) + inv_std * inner_term).astype(jnp.bfloat16)
    return (token_grad, weight_term)


def weight_sum_kernel(rep_count, tile_count, col_tiles, blocks_ref, spread_ref, out_ref,
                      returned_ref, arrived, partial, held, returned_held, send_sems, recv_sems,
                      rep_send_sems, rep_recv_sems, back_send_sems, back_recv_sems, back_own_sem):
    me = lax.axis_index("rep")
    row = lax.axis_index("ty")
    col = lax.axis_index("tx")
    tile = row * col_tiles + col
    barrier = pltpu.get_barrier_semaphore()

    def tile_peer(step):
        peer = lax.rem(tile + step, tile_count)
        return (me, peer // col_tiles, lax.rem(peer, col_tiles))

    def rep_peer(step):
        return (lax.rem(me + step, rep_count), row, col)

    @pl.loop(1, tile_count)
    def _(step):
        pl.semaphore_signal(barrier, inc=1, device_id=tile_peer(step),
                            device_id_type=pl.DeviceIdType.MESH)

    @pl.loop(1, rep_count)
    def _(step):
        pl.semaphore_signal(barrier, inc=1, device_id=rep_peer(step),
                            device_id_type=pl.DeviceIdType.MESH)

    pl.semaphore_wait(barrier, tile_count + rep_count - 2)

    def back_copy(step):
        peer = lax.rem(tile + step, tile_count)
        return pltpu.make_async_remote_copy(
            src_ref=spread_ref.at[peer],
            dst_ref=returned_held.at[tile],
            send_sem=back_send_sems.at[step],
            recv_sem=back_recv_sems.at[step],
            device_id=tile_peer(step),
            device_id_type=pl.DeviceIdType.MESH,
        )

    back_own = pltpu.make_async_copy(spread_ref.at[tile], returned_held.at[tile], back_own_sem.at[0])
    back_own.start()

    @pl.loop(1, tile_count)
    def _(step):
        back_copy(step).start()

    def tile_copy(step):
        peer = lax.rem(tile + step, tile_count)
        return pltpu.make_async_remote_copy(
            src_ref=blocks_ref.at[peer],
            dst_ref=arrived.at[tile],
            send_sem=send_sems.at[step],
            recv_sem=recv_sems.at[step],
            device_id=tile_peer(step),
            device_id_type=pl.DeviceIdType.MESH,
        )

    own = pltpu.make_async_copy(blocks_ref.at[tile], arrived.at[tile], send_sems.at[0])
    own.start()

    @pl.loop(1, tile_count)
    def _(step):
        tile_copy(step).start()

    own.wait()

    @pl.loop(1, tile_count)
    def _(step):
        tile_copy(step).wait()

    def add_source(source, total):
        return total + arrived[source].astype(jnp.float32)

    partial[...] = lax.fori_loop(
        0, tile_count, add_source, jnp.zeros(partial.shape, jnp.float32)
    )
    held[me] = partial[...]

    def rep_copy(step):
        return pltpu.make_async_remote_copy(
            src_ref=partial,
            dst_ref=held.at[me],
            send_sem=rep_send_sems.at[step],
            recv_sem=rep_recv_sems.at[step],
            device_id=rep_peer(step),
            device_id_type=pl.DeviceIdType.MESH,
        )

    @pl.loop(1, rep_count)
    def _(step):
        rep_copy(step).start()

    @pl.loop(1, rep_count)
    def _(step):
        rep_copy(step).wait()

    back_own.wait()

    @pl.loop(1, tile_count)
    def _(step):
        back_copy(step).wait()

    returned_ref[...] = returned_held[...]
    total = held[0]
    for source in range(1, rep_count):
        total = total + held[source]
    out_ref[...] = total


def weight_sum(row_blocks, spread):
    rep_count = lax.axis_size("rep")
    col_tiles = lax.axis_size("tx")
    tile_count = row_blocks.shape[0]
    block_shape = row_blocks.shape[1:]
    return pl.pallas_call(
        functools.partial(weight_sum_kernel, rep_count, tile_count, col_tiles),
        out_shape=[
            jax.ShapeDtypeStruct(block_shape, jnp.float32),
            jax.ShapeDtypeStruct(spread.shape, spread.dtype),
        ],
        in_specs=[pl.BlockSpec(memory_space=pltpu.VMEM)] * 2,
        out_specs=[pl.BlockSpec(memory_space=pltpu.VMEM)] * 2,
        scratch_shapes=[
            pltpu.VMEM(row_blocks.shape, row_blocks.dtype),
            pltpu.VMEM(block_shape, jnp.float32),
            pltpu.VMEM((rep_count,) + block_shape, jnp.float32),
            pltpu.VMEM(spread.shape, spread.dtype),
            pltpu.SemaphoreType.DMA((tile_count,)),
            pltpu.SemaphoreType.DMA((tile_count,)),
            pltpu.SemaphoreType.DMA((rep_count,)),
            pltpu.SemaphoreType.DMA((rep_count,)),
            pltpu.SemaphoreType.DMA((tile_count,)),
            pltpu.SemaphoreType.DMA((tile_count,)),
            pltpu.SemaphoreType.DMA((1,)),
        ],
        compiler_params=pltpu.CompilerParams(collective_id=0, has_side_effects=True),
    )(row_blocks, spread)


def paired_sum_kernel(rep_count, tile_count, col_tiles, blocks_ref, spread_ref, out_ref,
                      returned_ref, pair_held, pair_sum, arrived, partial, held, final,
                      returned_held, pair_sems, tile_send_sems, tile_recv_sems, zh_send_sems,
                      zh_recv_sems, final_sems, back_send_sems, back_recv_sems, own_sems):
    me = lax.axis_index("rep")
    row = lax.axis_index("ty")
    col = lax.axis_index("tx")
    tile = row * col_tiles + col
    core = lax.rem(me, 2)
    plane = me // 2
    planes = rep_count // 2
    partner = me + 1 - 2 * core
    half = tile_count // 2
    mine_start = core * half
    receiver = tile // half == core
    barrier = pltpu.get_barrier_semaphore()

    def tile_device(peer):
        return (me, peer // col_tiles, lax.rem(peer, col_tiles))

    def tile_peer(step):
        return tile_device(lax.rem(tile + step, tile_count))

    def plane_peer(step):
        return (2 * lax.rem(plane + step, planes) + core, row, col)

    mesh_id = pl.DeviceIdType.MESH
    pl.semaphore_signal(barrier, inc=1, device_id=(partner, row, col), device_id_type=mesh_id)

    @pl.loop(1, tile_count)
    def _(step):
        pl.semaphore_signal(barrier, inc=1, device_id=tile_peer(step), device_id_type=mesh_id)

    @pl.when(receiver)
    def _():
        @pl.loop(1, planes)
        def _(step):
            pl.semaphore_signal(barrier, inc=1, device_id=plane_peer(step), device_id_type=mesh_id)

    pl.semaphore_wait(barrier, tile_count + (planes - 1) * receiver.astype(jnp.int32))

    pair_copy = pltpu.make_async_remote_copy(
        src_ref=blocks_ref.at[pl.ds((1 - core) * half, half)],
        dst_ref=pair_held,
        send_sem=pair_sems.at[0],
        recv_sem=pair_sems.at[1],
        device_id=(partner, row, col),
        device_id_type=mesh_id,
    )
    pair_copy.start()

    def back_copy(step):
        peer = lax.rem(tile + step, tile_count)
        return pltpu.make_async_remote_copy(
            src_ref=spread_ref.at[peer],
            dst_ref=returned_held.at[tile],
            send_sem=back_send_sems.at[step],
            recv_sem=back_recv_sems.at[step],
            device_id=tile_peer(step),
            device_id_type=mesh_id,
        )

    back_own = pltpu.make_async_copy(spread_ref.at[tile], returned_held.at[tile], own_sems.at[0])
    back_own.start()

    @pl.loop(1, tile_count)
    def _(step):
        back_copy(step).start()

    pair_copy.wait()

    @pl.loop(0, half)
    def _(index):
        pair_sum[index] = (
            blocks_ref[mine_start + index].astype(jnp.float32)
            + pair_held[index].astype(jnp.float32)
        ).astype(pair_sum.dtype)

    def sum_copy(index):
        target = mine_start + index
        step = lax.rem(target - tile + tile_count, tile_count)
        return pltpu.make_async_remote_copy(
            src_ref=pair_sum.at[index],
            dst_ref=arrived.at[tile],
            send_sem=tile_send_sems.at[step],
            recv_sem=tile_recv_sems.at[step],
            device_id=tile_device(target),
            device_id_type=mesh_id,
        )

    @pl.loop(0, half)
    def _(index):
        @pl.when(mine_start + index != tile)
        def _():
            sum_copy(index).start()

    def final_copy():
        return pltpu.make_async_remote_copy(
            src_ref=final,
            dst_ref=final,
            send_sem=final_sems.at[0],
            recv_sem=final_sems.at[1],
            device_id=(partner, row, col),
            device_id_type=mesh_id,
        )

    @pl.when(receiver)
    def _():
        own = pltpu.make_async_copy(
            pair_sum.at[tile - mine_start], arrived.at[tile], own_sems.at[1]
        )
        own.start()
        own.wait()

        @pl.loop(1, tile_count)
        def _(step):
            pltpu.make_async_remote_copy(
                src_ref=pair_sum.at[0],
                dst_ref=arrived.at[tile],
                send_sem=tile_send_sems.at[step],
                recv_sem=tile_recv_sems.at[step],
                device_id=tile_peer(step),
                device_id_type=mesh_id,
            ).wait_recv()

        def add_source(source, total):
            return total + arrived[source].astype(jnp.float32)

        partial[...] = lax.fori_loop(
            0, tile_count, add_source, jnp.zeros(partial.shape, jnp.float32)
        )
        held[plane] = partial[...]

        def plane_copy(step):
            return pltpu.make_async_remote_copy(
                src_ref=partial,
                dst_ref=held.at[plane],
                send_sem=zh_send_sems.at[step],
                recv_sem=zh_recv_sems.at[step],
                device_id=plane_peer(step),
                device_id_type=mesh_id,
            )

        @pl.loop(1, planes)
        def _(step):
            plane_copy(step).start()

        @pl.loop(1, planes)
        def _(step):
            plane_copy(step).wait()

        total = held[0]
        for source in range(1, planes):
            total = total + held[source]
        final[...] = total
        copy = final_copy()
        copy.start()
        copy.wait_send()

    @pl.when(jnp.logical_not(receiver))
    def _():
        final_copy().wait_recv()

    @pl.loop(0, half)
    def _(index):
        @pl.when(mine_start + index != tile)
        def _():
            sum_copy(index).wait_send()

    back_own.wait()

    @pl.loop(1, tile_count)
    def _(step):
        back_copy(step).wait()

    returned_ref[...] = returned_held[...]
    out_ref[...] = final[...]


def paired_sum(row_blocks, spread):
    rep_count = lax.axis_size("rep")
    col_tiles = lax.axis_size("tx")
    tile_count = row_blocks.shape[0]
    block_shape = row_blocks.shape[1:]
    half_shape = (tile_count // 2,) + block_shape
    return pl.pallas_call(
        functools.partial(paired_sum_kernel, rep_count, tile_count, col_tiles),
        out_shape=[
            jax.ShapeDtypeStruct(block_shape, jnp.float32),
            jax.ShapeDtypeStruct(spread.shape, spread.dtype),
        ],
        in_specs=[pl.BlockSpec(memory_space=pltpu.VMEM)] * 2,
        out_specs=[pl.BlockSpec(memory_space=pltpu.VMEM)] * 2,
        scratch_shapes=[
            pltpu.VMEM(half_shape, row_blocks.dtype),
            pltpu.VMEM(half_shape, row_blocks.dtype),
            pltpu.VMEM(row_blocks.shape, row_blocks.dtype),
            pltpu.VMEM(block_shape, jnp.float32),
            pltpu.VMEM((rep_count // 2,) + block_shape, jnp.float32),
            pltpu.VMEM(block_shape, jnp.float32),
            pltpu.VMEM(spread.shape, spread.dtype),
            pltpu.SemaphoreType.DMA((2,)),
            pltpu.SemaphoreType.DMA((tile_count,)),
            pltpu.SemaphoreType.DMA((tile_count,)),
            pltpu.SemaphoreType.DMA((rep_count // 2,)),
            pltpu.SemaphoreType.DMA((rep_count // 2,)),
            pltpu.SemaphoreType.DMA((2,)),
            pltpu.SemaphoreType.DMA((tile_count,)),
            pltpu.SemaphoreType.DMA((tile_count,)),
            pltpu.SemaphoreType.DMA((2,)),
        ],
        compiler_params=pltpu.CompilerParams(collective_id=2, has_side_effects=True),
    )(row_blocks, spread)


def balanced_sum_kernel(rep_count, tile_count, col_tiles, blocks_ref, spread_ref, out_ref,
                        returned_ref, pair_held, pair_sum, arrived, partial, held,
                        returned_held, pair_sems, sum_send_sems, sum_recv_sems, rep_send_sems,
                        rep_recv_sems, back_send_sems, back_recv_sems, own_sems):
    me = lax.axis_index("rep")
    row = lax.axis_index("ty")
    col = lax.axis_index("tx")
    tile = row * col_tiles + col
    core = lax.rem(me, 2)
    partner = me + 1 - 2 * core
    target_rep = me - core + lax.rem(tile, 2)
    half = tile_count // 2
    mine_start = core * half
    barrier = pltpu.get_barrier_semaphore()
    mesh_id = pl.DeviceIdType.MESH

    def tile_device(rep, peer):
        return (rep, peer // col_tiles, lax.rem(peer, col_tiles))

    def tile_peer(step):
        return tile_device(me, lax.rem(tile + step, tile_count))

    def rep_peer(step):
        return (lax.rem(me + step, rep_count), row, col)

    @pl.loop(1, tile_count)
    def _(step):
        pl.semaphore_signal(barrier, inc=1, device_id=tile_peer(step), device_id_type=mesh_id)

    @pl.loop(0, tile_count)
    def _(peer):
        pl.semaphore_signal(
            barrier, inc=1, device_id=tile_device(partner, peer), device_id_type=mesh_id
        )

    @pl.loop(1, rep_count)
    def _(step):
        @pl.when(lax.rem(me + step, rep_count) != partner)
        def _():
            pl.semaphore_signal(barrier, inc=1, device_id=rep_peer(step), device_id_type=mesh_id)

    pl.semaphore_wait(barrier, 2 * tile_count + rep_count - 3)

    pair_copy = pltpu.make_async_remote_copy(
        src_ref=blocks_ref.at[pl.ds((1 - core) * half, half)],
        dst_ref=pair_held,
        send_sem=pair_sems.at[0],
        recv_sem=pair_sems.at[1],
        device_id=(partner, row, col),
        device_id_type=mesh_id,
    )
    pair_copy.start()

    def back_copy(step):
        peer = lax.rem(tile + step, tile_count)
        return pltpu.make_async_remote_copy(
            src_ref=spread_ref.at[peer],
            dst_ref=returned_held.at[tile],
            send_sem=back_send_sems.at[step],
            recv_sem=back_recv_sems.at[step],
            device_id=tile_peer(step),
            device_id_type=mesh_id,
        )

    back_own = pltpu.make_async_copy(spread_ref.at[tile], returned_held.at[tile], own_sems.at[0])
    back_own.start()

    @pl.loop(1, tile_count)
    def _(step):
        back_copy(step).start()

    pair_copy.wait()

    @pl.loop(0, half)
    def _(index):
        pair_sum[index] = (
            blocks_ref[mine_start + index].astype(jnp.float32)
            + pair_held[index].astype(jnp.float32)
        ).astype(pair_sum.dtype)

    def is_self(target):
        return jnp.logical_and(target_rep == me, target == tile)

    def sum_copy(index):
        target = mine_start + index
        return pltpu.make_async_remote_copy(
            src_ref=pair_sum.at[index],
            dst_ref=arrived.at[tile],
            send_sem=sum_send_sems.at[index],
            recv_sem=sum_recv_sems.at[tile],
            device_id=tile_device(target_rep, target),
            device_id_type=mesh_id,
        )

    @pl.loop(0, half)
    def _(index):
        target = mine_start + index

        @pl.when(is_self(target))
        def _():
            own = pltpu.make_async_copy(pair_sum.at[index], arrived.at[tile], own_sems.at[1])
            own.start()
            own.wait()

        @pl.when(jnp.logical_not(is_self(target)))
        def _():
            sum_copy(index).start()

    @pl.loop(0, half)
    def _(index):
        source = core + 2 * index
        from_self = jnp.logical_and(source == tile, tile // half == core)

        @pl.when(jnp.logical_not(from_self))
        def _():
            pltpu.make_async_remote_copy(
                src_ref=pair_sum.at[0],
                dst_ref=arrived.at[source],
                send_sem=sum_send_sems.at[0],
                recv_sem=sum_recv_sems.at[source],
                device_id=tile_peer(1),
                device_id_type=mesh_id,
            ).wait_recv()

    def add_source(index, total):
        return total + arrived[core + 2 * index].astype(jnp.float32)

    partial[...] = lax.fori_loop(0, half, add_source, jnp.zeros(partial.shape, jnp.float32))
    held[me] = partial[...]

    def rep_copy(step):
        return pltpu.make_async_remote_copy(
            src_ref=partial,
            dst_ref=held.at[me],
            send_sem=rep_send_sems.at[step],
            recv_sem=rep_recv_sems.at[step],
            device_id=rep_peer(step),
            device_id_type=mesh_id,
        )

    @pl.loop(1, rep_count)
    def _(step):
        rep_copy(step).start()

    @pl.loop(1, rep_count)
    def _(step):
        rep_copy(step).wait()

    @pl.loop(0, half)
    def _(index):
        @pl.when(jnp.logical_not(is_self(mine_start + index)))
        def _():
            sum_copy(index).wait_send()

    back_own.wait()

    @pl.loop(1, tile_count)
    def _(step):
        back_copy(step).wait()

    returned_ref[...] = returned_held[...]
    total = held[0]
    for source in range(1, rep_count):
        total = total + held[source]
    out_ref[...] = total


def balanced_sum(row_blocks, spread):
    rep_count = lax.axis_size("rep")
    col_tiles = lax.axis_size("tx")
    tile_count = row_blocks.shape[0]
    block_shape = row_blocks.shape[1:]
    half_shape = (tile_count // 2,) + block_shape
    return pl.pallas_call(
        functools.partial(balanced_sum_kernel, rep_count, tile_count, col_tiles),
        out_shape=[
            jax.ShapeDtypeStruct(block_shape, jnp.float32),
            jax.ShapeDtypeStruct(spread.shape, spread.dtype),
        ],
        in_specs=[pl.BlockSpec(memory_space=pltpu.VMEM)] * 2,
        out_specs=[pl.BlockSpec(memory_space=pltpu.VMEM)] * 2,
        scratch_shapes=[
            pltpu.VMEM(half_shape, row_blocks.dtype),
            pltpu.VMEM(half_shape, row_blocks.dtype),
            pltpu.VMEM(row_blocks.shape, row_blocks.dtype),
            pltpu.VMEM(block_shape, jnp.float32),
            pltpu.VMEM((rep_count,) + block_shape, jnp.float32),
            pltpu.VMEM(spread.shape, spread.dtype),
            pltpu.SemaphoreType.DMA((2,)),
            pltpu.SemaphoreType.DMA((tile_count // 2,)),
            pltpu.SemaphoreType.DMA((tile_count,)),
            pltpu.SemaphoreType.DMA((rep_count,)),
            pltpu.SemaphoreType.DMA((rep_count,)),
            pltpu.SemaphoreType.DMA((tile_count,)),
            pltpu.SemaphoreType.DMA((tile_count,)),
            pltpu.SemaphoreType.DMA((2,)),
        ],
        compiler_params=pltpu.CompilerParams(collective_id=3, has_side_effects=True),
    )(row_blocks, spread)


def exchange_kernel(tile_count, col_tiles, tokens_ref, cot_ref, tokens_out, cot_out,
                    tokens_held, cot_held, send_sems, recv_sems, own_sems):
    me = lax.axis_index("rep")
    row = lax.axis_index("ty")
    col = lax.axis_index("tx")
    tile = row * col_tiles + col
    barrier = pltpu.get_barrier_semaphore()

    def tile_peer(step):
        peer = lax.rem(tile + step, tile_count)
        return (me, peer // col_tiles, lax.rem(peer, col_tiles))

    @pl.loop(1, tile_count)
    def _(step):
        pl.semaphore_signal(barrier, inc=1, device_id=tile_peer(step),
                            device_id_type=pl.DeviceIdType.MESH)

    pl.semaphore_wait(barrier, tile_count - 1)

    def tile_copies(step):
        peer = lax.rem(tile + step, tile_count)
        return [
            pltpu.make_async_remote_copy(
                src_ref=source.at[0, peer],
                dst_ref=held.at[tile],
                send_sem=send_sems.at[step, index],
                recv_sem=recv_sems.at[step, index],
                device_id=tile_peer(step),
                device_id_type=pl.DeviceIdType.MESH,
            )
            for index, (source, held) in enumerate(((tokens_ref, tokens_held), (cot_ref, cot_held)))
        ]

    own = [
        pltpu.make_async_copy(tokens_ref.at[0, tile], tokens_held.at[tile], own_sems.at[0]),
        pltpu.make_async_copy(cot_ref.at[0, tile], cot_held.at[tile], own_sems.at[1]),
    ]
    for copy in own:
        copy.start()

    @pl.loop(1, tile_count)
    def _(step):
        for copy in tile_copies(step):
            copy.start()

    for copy in own:
        copy.wait()

    @pl.loop(1, tile_count)
    def _(step):
        for copy in tile_copies(step):
            copy.wait()

    tokens_out[...] = tokens_held[...]
    cot_out[...] = cot_held[...]


def exchange(tokens, cotangent):
    col_tiles = lax.axis_size("tx")
    tile_count = lax.axis_size("ty") * col_tiles
    held_shape = (tile_count,) + tokens.shape[2:]
    return pl.pallas_call(
        functools.partial(exchange_kernel, tile_count, col_tiles),
        out_shape=[jax.ShapeDtypeStruct(held_shape, tokens.dtype)] * 2,
        in_specs=[pl.BlockSpec(memory_space=pltpu.VMEM)] * 2,
        out_specs=[pl.BlockSpec(memory_space=pltpu.VMEM)] * 2,
        scratch_shapes=[
            pltpu.VMEM(held_shape, tokens.dtype),
            pltpu.VMEM(held_shape, tokens.dtype),
            pltpu.SemaphoreType.DMA((tile_count, 2)),
            pltpu.SemaphoreType.DMA((tile_count, 2)),
            pltpu.SemaphoreType.DMA((2,)),
        ],
        compiler_params=pltpu.CompilerParams(collective_id=1, has_side_effects=True),
    )(tokens, cotangent)


def shards(tokens, qkv_weight, cotangent):
    rep_count = lax.axis_size("rep")
    row_tiles = lax.axis_size("ty")
    col_tiles = lax.axis_size("tx")
    tile_count = row_tiles * col_tiles
    tile_height = tokens.shape[1]
    tile_width = tokens.shape[2]
    channels = tokens.shape[3]
    stride_rows = row_tiles * tile_height // GRID
    stride_cols = col_tiles * tile_width // GRID
    block_rows = min(tile_height, stride_rows)
    fold_rows = stride_rows // block_rows
    col_groups = tile_width // stride_cols
    outer_rows = tile_height // block_rows
    inner_rows = block_rows // tile_count
    split_shape = (outer_rows, tile_count, inner_rows, tile_width, channels)
    if tile_height == tile_count and outer_rows == 1 and inner_rows == 1:
        grid_x, grid_g = (
            values.reshape(split_shape) for values in exchange(tokens, cotangent)
        )
    else:
        grid_x, grid_g = (
            lax.all_to_all(
                values.reshape(split_shape), ("ty", "tx"), split_axis=1, concat_axis=1, tiled=True
            )
            for values in (tokens, cotangent)
        )
    token_shape = (
        outer_rows,
        row_tiles // fold_rows,
        fold_rows,
        col_tiles,
        inner_rows,
        col_groups,
        stride_cols,
        channels,
    )
    win_count = fold_rows * inner_rows * stride_cols

    def to_windows(values):
        return (
            values.reshape(token_shape)
            .transpose(2, 4, 6, 1, 0, 3, 5, 7)
            .reshape(win_count, GRID * GRID, channels)
        )

    grad_windows, weight_term = window_grads(to_windows(grid_x), to_windows(grid_g), qkv_weight)
    back_shape = (
        fold_rows,
        inner_rows,
        stride_cols,
        row_tiles // fold_rows,
        outer_rows,
        col_tiles,
        col_groups,
        channels,
    )
    spread = grad_windows.reshape(back_shape).transpose(4, 3, 0, 5, 1, 6, 2, 7).reshape(split_shape)
    row_blocks = weight_term.reshape(tile_count, channels // tile_count, weight_term.shape[1])
    if tile_height == tile_count and outer_rows == 1 and inner_rows == 1:
        weight_grad, returned = balanced_sum(
            row_blocks.astype(jnp.bfloat16), spread.reshape((tile_count,) + tokens.shape[2:])
        )
    else:
        returned = lax.all_to_all(spread, ("ty", "tx"), split_axis=1, concat_axis=1, tiled=True)
        gathered = lax.all_to_all(row_blocks.astype(jnp.bfloat16), ("ty", "tx"), 0, 0, tiled=True)
        weight_grad = lax.psum(jnp.sum(gathered.astype(jnp.float32), axis=0), "rep")
    token_grad = returned.reshape(1, tile_height, tile_width, channels)
    weight_grad = weight_grad / (rep_count * tile_count)
    return (token_grad, weight_grad)


def solution(mesh):
    placed = (P("rep", "ty", "tx", None), P(), P("rep", "ty", "tx", None))
    return jax.shard_map(
        shards,
        mesh=mesh,
        in_specs=placed,
        out_specs=(P("rep", "ty", "tx", None), P(("ty", "tx"), None)),
        check_vma=False,
    )
```

```python
import functools

import jax
import jax.numpy as jnp
from jax import lax
from jax.experimental import pallas as pl
from jax.experimental.pallas import tpu as pltpu
from jax.sharding import PartitionSpec as P

HEADS = 16
HEAD_DIM = 32
GRID = 8


eps_norm = 1e-05


def normalize(values):
    center = values - jnp.mean(values, axis=-1, keepdims=True)
    inv_std = lax.rsqrt(jnp.mean(center * center, axis=-1, keepdims=True) + eps_norm)
    return (center * inv_std, inv_std)


def window_grads(window_x, window_g, qkv_weight):
    win_count, win_tokens, channels = window_x.shape
    standard, inv_std = normalize(window_x.astype(jnp.float32))
    normed = standard.astype(jnp.bfloat16).reshape(win_count * win_tokens, channels)
    projection = jnp.dot(normed, qkv_weight, preferred_element_type=jnp.float32)
    flat_shape = (win_count, win_tokens, channels)
    query = (projection[:, :channels] * HEAD_DIM ** (-0.5)).astype(jnp.bfloat16).reshape(flat_shape)
    key = projection[:, channels : 2 * channels].astype(jnp.bfloat16).reshape(flat_shape)
    value = projection[:, 2 * channels :].astype(jnp.bfloat16).reshape(flat_shape)
    grad = window_g.astype(jnp.bfloat16)
    head_mask = (
        lax.broadcasted_iota(jnp.int32, (HEADS, channels), 1) // HEAD_DIM
        == lax.broadcasted_iota(jnp.int32, (HEADS, channels), 0)
    ).astype(jnp.bfloat16)

    def spread(values):
        return values[:, None, :, :] * head_mask[None, :, None, :]

    query_spread = spread(query)
    grad_spread = spread(grad)
    scores = jnp.einsum("wnqc,wkc->wnqk", query_spread, key, preferred_element_type=jnp.float32)
    peak_score = jnp.max(scores, axis=-1, keepdims=True)
    exponent = jnp.exp(scores - peak_score)
    attn_probs = exponent / jnp.sum(exponent, axis=-1, keepdims=True)
    probs_low = attn_probs.astype(jnp.bfloat16)
    attn_grad = jnp.einsum("wnqc,wkc->wnqk", grad_spread, value, preferred_element_type=jnp.float32)
    value_grad = jnp.einsum(
        "wnqk,wnqc->wkc", probs_low, grad_spread, preferred_element_type=jnp.float32
    ).astype(jnp.bfloat16)
    score_grad = (
        attn_probs * (attn_grad - jnp.sum(attn_probs * attn_grad, axis=-1, keepdims=True))
    ).astype(jnp.bfloat16)
    key_grad = jnp.einsum(
        "wnqk,wnqc->wkc", score_grad, query_spread, preferred_element_type=jnp.float32
    ).astype(jnp.bfloat16)
    query_full = jnp.einsum("wnqk,wkc->wnqc", score_grad, key, preferred_element_type=jnp.float32)
    query_grad = (
        jnp.sum(query_full * head_mask[None, :, None, :].astype(jnp.float32), axis=1)
        * HEAD_DIM ** (-0.5)
    ).astype(jnp.bfloat16)
    flat_shape = (win_count * win_tokens, channels)
    proj_grad = jnp.concatenate(
        [
            query_grad.reshape(flat_shape),
            key_grad.reshape(flat_shape),
            value_grad.reshape(flat_shape),
        ],
        axis=1,
    )
    normed_grad = lax.dot_general(
        proj_grad, qkv_weight, (((1,), (1,)), ((), ())), preferred_element_type=jnp.float32
    )
    normed_grad = normed_grad.reshape(win_count, win_tokens, channels)
    weight_term = lax.dot_general(
        normed, proj_grad, (((0,), (0,)), ((), ())), preferred_element_type=jnp.float32
    )
    inner_term = (
        normed_grad
        - jnp.mean(normed_grad, axis=-1, keepdims=True)
        - standard * jnp.mean(normed_grad * standard, axis=-1, keepdims=True)
    )
    token_grad = (window_g.astype(jnp.float32) + inv_std * inner_term).astype(jnp.bfloat16)
    return (token_grad, weight_term)


def weight_sum_kernel(rep_count, tile_count, col_tiles, blocks_ref, spread_ref, out_ref,
                      returned_ref, arrived, partial, held, returned_held, send_sems, recv_sems,
                      rep_send_sems, rep_recv_sems, back_send_sems, back_recv_sems, back_own_sem):
    me = lax.axis_index("rep")
    row = lax.axis_index("ty")
    col = lax.axis_index("tx")
    tile = row * col_tiles + col
    barrier = pltpu.get_barrier_semaphore()

    def tile_peer(step):
        peer = lax.rem(tile + step, tile_count)
        return (me, peer // col_tiles, lax.rem(peer, col_tiles))

    def rep_peer(step):
        return (lax.rem(me + step, rep_count), row, col)

    @pl.loop(1, tile_count)
    def _(step):
        pl.semaphore_signal(barrier, inc=1, device_id=tile_peer(step),
                            device_id_type=pl.DeviceIdType.MESH)

    @pl.loop(1, rep_count)
    def _(step):
        pl.semaphore_signal(barrier, inc=1, device_id=rep_peer(step),
                            device_id_type=pl.DeviceIdType.MESH)

    pl.semaphore_wait(barrier, tile_count + rep_count - 2)

    def back_copy(step):
        peer = lax.rem(tile + step, tile_count)
        return pltpu.make_async_remote_copy(
            src_ref=spread_ref.at[peer],
            dst_ref=returned_held.at[tile],
            send_sem=back_send_sems.at[step],
            recv_sem=back_recv_sems.at[step],
            device_id=tile_peer(step),
            device_id_type=pl.DeviceIdType.MESH,
        )

    back_own = pltpu.make_async_copy(spread_ref.at[tile], returned_held.at[tile], back_own_sem.at[0])
    back_own.start()

    @pl.loop(1, tile_count)
    def _(step):
        back_copy(step).start()

    def tile_copy(step):
        peer = lax.rem(tile + step, tile_count)
        return pltpu.make_async_remote_copy(
            src_ref=blocks_ref.at[peer],
            dst_ref=arrived.at[tile],
            send_sem=send_sems.at[step],
            recv_sem=recv_sems.at[step],
            device_id=tile_peer(step),
            device_id_type=pl.DeviceIdType.MESH,
        )

    own = pltpu.make_async_copy(blocks_ref.at[tile], arrived.at[tile], send_sems.at[0])
    own.start()

    @pl.loop(1, tile_count)
    def _(step):
        tile_copy(step).start()

    own.wait()

    @pl.loop(1, tile_count)
    def _(step):
        tile_copy(step).wait()

    def add_source(source, total):
        return total + arrived[source].astype(jnp.float32)

    partial[...] = lax.fori_loop(
        0, tile_count, add_source, jnp.zeros(partial.shape, jnp.float32)
    )
    held[me] = partial[...]

    def rep_copy(step):
        return pltpu.make_async_remote_copy(
            src_ref=partial,
            dst_ref=held.at[me],
            send_sem=rep_send_sems.at[step],
            recv_sem=rep_recv_sems.at[step],
            device_id=rep_peer(step),
            device_id_type=pl.DeviceIdType.MESH,
        )

    @pl.loop(1, rep_count)
    def _(step):
        rep_copy(step).start()

    @pl.loop(1, rep_count)
    def _(step):
        rep_copy(step).wait()

    back_own.wait()

    @pl.loop(1, tile_count)
    def _(step):
        back_copy(step).wait()

    returned_ref[...] = returned_held[...]
    total = held[0]
    for source in range(1, rep_count):
        total = total + held[source]
    out_ref[...] = total


def weight_sum(row_blocks, spread):
    rep_count = lax.axis_size("rep")
    col_tiles = lax.axis_size("tx")
    tile_count = row_blocks.shape[0]
    block_shape = row_blocks.shape[1:]
    return pl.pallas_call(
        functools.partial(weight_sum_kernel, rep_count, tile_count, col_tiles),
        out_shape=[
            jax.ShapeDtypeStruct(block_shape, jnp.float32),
            jax.ShapeDtypeStruct(spread.shape, spread.dtype),
        ],
        in_specs=[pl.BlockSpec(memory_space=pltpu.VMEM)] * 2,
        out_specs=[pl.BlockSpec(memory_space=pltpu.VMEM)] * 2,
        scratch_shapes=[
            pltpu.VMEM(row_blocks.shape, row_blocks.dtype),
            pltpu.VMEM(block_shape, jnp.float32),
            pltpu.VMEM((rep_count,) + block_shape, jnp.float32),
            pltpu.VMEM(spread.shape, spread.dtype),
            pltpu.SemaphoreType.DMA((tile_count,)),
            pltpu.SemaphoreType.DMA((tile_count,)),
            pltpu.SemaphoreType.DMA((rep_count,)),
            pltpu.SemaphoreType.DMA((rep_count,)),
            pltpu.SemaphoreType.DMA((tile_count,)),
            pltpu.SemaphoreType.DMA((tile_count,)),
            pltpu.SemaphoreType.DMA((1,)),
        ],
        compiler_params=pltpu.CompilerParams(collective_id=0, has_side_effects=True),
    )(row_blocks, spread)


def paired_sum_kernel(rep_count, tile_count, col_tiles, blocks_ref, spread_ref, out_ref,
                      returned_ref, pair_held, pair_sum, arrived, partial, held, final,
                      returned_held, pair_sems, tile_send_sems, tile_recv_sems, zh_send_sems,
                      zh_recv_sems, final_sems, back_send_sems, back_recv_sems, own_sems):
    me = lax.axis_index("rep")
    row = lax.axis_index("ty")
    col = lax.axis_index("tx")
    tile = row * col_tiles + col
    core = lax.rem(me, 2)
    plane = me // 2
    planes = rep_count // 2
    partner = me + 1 - 2 * core
    half = tile_count // 2
    mine_start = core * half
    receiver = tile // half == core
    barrier = pltpu.get_barrier_semaphore()

    def tile_device(peer):
        return (me, peer // col_tiles, lax.rem(peer, col_tiles))

    def tile_peer(step):
        return tile_device(lax.rem(tile + step, tile_count))

    def plane_peer(step):
        return (2 * lax.rem(plane + step, planes) + core, row, col)

    mesh_id = pl.DeviceIdType.MESH
    pl.semaphore_signal(barrier, inc=1, device_id=(partner, row, col), device_id_type=mesh_id)

    @pl.loop(1, tile_count)
    def _(step):
        pl.semaphore_signal(barrier, inc=1, device_id=tile_peer(step), device_id_type=mesh_id)

    @pl.when(receiver)
    def _():
        @pl.loop(1, planes)
        def _(step):
            pl.semaphore_signal(barrier, inc=1, device_id=plane_peer(step), device_id_type=mesh_id)

    pl.semaphore_wait(barrier, tile_count + (planes - 1) * receiver.astype(jnp.int32))

    pair_copy = pltpu.make_async_remote_copy(
        src_ref=blocks_ref.at[pl.ds((1 - core) * half, half)],
        dst_ref=pair_held,
        send_sem=pair_sems.at[0],
        recv_sem=pair_sems.at[1],
        device_id=(partner, row, col),
        device_id_type=mesh_id,
    )
    pair_copy.start()

    def back_copy(step):
        peer = lax.rem(tile + step, tile_count)
        return pltpu.make_async_remote_copy(
            src_ref=spread_ref.at[peer],
            dst_ref=returned_held.at[tile],
            send_sem=back_send_sems.at[step],
            recv_sem=back_recv_sems.at[step],
            device_id=tile_peer(step),
            device_id_type=mesh_id,
        )

    back_own = pltpu.make_async_copy(spread_ref.at[tile], returned_held.at[tile], own_sems.at[0])
    back_own.start()

    @pl.loop(1, tile_count)
    def _(step):
        back_copy(step).start()

    pair_copy.wait()

    @pl.loop(0, half)
    def _(index):
        pair_sum[index] = (
            blocks_ref[mine_start + index].astype(jnp.float32)
            + pair_held[index].astype(jnp.float32)
        ).astype(pair_sum.dtype)

    def sum_copy(index):
        target = mine_start + index
        step = lax.rem(target - tile + tile_count, tile_count)
        return pltpu.make_async_remote_copy(
            src_ref=pair_sum.at[index],
            dst_ref=arrived.at[tile],
            send_sem=tile_send_sems.at[step],
            recv_sem=tile_recv_sems.at[step],
            device_id=tile_device(target),
            device_id_type=mesh_id,
        )

    @pl.loop(0, half)
    def _(index):
        @pl.when(mine_start + index != tile)
        def _():
            sum_copy(index).start()

    def final_copy():
        return pltpu.make_async_remote_copy(
            src_ref=final,
            dst_ref=final,
            send_sem=final_sems.at[0],
            recv_sem=final_sems.at[1],
            device_id=(partner, row, col),
            device_id_type=mesh_id,
        )

    @pl.when(receiver)
    def _():
        own = pltpu.make_async_copy(
            pair_sum.at[tile - mine_start], arrived.at[tile], own_sems.at[1]
        )
        own.start()
        own.wait()

        @pl.loop(1, tile_count)
        def _(step):
            pltpu.make_async_remote_copy(
                src_ref=pair_sum.at[0],
                dst_ref=arrived.at[tile],
                send_sem=tile_send_sems.at[step],
                recv_sem=tile_recv_sems.at[step],
                device_id=tile_peer(step),
                device_id_type=mesh_id,
            ).wait_recv()

        def add_source(source, total):
            return total + arrived[source].astype(jnp.float32)

        partial[...] = lax.fori_loop(
            0, tile_count, add_source, jnp.zeros(partial.shape, jnp.float32)
        )
        held[plane] = partial[...]

        def plane_copy(step):
            return pltpu.make_async_remote_copy(
                src_ref=partial,
                dst_ref=held.at[plane],
                send_sem=zh_send_sems.at[step],
                recv_sem=zh_recv_sems.at[step],
                device_id=plane_peer(step),
                device_id_type=mesh_id,
            )

        @pl.loop(1, planes)
        def _(step):
            plane_copy(step).start()

        @pl.loop(1, planes)
        def _(step):
            plane_copy(step).wait()

        total = held[0]
        for source in range(1, planes):
            total = total + held[source]
        final[...] = total
        copy = final_copy()
        copy.start()
        copy.wait_send()

    @pl.when(jnp.logical_not(receiver))
    def _():
        final_copy().wait_recv()

    @pl.loop(0, half)
    def _(index):
        @pl.when(mine_start + index != tile)
        def _():
            sum_copy(index).wait_send()

    back_own.wait()

    @pl.loop(1, tile_count)
    def _(step):
        back_copy(step).wait()

    returned_ref[...] = returned_held[...]
    out_ref[...] = final[...]


def paired_sum(row_blocks, spread):
    rep_count = lax.axis_size("rep")
    col_tiles = lax.axis_size("tx")
    tile_count = row_blocks.shape[0]
    block_shape = row_blocks.shape[1:]
    half_shape = (tile_count // 2,) + block_shape
    return pl.pallas_call(
        functools.partial(paired_sum_kernel, rep_count, tile_count, col_tiles),
        out_shape=[
            jax.ShapeDtypeStruct(block_shape, jnp.float32),
            jax.ShapeDtypeStruct(spread.shape, spread.dtype),
        ],
        in_specs=[pl.BlockSpec(memory_space=pltpu.VMEM)] * 2,
        out_specs=[pl.BlockSpec(memory_space=pltpu.VMEM)] * 2,
        scratch_shapes=[
            pltpu.VMEM(half_shape, row_blocks.dtype),
            pltpu.VMEM(half_shape, row_blocks.dtype),
            pltpu.VMEM(row_blocks.shape, row_blocks.dtype),
            pltpu.VMEM(block_shape, jnp.float32),
            pltpu.VMEM((rep_count // 2,) + block_shape, jnp.float32),
            pltpu.VMEM(block_shape, jnp.float32),
            pltpu.VMEM(spread.shape, spread.dtype),
            pltpu.SemaphoreType.DMA((2,)),
            pltpu.SemaphoreType.DMA((tile_count,)),
            pltpu.SemaphoreType.DMA((tile_count,)),
            pltpu.SemaphoreType.DMA((rep_count // 2,)),
            pltpu.SemaphoreType.DMA((rep_count // 2,)),
            pltpu.SemaphoreType.DMA((2,)),
            pltpu.SemaphoreType.DMA((tile_count,)),
            pltpu.SemaphoreType.DMA((tile_count,)),
            pltpu.SemaphoreType.DMA((2,)),
        ],
        compiler_params=pltpu.CompilerParams(collective_id=2, has_side_effects=True),
    )(row_blocks, spread)


def exchange_kernel(tile_count, col_tiles, rows_ref, rows_out, held, send_sems, recv_sems,
                    own_sems):
    me = lax.axis_index("rep")
    row = lax.axis_index("ty")
    col = lax.axis_index("tx")
    tile = row * col_tiles + col
    barrier = pltpu.get_barrier_semaphore()

    def tile_peer(step):
        peer = lax.rem(tile + step, tile_count)
        return (me, peer // col_tiles, lax.rem(peer, col_tiles))

    @pl.loop(1, tile_count)
    def _(step):
        pl.semaphore_signal(barrier, inc=1, device_id=tile_peer(step),
                            device_id_type=pl.DeviceIdType.MESH)

    pl.semaphore_wait(barrier, tile_count - 1)

    def tile_copy(step):
        peer = lax.rem(tile + step, tile_count)
        return pltpu.make_async_remote_copy(
            src_ref=rows_ref.at[peer],
            dst_ref=held.at[tile],
            send_sem=send_sems.at[step],
            recv_sem=recv_sems.at[step],
            device_id=tile_peer(step),
            device_id_type=pl.DeviceIdType.MESH,
        )

    own = pltpu.make_async_copy(rows_ref.at[tile], held.at[tile], own_sems.at[0])
    own.start()

    @pl.loop(1, tile_count)
    def _(step):
        tile_copy(step).start()

    own.wait()

    @pl.loop(1, tile_count)
    def _(step):
        tile_copy(step).wait()

    rows_out[...] = held[...]


def exchange(tokens, cotangent):
    col_tiles = lax.axis_size("tx")
    tile_count = lax.axis_size("ty") * col_tiles
    row_shape = (tile_count,) + tokens.shape[2:]
    rows = jnp.stack([tokens.reshape(row_shape), cotangent.reshape(row_shape)], axis=1)
    held = pl.pallas_call(
        functools.partial(exchange_kernel, tile_count, col_tiles),
        out_shape=jax.ShapeDtypeStruct(rows.shape, rows.dtype),
        in_specs=[pl.BlockSpec(memory_space=pltpu.VMEM)],
        out_specs=pl.BlockSpec(memory_space=pltpu.VMEM),
        scratch_shapes=[
            pltpu.VMEM(rows.shape, rows.dtype),
            pltpu.SemaphoreType.DMA((tile_count,)),
            pltpu.SemaphoreType.DMA((tile_count,)),
            pltpu.SemaphoreType.DMA((1,)),
        ],
        compiler_params=pltpu.CompilerParams(collective_id=1, has_side_effects=True),
    )(rows)
    return held[:, 0], held[:, 1]


def shards(tokens, qkv_weight, cotangent):
    rep_count = lax.axis_size("rep")
    row_tiles = lax.axis_size("ty")
    col_tiles = lax.axis_size("tx")
    tile_count = row_tiles * col_tiles
    tile_height = tokens.shape[1]
    tile_width = tokens.shape[2]
    channels = tokens.shape[3]
    stride_rows = row_tiles * tile_height // GRID
    stride_cols = col_tiles * tile_width // GRID
    block_rows = min(tile_height, stride_rows)
    fold_rows = stride_rows // block_rows
    col_groups = tile_width // stride_cols
    outer_rows = tile_height // block_rows
    inner_rows = block_rows // tile_count
    split_shape = (outer_rows, tile_count, inner_rows, tile_width, channels)
    if tile_height == tile_count and outer_rows == 1 and inner_rows == 1:
        grid_x, grid_g = (
            values.reshape(split_shape) for values in exchange(tokens, cotangent)
        )
    else:
        grid_x, grid_g = (
            lax.all_to_all(
                values.reshape(split_shape), ("ty", "tx"), split_axis=1, concat_axis=1, tiled=True
            )
            for values in (tokens, cotangent)
        )
    token_shape = (
        outer_rows,
        row_tiles // fold_rows,
        fold_rows,
        col_tiles,
        inner_rows,
        col_groups,
        stride_cols,
        channels,
    )
    win_count = fold_rows * inner_rows * stride_cols

    def to_windows(values):
        return (
            values.reshape(token_shape)
            .transpose(2, 4, 6, 1, 0, 3, 5, 7)
            .reshape(win_count, GRID * GRID, channels)
        )

    grad_windows, weight_term = window_grads(to_windows(grid_x), to_windows(grid_g), qkv_weight)
    back_shape = (
        fold_rows,
        inner_rows,
        stride_cols,
        row_tiles // fold_rows,
        outer_rows,
        col_tiles,
        col_groups,
        channels,
    )
    spread = grad_windows.reshape(back_shape).transpose(4, 3, 0, 5, 1, 6, 2, 7).reshape(split_shape)
    row_blocks = weight_term.reshape(tile_count, channels // tile_count, weight_term.shape[1])
    if tile_height == tile_count and outer_rows == 1 and inner_rows == 1:
        weight_grad, returned = paired_sum(
            row_blocks.astype(jnp.bfloat16), spread.reshape((tile_count,) + tokens.shape[2:])
        )
    else:
        returned = lax.all_to_all(spread, ("ty", "tx"), split_axis=1, concat_axis=1, tiled=True)
        gathered = lax.all_to_all(row_blocks.astype(jnp.bfloat16), ("ty", "tx"), 0, 0, tiled=True)
        weight_grad = lax.psum(jnp.sum(gathered.astype(jnp.float32), axis=0), "rep")
    token_grad = returned.reshape(1, tile_height, tile_width, channels)
    weight_grad = weight_grad / (rep_count * tile_count)
    return (token_grad, weight_grad)


def solution(mesh):
    placed = (P("rep", "ty", "tx", None), P(), P("rep", "ty", "tx", None))
    return jax.shard_map(
        shards,
        mesh=mesh,
        in_specs=placed,
        out_specs=(P("rep", "ty", "tx", None), P(("ty", "tx"), None)),
        check_vma=False,
    )
```

```python
import functools

import jax
import jax.numpy as jnp
from jax import lax
from jax.experimental import pallas as pl
from jax.experimental.pallas import tpu as pltpu
from jax.sharding import PartitionSpec as P

HEADS = 16
HEAD_DIM = 32
GRID = 8


eps_norm = 1e-05


def normalize(values):
    center = values - jnp.mean(values, axis=-1, keepdims=True)
    inv_std = lax.rsqrt(jnp.mean(center * center, axis=-1, keepdims=True) + eps_norm)
    return (center * inv_std, inv_std)


def window_grads(window_x, window_g, qkv_weight):
    win_count, win_tokens, channels = window_x.shape
    standard, inv_std = normalize(window_x.astype(jnp.float32))
    normed = standard.astype(jnp.bfloat16).reshape(win_count * win_tokens, channels)
    projection = jnp.dot(normed, qkv_weight, preferred_element_type=jnp.float32)
    flat_shape = (win_count, win_tokens, channels)
    query = (projection[:, :channels] * HEAD_DIM ** (-0.5)).astype(jnp.bfloat16).reshape(flat_shape)
    key = projection[:, channels : 2 * channels].astype(jnp.bfloat16).reshape(flat_shape)
    value = projection[:, 2 * channels :].astype(jnp.bfloat16).reshape(flat_shape)
    grad = window_g.astype(jnp.bfloat16)
    head_mask = (
        lax.broadcasted_iota(jnp.int32, (HEADS, channels), 1) // HEAD_DIM
        == lax.broadcasted_iota(jnp.int32, (HEADS, channels), 0)
    ).astype(jnp.bfloat16)

    def spread(values):
        return values[:, None, :, :] * head_mask[None, :, None, :]

    query_spread = spread(query)
    grad_spread = spread(grad)
    scores = jnp.einsum("wnqc,wkc->wnqk", query_spread, key, preferred_element_type=jnp.float32)
    peak_score = jnp.max(scores, axis=-1, keepdims=True)
    exponent = jnp.exp(scores - peak_score)
    attn_probs = exponent / jnp.sum(exponent, axis=-1, keepdims=True)
    probs_low = attn_probs.astype(jnp.bfloat16)
    attn_grad = jnp.einsum("wnqc,wkc->wnqk", grad_spread, value, preferred_element_type=jnp.float32)
    value_grad = jnp.einsum(
        "wnqk,wnqc->wkc", probs_low, grad_spread, preferred_element_type=jnp.float32
    ).astype(jnp.bfloat16)
    score_grad = (
        attn_probs * (attn_grad - jnp.sum(attn_probs * attn_grad, axis=-1, keepdims=True))
    ).astype(jnp.bfloat16)
    key_grad = jnp.einsum(
        "wnqk,wnqc->wkc", score_grad, query_spread, preferred_element_type=jnp.float32
    ).astype(jnp.bfloat16)
    query_full = jnp.einsum("wnqk,wkc->wnqc", score_grad, key, preferred_element_type=jnp.float32)
    query_grad = (
        jnp.sum(query_full * head_mask[None, :, None, :].astype(jnp.float32), axis=1)
        * HEAD_DIM ** (-0.5)
    ).astype(jnp.bfloat16)
    flat_shape = (win_count * win_tokens, channels)
    proj_grad = jnp.concatenate(
        [
            query_grad.reshape(flat_shape),
            key_grad.reshape(flat_shape),
            value_grad.reshape(flat_shape),
        ],
        axis=1,
    )
    normed_grad = lax.dot_general(
        proj_grad, qkv_weight, (((1,), (1,)), ((), ())), preferred_element_type=jnp.float32
    )
    normed_grad = normed_grad.reshape(win_count, win_tokens, channels)
    weight_term = lax.dot_general(
        normed, proj_grad, (((0,), (0,)), ((), ())), preferred_element_type=jnp.float32
    )
    inner_term = (
        normed_grad
        - jnp.mean(normed_grad, axis=-1, keepdims=True)
        - standard * jnp.mean(normed_grad * standard, axis=-1, keepdims=True)
    )
    token_grad = (window_g.astype(jnp.float32) + inv_std * inner_term).astype(jnp.bfloat16)
    return (token_grad, weight_term)


def weight_sum_kernel(rep_count, tile_count, col_tiles, blocks_ref, spread_ref, out_ref,
                      returned_ref, arrived, partial, held, returned_held, send_sems, recv_sems,
                      rep_send_sems, rep_recv_sems, back_send_sems, back_recv_sems, back_own_sem):
    me = lax.axis_index("rep")
    row = lax.axis_index("ty")
    col = lax.axis_index("tx")
    tile = row * col_tiles + col
    barrier = pltpu.get_barrier_semaphore()

    def tile_peer(step):
        peer = lax.rem(tile + step, tile_count)
        return (me, peer // col_tiles, lax.rem(peer, col_tiles))

    def rep_peer(step):
        return (lax.rem(me + step, rep_count), row, col)

    @pl.loop(1, tile_count)
    def _(step):
        pl.semaphore_signal(barrier, inc=1, device_id=tile_peer(step),
                            device_id_type=pl.DeviceIdType.MESH)

    @pl.loop(1, rep_count)
    def _(step):
        pl.semaphore_signal(barrier, inc=1, device_id=rep_peer(step),
                            device_id_type=pl.DeviceIdType.MESH)

    pl.semaphore_wait(barrier, tile_count + rep_count - 2)

    def back_copy(step):
        peer = lax.rem(tile + step, tile_count)
        return pltpu.make_async_remote_copy(
            src_ref=spread_ref.at[peer],
            dst_ref=returned_held.at[tile],
            send_sem=back_send_sems.at[step],
            recv_sem=back_recv_sems.at[step],
            device_id=tile_peer(step),
            device_id_type=pl.DeviceIdType.MESH,
        )

    back_own = pltpu.make_async_copy(spread_ref.at[tile], returned_held.at[tile], back_own_sem.at[0])
    back_own.start()

    @pl.loop(1, tile_count)
    def _(step):
        back_copy(step).start()

    def tile_copy(step):
        peer = lax.rem(tile + step, tile_count)
        return pltpu.make_async_remote_copy(
            src_ref=blocks_ref.at[peer],
            dst_ref=arrived.at[tile],
            send_sem=send_sems.at[step],
            recv_sem=recv_sems.at[step],
            device_id=tile_peer(step),
            device_id_type=pl.DeviceIdType.MESH,
        )

    own = pltpu.make_async_copy(blocks_ref.at[tile], arrived.at[tile], send_sems.at[0])
    own.start()

    @pl.loop(1, tile_count)
    def _(step):
        tile_copy(step).start()

    own.wait()

    @pl.loop(1, tile_count)
    def _(step):
        tile_copy(step).wait()

    def add_source(source, total):
        return total + arrived[source].astype(jnp.float32)

    partial[...] = lax.fori_loop(
        0, tile_count, add_source, jnp.zeros(partial.shape, jnp.float32)
    )
    held[me] = partial[...]

    def rep_copy(step):
        return pltpu.make_async_remote_copy(
            src_ref=partial,
            dst_ref=held.at[me],
            send_sem=rep_send_sems.at[step],
            recv_sem=rep_recv_sems.at[step],
            device_id=rep_peer(step),
            device_id_type=pl.DeviceIdType.MESH,
        )

    @pl.loop(1, rep_count)
    def _(step):
        rep_copy(step).start()

    @pl.loop(1, rep_count)
    def _(step):
        rep_copy(step).wait()

    back_own.wait()

    @pl.loop(1, tile_count)
    def _(step):
        back_copy(step).wait()

    returned_ref[...] = returned_held[...]
    total = held[0]
    for source in range(1, rep_count):
        total = total + held[source]
    out_ref[...] = total


def weight_sum(row_blocks, spread):
    rep_count = lax.axis_size("rep")
    col_tiles = lax.axis_size("tx")
    tile_count = row_blocks.shape[0]
    block_shape = row_blocks.shape[1:]
    return pl.pallas_call(
        functools.partial(weight_sum_kernel, rep_count, tile_count, col_tiles),
        out_shape=[
            jax.ShapeDtypeStruct(block_shape, jnp.float32),
            jax.ShapeDtypeStruct(spread.shape, spread.dtype),
        ],
        in_specs=[pl.BlockSpec(memory_space=pltpu.VMEM)] * 2,
        out_specs=[pl.BlockSpec(memory_space=pltpu.VMEM)] * 2,
        scratch_shapes=[
            pltpu.VMEM(row_blocks.shape, row_blocks.dtype),
            pltpu.VMEM(block_shape, jnp.float32),
            pltpu.VMEM((rep_count,) + block_shape, jnp.float32),
            pltpu.VMEM(spread.shape, spread.dtype),
            pltpu.SemaphoreType.DMA((tile_count,)),
            pltpu.SemaphoreType.DMA((tile_count,)),
            pltpu.SemaphoreType.DMA((rep_count,)),
            pltpu.SemaphoreType.DMA((rep_count,)),
            pltpu.SemaphoreType.DMA((tile_count,)),
            pltpu.SemaphoreType.DMA((tile_count,)),
            pltpu.SemaphoreType.DMA((1,)),
        ],
        compiler_params=pltpu.CompilerParams(collective_id=0, has_side_effects=True),
    )(row_blocks, spread)


def paired_sum_kernel(rep_count, tile_count, col_tiles, blocks_ref, spread_ref, out_ref,
                      returned_ref, pair_held, pair_sum, arrived, partial, held, final,
                      returned_held, pair_sems, tile_send_sems, tile_recv_sems, zh_send_sems,
                      zh_recv_sems, final_sems, back_send_sems, back_recv_sems, own_sems):
    me = lax.axis_index("rep")
    row = lax.axis_index("ty")
    col = lax.axis_index("tx")
    tile = row * col_tiles + col
    core = lax.rem(me, 2)
    plane = me // 2
    planes = rep_count // 2
    partner = me + 1 - 2 * core
    half = tile_count // 2
    mine_start = core * half
    receiver = tile // half == core
    barrier = pltpu.get_barrier_semaphore()

    def tile_device(peer):
        return (me, peer // col_tiles, lax.rem(peer, col_tiles))

    def tile_peer(step):
        return tile_device(lax.rem(tile + step, tile_count))

    def plane_peer(step):
        return (2 * lax.rem(plane + step, planes) + core, row, col)

    mesh_id = pl.DeviceIdType.MESH
    pl.semaphore_signal(barrier, inc=1, device_id=(partner, row, col), device_id_type=mesh_id)

    @pl.loop(1, tile_count)
    def _(step):
        pl.semaphore_signal(barrier, inc=1, device_id=tile_peer(step), device_id_type=mesh_id)

    @pl.when(receiver)
    def _():
        @pl.loop(1, planes)
        def _(step):
            pl.semaphore_signal(barrier, inc=1, device_id=plane_peer(step), device_id_type=mesh_id)

    pl.semaphore_wait(barrier, tile_count + (planes - 1) * receiver.astype(jnp.int32))

    pair_copy = pltpu.make_async_remote_copy(
        src_ref=blocks_ref.at[pl.ds((1 - core) * half, half)],
        dst_ref=pair_held,
        send_sem=pair_sems.at[0],
        recv_sem=pair_sems.at[1],
        device_id=(partner, row, col),
        device_id_type=mesh_id,
    )
    pair_copy.start()

    def back_copy(step):
        peer = lax.rem(tile + step, tile_count)
        return pltpu.make_async_remote_copy(
            src_ref=spread_ref.at[peer],
            dst_ref=returned_held.at[tile],
            send_sem=back_send_sems.at[step],
            recv_sem=back_recv_sems.at[step],
            device_id=tile_peer(step),
            device_id_type=mesh_id,
        )

    back_own = pltpu.make_async_copy(spread_ref.at[tile], returned_held.at[tile], own_sems.at[0])

    pair_copy.wait()

    @pl.loop(0, half)
    def _(index):
        pair_sum[index] = (
            blocks_ref[mine_start + index].astype(jnp.float32)
            + pair_held[index].astype(jnp.float32)
        ).astype(pair_sum.dtype)

    def sum_copy(index):
        target = mine_start + index
        step = lax.rem(target - tile + tile_count, tile_count)
        return pltpu.make_async_remote_copy(
            src_ref=pair_sum.at[index],
            dst_ref=arrived.at[tile],
            send_sem=tile_send_sems.at[step],
            recv_sem=tile_recv_sems.at[step],
            device_id=tile_device(target),
            device_id_type=mesh_id,
        )

    @pl.loop(0, half)
    def _(index):
        @pl.when(mine_start + index != tile)
        def _():
            sum_copy(index).start()

    back_own.start()

    @pl.loop(1, tile_count)
    def _(step):
        back_copy(step).start()

    def final_copy():
        return pltpu.make_async_remote_copy(
            src_ref=final,
            dst_ref=final,
            send_sem=final_sems.at[0],
            recv_sem=final_sems.at[1],
            device_id=(partner, row, col),
            device_id_type=mesh_id,
        )

    @pl.when(receiver)
    def _():
        own = pltpu.make_async_copy(
            pair_sum.at[tile - mine_start], arrived.at[tile], own_sems.at[1]
        )
        own.start()
        own.wait()

        @pl.loop(1, tile_count)
        def _(step):
            pltpu.make_async_remote_copy(
                src_ref=pair_sum.at[0],
                dst_ref=arrived.at[tile],
                send_sem=tile_send_sems.at[step],
                recv_sem=tile_recv_sems.at[step],
                device_id=tile_peer(step),
                device_id_type=mesh_id,
            ).wait_recv()

        def add_source(source, total):
            return total + arrived[source].astype(jnp.float32)

        partial[...] = lax.fori_loop(
            0, tile_count, add_source, jnp.zeros(partial.shape, jnp.float32)
        )
        held[plane] = partial[...]

        def plane_copy(step):
            return pltpu.make_async_remote_copy(
                src_ref=partial,
                dst_ref=held.at[plane],
                send_sem=zh_send_sems.at[step],
                recv_sem=zh_recv_sems.at[step],
                device_id=plane_peer(step),
                device_id_type=mesh_id,
            )

        @pl.loop(1, planes)
        def _(step):
            plane_copy(step).start()

        @pl.loop(1, planes)
        def _(step):
            plane_copy(step).wait()

        total = held[0]
        for source in range(1, planes):
            total = total + held[source]
        final[...] = total
        copy = final_copy()
        copy.start()
        copy.wait_send()

    @pl.when(jnp.logical_not(receiver))
    def _():
        final_copy().wait_recv()

    @pl.loop(0, half)
    def _(index):
        @pl.when(mine_start + index != tile)
        def _():
            sum_copy(index).wait_send()

    back_own.wait()

    @pl.loop(1, tile_count)
    def _(step):
        back_copy(step).wait()

    returned_ref[...] = returned_held[...]
    out_ref[...] = final[...]


def paired_sum(row_blocks, spread):
    rep_count = lax.axis_size("rep")
    col_tiles = lax.axis_size("tx")
    tile_count = row_blocks.shape[0]
    block_shape = row_blocks.shape[1:]
    half_shape = (tile_count // 2,) + block_shape
    return pl.pallas_call(
        functools.partial(paired_sum_kernel, rep_count, tile_count, col_tiles),
        out_shape=[
            jax.ShapeDtypeStruct(block_shape, jnp.float32),
            jax.ShapeDtypeStruct(spread.shape, spread.dtype),
        ],
        in_specs=[pl.BlockSpec(memory_space=pltpu.VMEM)] * 2,
        out_specs=[pl.BlockSpec(memory_space=pltpu.VMEM)] * 2,
        scratch_shapes=[
            pltpu.VMEM(half_shape, row_blocks.dtype),
            pltpu.VMEM(half_shape, row_blocks.dtype),
            pltpu.VMEM(row_blocks.shape, row_blocks.dtype),
            pltpu.VMEM(block_shape, jnp.float32),
            pltpu.VMEM((rep_count // 2,) + block_shape, jnp.float32),
            pltpu.VMEM(block_shape, jnp.float32),
            pltpu.VMEM(spread.shape, spread.dtype),
            pltpu.SemaphoreType.DMA((2,)),
            pltpu.SemaphoreType.DMA((tile_count,)),
            pltpu.SemaphoreType.DMA((tile_count,)),
            pltpu.SemaphoreType.DMA((rep_count // 2,)),
            pltpu.SemaphoreType.DMA((rep_count // 2,)),
            pltpu.SemaphoreType.DMA((2,)),
            pltpu.SemaphoreType.DMA((tile_count,)),
            pltpu.SemaphoreType.DMA((tile_count,)),
            pltpu.SemaphoreType.DMA((2,)),
        ],
        compiler_params=pltpu.CompilerParams(collective_id=2, has_side_effects=True),
    )(row_blocks, spread)


def exchange_kernel(tile_count, col_tiles, tokens_ref, cot_ref, tokens_out, cot_out,
                    tokens_held, cot_held, send_sems, recv_sems, own_sems):
    me = lax.axis_index("rep")
    row = lax.axis_index("ty")
    col = lax.axis_index("tx")
    tile = row * col_tiles + col
    barrier = pltpu.get_barrier_semaphore()

    def tile_peer(step):
        peer = lax.rem(tile + step, tile_count)
        return (me, peer // col_tiles, lax.rem(peer, col_tiles))

    @pl.loop(1, tile_count)
    def _(step):
        pl.semaphore_signal(barrier, inc=1, device_id=tile_peer(step),
                            device_id_type=pl.DeviceIdType.MESH)

    pl.semaphore_wait(barrier, tile_count - 1)

    def tile_copies(step):
        peer = lax.rem(tile + step, tile_count)
        return [
            pltpu.make_async_remote_copy(
                src_ref=source.at[0, peer],
                dst_ref=held.at[tile],
                send_sem=send_sems.at[step, index],
                recv_sem=recv_sems.at[step, index],
                device_id=tile_peer(step),
                device_id_type=pl.DeviceIdType.MESH,
            )
            for index, (source, held) in enumerate(((tokens_ref, tokens_held), (cot_ref, cot_held)))
        ]

    own = [
        pltpu.make_async_copy(tokens_ref.at[0, tile], tokens_held.at[tile], own_sems.at[0]),
        pltpu.make_async_copy(cot_ref.at[0, tile], cot_held.at[tile], own_sems.at[1]),
    ]
    for copy in own:
        copy.start()

    @pl.loop(1, tile_count)
    def _(step):
        for copy in tile_copies(step):
            copy.start()

    for copy in own:
        copy.wait()

    @pl.loop(1, tile_count)
    def _(step):
        for copy in tile_copies(step):
            copy.wait()

    tokens_out[...] = tokens_held[...]
    cot_out[...] = cot_held[...]


def exchange(tokens, cotangent):
    col_tiles = lax.axis_size("tx")
    tile_count = lax.axis_size("ty") * col_tiles
    held_shape = (tile_count,) + tokens.shape[2:]
    return pl.pallas_call(
        functools.partial(exchange_kernel, tile_count, col_tiles),
        out_shape=[jax.ShapeDtypeStruct(held_shape, tokens.dtype)] * 2,
        in_specs=[pl.BlockSpec(memory_space=pltpu.VMEM)] * 2,
        out_specs=[pl.BlockSpec(memory_space=pltpu.VMEM)] * 2,
        scratch_shapes=[
            pltpu.VMEM(held_shape, tokens.dtype),
            pltpu.VMEM(held_shape, tokens.dtype),
            pltpu.SemaphoreType.DMA((tile_count, 2)),
            pltpu.SemaphoreType.DMA((tile_count, 2)),
            pltpu.SemaphoreType.DMA((2,)),
        ],
        compiler_params=pltpu.CompilerParams(collective_id=1, has_side_effects=True),
    )(tokens, cotangent)


def shards(tokens, qkv_weight, cotangent):
    rep_count = lax.axis_size("rep")
    row_tiles = lax.axis_size("ty")
    col_tiles = lax.axis_size("tx")
    tile_count = row_tiles * col_tiles
    tile_height = tokens.shape[1]
    tile_width = tokens.shape[2]
    channels = tokens.shape[3]
    stride_rows = row_tiles * tile_height // GRID
    stride_cols = col_tiles * tile_width // GRID
    block_rows = min(tile_height, stride_rows)
    fold_rows = stride_rows // block_rows
    col_groups = tile_width // stride_cols
    outer_rows = tile_height // block_rows
    inner_rows = block_rows // tile_count
    split_shape = (outer_rows, tile_count, inner_rows, tile_width, channels)
    if tile_height == tile_count and outer_rows == 1 and inner_rows == 1:
        grid_x, grid_g = (
            values.reshape(split_shape) for values in exchange(tokens, cotangent)
        )
    else:
        grid_x, grid_g = (
            lax.all_to_all(
                values.reshape(split_shape), ("ty", "tx"), split_axis=1, concat_axis=1, tiled=True
            )
            for values in (tokens, cotangent)
        )
    token_shape = (
        outer_rows,
        row_tiles // fold_rows,
        fold_rows,
        col_tiles,
        inner_rows,
        col_groups,
        stride_cols,
        channels,
    )
    win_count = fold_rows * inner_rows * stride_cols

    def to_windows(values):
        return (
            values.reshape(token_shape)
            .transpose(2, 4, 6, 1, 0, 3, 5, 7)
            .reshape(win_count, GRID * GRID, channels)
        )

    grad_windows, weight_term = window_grads(to_windows(grid_x), to_windows(grid_g), qkv_weight)
    back_shape = (
        fold_rows,
        inner_rows,
        stride_cols,
        row_tiles // fold_rows,
        outer_rows,
        col_tiles,
        col_groups,
        channels,
    )
    spread = grad_windows.reshape(back_shape).transpose(4, 3, 0, 5, 1, 6, 2, 7).reshape(split_shape)
    row_blocks = weight_term.reshape(tile_count, channels // tile_count, weight_term.shape[1])
    if tile_height == tile_count and outer_rows == 1 and inner_rows == 1:
        weight_grad, returned = paired_sum(
            row_blocks.astype(jnp.bfloat16), spread.reshape((tile_count,) + tokens.shape[2:])
        )
    else:
        returned = lax.all_to_all(spread, ("ty", "tx"), split_axis=1, concat_axis=1, tiled=True)
        gathered = lax.all_to_all(row_blocks.astype(jnp.bfloat16), ("ty", "tx"), 0, 0, tiled=True)
        weight_grad = lax.psum(jnp.sum(gathered.astype(jnp.float32), axis=0), "rep")
    token_grad = returned.reshape(1, tile_height, tile_width, channels)
    weight_grad = weight_grad / (rep_count * tile_count)
    return (token_grad, weight_grad)


def solution(mesh):
    placed = (P("rep", "ty", "tx", None), P(), P("rep", "ty", "tx", None))
    return jax.shard_map(
        shards,
        mesh=mesh,
        in_specs=placed,
        out_specs=(P("rep", "ty", "tx", None), P(("ty", "tx"), None)),
        check_vma=False,
    )
```

```python
import functools

import jax
import jax.numpy as jnp
from jax import lax
from jax.experimental import pallas as pl
from jax.experimental.pallas import tpu as pltpu
from jax.sharding import PartitionSpec as P

HEADS = 16
HEAD_DIM = 32
GRID = 8


eps_norm = 1e-05


def normalize(values):
    center = values - jnp.mean(values, axis=-1, keepdims=True)
    inv_std = lax.rsqrt(jnp.mean(center * center, axis=-1, keepdims=True) + eps_norm)
    return (center * inv_std, inv_std)


def window_grads(window_x, window_g, qkv_weight):
    win_count, win_tokens, channels = window_x.shape
    standard, inv_std = normalize(window_x.astype(jnp.float32))
    normed = standard.astype(jnp.bfloat16).reshape(win_count * win_tokens, channels)
    projection = jnp.dot(normed, qkv_weight, preferred_element_type=jnp.float32)
    flat_shape = (win_count, win_tokens, channels)
    query = (projection[:, :channels] * HEAD_DIM ** (-0.5)).astype(jnp.bfloat16).reshape(flat_shape)
    key = projection[:, channels : 2 * channels].astype(jnp.bfloat16).reshape(flat_shape)
    value = projection[:, 2 * channels :].astype(jnp.bfloat16).reshape(flat_shape)
    grad = window_g.astype(jnp.bfloat16)
    head_mask = (
        lax.broadcasted_iota(jnp.int32, (HEADS, channels), 1) // HEAD_DIM
        == lax.broadcasted_iota(jnp.int32, (HEADS, channels), 0)
    ).astype(jnp.bfloat16)

    def spread(values):
        return values[:, None, :, :] * head_mask[None, :, None, :]

    query_spread = spread(query)
    grad_spread = spread(grad)
    scores = jnp.einsum("wnqc,wkc->wnqk", query_spread, key, preferred_element_type=jnp.float32)
    peak_score = jnp.max(scores, axis=-1, keepdims=True)
    exponent = jnp.exp(scores - peak_score)
    attn_probs = exponent / jnp.sum(exponent, axis=-1, keepdims=True)
    probs_low = attn_probs.astype(jnp.bfloat16)
    attn_grad = jnp.einsum("wnqc,wkc->wnqk", grad_spread, value, preferred_element_type=jnp.float32)
    value_grad = jnp.einsum(
        "wnqk,wnqc->wkc", probs_low, grad_spread, preferred_element_type=jnp.float32
    ).astype(jnp.bfloat16)
    score_grad = (
        attn_probs * (attn_grad - jnp.sum(attn_probs * attn_grad, axis=-1, keepdims=True))
    ).astype(jnp.bfloat16)
    key_grad = jnp.einsum(
        "wnqk,wnqc->wkc", score_grad, query_spread, preferred_element_type=jnp.float32
    ).astype(jnp.bfloat16)
    query_full = jnp.einsum("wnqk,wkc->wnqc", score_grad, key, preferred_element_type=jnp.float32)
    query_grad = (
        jnp.sum(query_full * head_mask[None, :, None, :].astype(jnp.float32), axis=1)
        * HEAD_DIM ** (-0.5)
    ).astype(jnp.bfloat16)
    flat_shape = (win_count * win_tokens, channels)
    proj_grad = jnp.concatenate(
        [
            query_grad.reshape(flat_shape),
            key_grad.reshape(flat_shape),
            value_grad.reshape(flat_shape),
        ],
        axis=1,
    )
    normed_grad = lax.dot_general(
        proj_grad, qkv_weight, (((1,), (1,)), ((), ())), preferred_element_type=jnp.float32
    )
    normed_grad = normed_grad.reshape(win_count, win_tokens, channels)
    weight_term = lax.dot_general(
        normed, proj_grad, (((0,), (0,)), ((), ())), preferred_element_type=jnp.float32
    )
    inner_term = (
        normed_grad
        - jnp.mean(normed_grad, axis=-1, keepdims=True)
        - standard * jnp.mean(normed_grad * standard, axis=-1, keepdims=True)
    )
    token_grad = (window_g.astype(jnp.float32) + inv_std * inner_term).astype(jnp.bfloat16)
    return (token_grad, weight_term)


def weight_sum_kernel(rep_count, tile_count, col_tiles, blocks_ref, spread_ref, out_ref,
                      returned_ref, arrived, partial, held, returned_held, send_sems, recv_sems,
                      rep_send_sems, rep_recv_sems, back_send_sems, back_recv_sems, back_own_sem):
    me = lax.axis_index("rep")
    row = lax.axis_index("ty")
    col = lax.axis_index("tx")
    tile = row * col_tiles + col
    barrier = pltpu.get_barrier_semaphore()

    def tile_peer(step):
        peer = lax.rem(tile + step, tile_count)
        return (me, peer // col_tiles, lax.rem(peer, col_tiles))

    def rep_peer(step):
        return (lax.rem(me + step, rep_count), row, col)

    @pl.loop(1, tile_count)
    def _(step):
        pl.semaphore_signal(barrier, inc=1, device_id=tile_peer(step),
                            device_id_type=pl.DeviceIdType.MESH)

    @pl.loop(1, rep_count)
    def _(step):
        pl.semaphore_signal(barrier, inc=1, device_id=rep_peer(step),
                            device_id_type=pl.DeviceIdType.MESH)

    pl.semaphore_wait(barrier, tile_count + rep_count - 2)

    def back_copy(step):
        peer = lax.rem(tile + step, tile_count)
        return pltpu.make_async_remote_copy(
            src_ref=spread_ref.at[peer],
            dst_ref=returned_held.at[tile],
            send_sem=back_send_sems.at[step],
            recv_sem=back_recv_sems.at[step],
            device_id=tile_peer(step),
            device_id_type=pl.DeviceIdType.MESH,
        )

    back_own = pltpu.make_async_copy(spread_ref.at[tile], returned_held.at[tile], back_own_sem.at[0])
    back_own.start()

    @pl.loop(1, tile_count)
    def _(step):
        back_copy(step).start()

    def tile_copy(step):
        peer = lax.rem(tile + step, tile_count)
        return pltpu.make_async_remote_copy(
            src_ref=blocks_ref.at[peer],
            dst_ref=arrived.at[tile],
            send_sem=send_sems.at[step],
            recv_sem=recv_sems.at[step],
            device_id=tile_peer(step),
            device_id_type=pl.DeviceIdType.MESH,
        )

    own = pltpu.make_async_copy(blocks_ref.at[tile], arrived.at[tile], send_sems.at[0])
    own.start()

    @pl.loop(1, tile_count)
    def _(step):
        tile_copy(step).start()

    own.wait()

    @pl.loop(1, tile_count)
    def _(step):
        tile_copy(step).wait()

    def add_source(source, total):
        return total + arrived[source].astype(jnp.float32)

    partial[...] = lax.fori_loop(
        0, tile_count, add_source, jnp.zeros(partial.shape, jnp.float32)
    )
    held[me] = partial[...]

    def rep_copy(step):
        return pltpu.make_async_remote_copy(
            src_ref=partial,
            dst_ref=held.at[me],
            send_sem=rep_send_sems.at[step],
            recv_sem=rep_recv_sems.at[step],
            device_id=rep_peer(step),
            device_id_type=pl.DeviceIdType.MESH,
        )

    @pl.loop(1, rep_count)
    def _(step):
        rep_copy(step).start()

    @pl.loop(1, rep_count)
    def _(step):
        rep_copy(step).wait()

    back_own.wait()

    @pl.loop(1, tile_count)
    def _(step):
        back_copy(step).wait()

    returned_ref[...] = returned_held[...]
    total = held[0]
    for source in range(1, rep_count):
        total = total + held[source]
    out_ref[...] = total


def weight_sum(row_blocks, spread):
    rep_count = lax.axis_size("rep")
    col_tiles = lax.axis_size("tx")
    tile_count = row_blocks.shape[0]
    block_shape = row_blocks.shape[1:]
    return pl.pallas_call(
        functools.partial(weight_sum_kernel, rep_count, tile_count, col_tiles),
        out_shape=[
            jax.ShapeDtypeStruct(block_shape, jnp.float32),
            jax.ShapeDtypeStruct(spread.shape, spread.dtype),
        ],
        in_specs=[pl.BlockSpec(memory_space=pltpu.VMEM)] * 2,
        out_specs=[pl.BlockSpec(memory_space=pltpu.VMEM)] * 2,
        scratch_shapes=[
            pltpu.VMEM(row_blocks.shape, row_blocks.dtype),
            pltpu.VMEM(block_shape, jnp.float32),
            pltpu.VMEM((rep_count,) + block_shape, jnp.float32),
            pltpu.VMEM(spread.shape, spread.dtype),
            pltpu.SemaphoreType.DMA((tile_count,)),
            pltpu.SemaphoreType.DMA((tile_count,)),
            pltpu.SemaphoreType.DMA((rep_count,)),
            pltpu.SemaphoreType.DMA((rep_count,)),
            pltpu.SemaphoreType.DMA((tile_count,)),
            pltpu.SemaphoreType.DMA((tile_count,)),
            pltpu.SemaphoreType.DMA((1,)),
        ],
        compiler_params=pltpu.CompilerParams(collective_id=0, has_side_effects=True),
    )(row_blocks, spread)


def paired_sum_kernel(rep_count, tile_count, col_tiles, blocks_ref, spread_ref, out_ref,
                      returned_ref, pair_held, pair_sum, arrived, partial, held, final,
                      returned_held, pair_sems, tile_send_sems, tile_recv_sems, zh_send_sems,
                      zh_recv_sems, final_sems, back_send_sems, back_recv_sems, own_sems):
    me = lax.axis_index("rep")
    row = lax.axis_index("ty")
    col = lax.axis_index("tx")
    tile = row * col_tiles + col
    core = lax.rem(me, 2)
    plane = me // 2
    planes = rep_count // 2
    partner = me + 1 - 2 * core
    half = tile_count // 2
    mine_start = core * half
    receiver = tile // half == core
    barrier = pltpu.get_barrier_semaphore()

    def tile_device(peer):
        return (me, peer // col_tiles, lax.rem(peer, col_tiles))

    def tile_peer(step):
        return tile_device(lax.rem(tile + step, tile_count))

    def plane_peer(step):
        return (2 * lax.rem(plane + step, planes) + core, row, col)

    mesh_id = pl.DeviceIdType.MESH
    pl.semaphore_signal(barrier, inc=1, device_id=(partner, row, col), device_id_type=mesh_id)

    @pl.loop(1, tile_count)
    def _(step):
        pl.semaphore_signal(barrier, inc=1, device_id=tile_peer(step), device_id_type=mesh_id)

    @pl.when(receiver)
    def _():
        @pl.loop(1, planes)
        def _(step):
            pl.semaphore_signal(barrier, inc=1, device_id=plane_peer(step), device_id_type=mesh_id)

    pl.semaphore_wait(barrier, tile_count + (planes - 1) * receiver.astype(jnp.int32))

    pair_copy = pltpu.make_async_remote_copy(
        src_ref=blocks_ref.at[pl.ds((1 - core) * half, half)],
        dst_ref=pair_held,
        send_sem=pair_sems.at[0],
        recv_sem=pair_sems.at[1],
        device_id=(partner, row, col),
        device_id_type=mesh_id,
    )
    pair_copy.start()

    def back_copy(step):
        peer = lax.rem(tile + step, tile_count)
        return pltpu.make_async_remote_copy(
            src_ref=spread_ref.at[peer],
            dst_ref=returned_held.at[tile],
            send_sem=back_send_sems.at[step],
            recv_sem=back_recv_sems.at[step],
            device_id=tile_peer(step),
            device_id_type=mesh_id,
        )

    back_own = pltpu.make_async_copy(spread_ref.at[tile], returned_held.at[tile], own_sems.at[0])
    back_own.start()

    @pl.loop(1, tile_count)
    def _(step):
        back_copy(step).start()

    pair_copy.wait()

    @pl.loop(0, half)
    def _(index):
        pair_sum[index] = (
            blocks_ref[mine_start + index].astype(jnp.float32)
            + pair_held[index].astype(jnp.float32)
        ).astype(pair_sum.dtype)

    def sum_copy(index):
        target = mine_start + index
        step = lax.rem(target - tile + tile_count, tile_count)
        return pltpu.make_async_remote_copy(
            src_ref=pair_sum.at[index],
            dst_ref=arrived.at[tile],
            send_sem=tile_send_sems.at[step],
            recv_sem=tile_recv_sems.at[step],
            device_id=tile_device(target),
            device_id_type=mesh_id,
        )

    @pl.loop(0, half)
    def _(index):
        @pl.when(mine_start + index != tile)
        def _():
            sum_copy(index).start()

    def final_copy():
        return pltpu.make_async_remote_copy(
            src_ref=final,
            dst_ref=final,
            send_sem=final_sems.at[0],
            recv_sem=final_sems.at[1],
            device_id=(partner, row, col),
            device_id_type=mesh_id,
        )

    @pl.when(receiver)
    def _():
        own = pltpu.make_async_copy(
            pair_sum.at[tile - mine_start], arrived.at[tile], own_sems.at[1]
        )
        own.start()
        own.wait()

        @pl.loop(1, tile_count)
        def _(step):
            pltpu.make_async_remote_copy(
                src_ref=pair_sum.at[0],
                dst_ref=arrived.at[tile],
                send_sem=tile_send_sems.at[step],
                recv_sem=tile_recv_sems.at[step],
                device_id=tile_peer(step),
                device_id_type=mesh_id,
            ).wait_recv()

        def add_source(source, total):
            return total + arrived[source].astype(jnp.float32)

        partial[...] = lax.fori_loop(
            0, tile_count, add_source, jnp.zeros(partial.shape, jnp.float32)
        )
        held[plane] = partial[...]

        def plane_copy(step):
            return pltpu.make_async_remote_copy(
                src_ref=partial,
                dst_ref=held.at[plane],
                send_sem=zh_send_sems.at[step],
                recv_sem=zh_recv_sems.at[step],
                device_id=plane_peer(step),
                device_id_type=mesh_id,
            )

        @pl.loop(1, planes)
        def _(step):
            plane_copy(step).start()

        @pl.loop(1, planes)
        def _(step):
            plane_copy(step).wait()

        total = held[0]
        for source in range(1, planes):
            total = total + held[source]
        final[...] = total
        copy = final_copy()
        copy.start()
        copy.wait_send()

    @pl.when(jnp.logical_not(receiver))
    def _():
        final_copy().wait_recv()

    @pl.loop(0, half)
    def _(index):
        @pl.when(mine_start + index != tile)
        def _():
            sum_copy(index).wait_send()

    back_own.wait()

    @pl.loop(1, tile_count)
    def _(step):
        back_copy(step).wait()

    returned_ref[...] = returned_held[...]
    out_ref[...] = final[...]


def paired_sum(row_blocks, spread):
    rep_count = lax.axis_size("rep")
    col_tiles = lax.axis_size("tx")
    tile_count = row_blocks.shape[0]
    block_shape = row_blocks.shape[1:]
    half_shape = (tile_count // 2,) + block_shape
    return pl.pallas_call(
        functools.partial(paired_sum_kernel, rep_count, tile_count, col_tiles),
        out_shape=[
            jax.ShapeDtypeStruct(block_shape, jnp.float32),
            jax.ShapeDtypeStruct(spread.shape, spread.dtype),
        ],
        in_specs=[pl.BlockSpec(memory_space=pltpu.VMEM)] * 2,
        out_specs=[pl.BlockSpec(memory_space=pltpu.VMEM)] * 2,
        scratch_shapes=[
            pltpu.VMEM(half_shape, row_blocks.dtype),
            pltpu.VMEM(half_shape, row_blocks.dtype),
            pltpu.VMEM(row_blocks.shape, row_blocks.dtype),
            pltpu.VMEM(block_shape, jnp.float32),
            pltpu.VMEM((rep_count // 2,) + block_shape, jnp.float32),
            pltpu.VMEM(block_shape, jnp.float32),
            pltpu.VMEM(spread.shape, spread.dtype),
            pltpu.SemaphoreType.DMA((2,)),
            pltpu.SemaphoreType.DMA((tile_count,)),
            pltpu.SemaphoreType.DMA((tile_count,)),
            pltpu.SemaphoreType.DMA((rep_count // 2,)),
            pltpu.SemaphoreType.DMA((rep_count // 2,)),
            pltpu.SemaphoreType.DMA((2,)),
            pltpu.SemaphoreType.DMA((tile_count,)),
            pltpu.SemaphoreType.DMA((tile_count,)),
            pltpu.SemaphoreType.DMA((2,)),
        ],
        compiler_params=pltpu.CompilerParams(collective_id=2, has_side_effects=True),
    )(row_blocks, spread)


def balanced_sum_kernel(rep_count, tile_count, col_tiles, blocks_ref, spread_ref, out_ref,
                        returned_ref, pair_held, pair_sum, arrived, partial, pair_part,
                        pair_total, held, returned_held, pair_sems, sum_send_sems, sum_recv_sems,
                        part_sems, rep_send_sems, rep_recv_sems, back_send_sems, back_recv_sems,
                        own_sems):
    me = lax.axis_index("rep")
    row = lax.axis_index("ty")
    col = lax.axis_index("tx")
    tile = row * col_tiles + col
    core = lax.rem(me, 2)
    plane = me // 2
    planes = rep_count // 2
    partner = me + 1 - 2 * core
    target_rep = me - core + lax.rem(tile, 2)
    half = tile_count // 2
    mine_start = core * half
    barrier = pltpu.get_barrier_semaphore()
    mesh_id = pl.DeviceIdType.MESH

    def tile_device(rep, peer):
        return (rep, peer // col_tiles, lax.rem(peer, col_tiles))

    def tile_peer(step):
        return tile_device(me, lax.rem(tile + step, tile_count))

    def plane_peer(step):
        return (2 * lax.rem(plane + step, planes) + core, row, col)

    @pl.loop(1, tile_count)
    def _(step):
        pl.semaphore_signal(barrier, inc=1, device_id=tile_peer(step), device_id_type=mesh_id)

    @pl.loop(0, tile_count)
    def _(peer):
        pl.semaphore_signal(
            barrier, inc=1, device_id=tile_device(partner, peer), device_id_type=mesh_id
        )

    @pl.loop(1, planes)
    def _(step):
        pl.semaphore_signal(barrier, inc=1, device_id=plane_peer(step), device_id_type=mesh_id)

    pl.semaphore_wait(barrier, 2 * tile_count + planes - 2)

    pair_copy = pltpu.make_async_remote_copy(
        src_ref=blocks_ref.at[pl.ds((1 - core) * half, half)],
        dst_ref=pair_held,
        send_sem=pair_sems.at[0],
        recv_sem=pair_sems.at[1],
        device_id=(partner, row, col),
        device_id_type=mesh_id,
    )
    pair_copy.start()

    def back_copy(step):
        peer = lax.rem(tile + step, tile_count)
        return pltpu.make_async_remote_copy(
            src_ref=spread_ref.at[peer],
            dst_ref=returned_held.at[tile],
            send_sem=back_send_sems.at[step],
            recv_sem=back_recv_sems.at[step],
            device_id=tile_peer(step),
            device_id_type=mesh_id,
        )

    back_own = pltpu.make_async_copy(spread_ref.at[tile], returned_held.at[tile], own_sems.at[0])
    back_own.start()

    @pl.loop(1, tile_count)
    def _(step):
        back_copy(step).start()

    pair_copy.wait()

    @pl.loop(0, half)
    def _(index):
        pair_sum[index] = (
            blocks_ref[mine_start + index].astype(jnp.float32)
            + pair_held[index].astype(jnp.float32)
        ).astype(pair_sum.dtype)

    def is_self(target):
        return jnp.logical_and(target_rep == me, target == tile)

    def sum_copy(index):
        target = mine_start + index
        return pltpu.make_async_remote_copy(
            src_ref=pair_sum.at[index],
            dst_ref=arrived.at[tile],
            send_sem=sum_send_sems.at[index],
            recv_sem=sum_recv_sems.at[tile],
            device_id=tile_device(target_rep, target),
            device_id_type=mesh_id,
        )

    @pl.loop(0, half)
    def _(index):
        target = mine_start + index

        @pl.when(is_self(target))
        def _():
            own = pltpu.make_async_copy(pair_sum.at[index], arrived.at[tile], own_sems.at[1])
            own.start()
            own.wait()

        @pl.when(jnp.logical_not(is_self(target)))
        def _():
            sum_copy(index).start()

    @pl.loop(0, half)
    def _(index):
        source = core + 2 * index
        from_self = jnp.logical_and(source == tile, tile // half == core)

        @pl.when(jnp.logical_not(from_self))
        def _():
            pltpu.make_async_remote_copy(
                src_ref=pair_sum.at[0],
                dst_ref=arrived.at[source],
                send_sem=sum_send_sems.at[0],
                recv_sem=sum_recv_sems.at[source],
                device_id=tile_peer(1),
                device_id_type=mesh_id,
            ).wait_recv()

    def add_source(index, total):
        return total + arrived[core + 2 * index].astype(jnp.float32)

    partial[...] = lax.fori_loop(0, half, add_source, jnp.zeros(partial.shape, jnp.float32))
    pair_part[core] = partial[...]
    part_copy = pltpu.make_async_remote_copy(
        src_ref=partial,
        dst_ref=pair_part.at[core],
        send_sem=part_sems.at[0],
        recv_sem=part_sems.at[1],
        device_id=(partner, row, col),
        device_id_type=mesh_id,
    )
    part_copy.start()
    part_copy.wait()
    pair_total[...] = pair_part[0] + pair_part[1]
    held[plane] = pair_total[...]

    def plane_copy(step):
        return pltpu.make_async_remote_copy(
            src_ref=pair_total,
            dst_ref=held.at[plane],
            send_sem=rep_send_sems.at[step],
            recv_sem=rep_recv_sems.at[step],
            device_id=plane_peer(step),
            device_id_type=mesh_id,
        )

    @pl.loop(1, planes)
    def _(step):
        plane_copy(step).start()

    @pl.loop(1, planes)
    def _(step):
        plane_copy(step).wait()

    @pl.loop(0, half)
    def _(index):
        @pl.when(jnp.logical_not(is_self(mine_start + index)))
        def _():
            sum_copy(index).wait_send()

    back_own.wait()

    @pl.loop(1, tile_count)
    def _(step):
        back_copy(step).wait()

    returned_ref[...] = returned_held[...]
    total = held[0]
    for source in range(1, planes):
        total = total + held[source]
    out_ref[...] = total


def balanced_sum(row_blocks, spread):
    rep_count = lax.axis_size("rep")
    col_tiles = lax.axis_size("tx")
    tile_count = row_blocks.shape[0]
    block_shape = row_blocks.shape[1:]
    half_shape = (tile_count // 2,) + block_shape
    return pl.pallas_call(
        functools.partial(balanced_sum_kernel, rep_count, tile_count, col_tiles),
        out_shape=[
            jax.ShapeDtypeStruct(block_shape, jnp.float32),
            jax.ShapeDtypeStruct(spread.shape, spread.dtype),
        ],
        in_specs=[pl.BlockSpec(memory_space=pltpu.VMEM)] * 2,
        out_specs=[pl.BlockSpec(memory_space=pltpu.VMEM)] * 2,
        scratch_shapes=[
            pltpu.VMEM(half_shape, row_blocks.dtype),
            pltpu.VMEM(half_shape, row_blocks.dtype),
            pltpu.VMEM(row_blocks.shape, row_blocks.dtype),
            pltpu.VMEM(block_shape, jnp.float32),
            pltpu.VMEM((2,) + block_shape, jnp.float32),
            pltpu.VMEM(block_shape, jnp.float32),
            pltpu.VMEM((rep_count // 2,) + block_shape, jnp.float32),
            pltpu.VMEM(spread.shape, spread.dtype),
            pltpu.SemaphoreType.DMA((2,)),
            pltpu.SemaphoreType.DMA((tile_count // 2,)),
            pltpu.SemaphoreType.DMA((tile_count,)),
            pltpu.SemaphoreType.DMA((2,)),
            pltpu.SemaphoreType.DMA((rep_count // 2,)),
            pltpu.SemaphoreType.DMA((rep_count // 2,)),
            pltpu.SemaphoreType.DMA((tile_count,)),
            pltpu.SemaphoreType.DMA((tile_count,)),
            pltpu.SemaphoreType.DMA((2,)),
        ],
        compiler_params=pltpu.CompilerParams(collective_id=3, has_side_effects=True),
    )(row_blocks, spread)


def exchange_kernel(tile_count, col_tiles, tokens_ref, cot_ref, tokens_out, cot_out,
                    tokens_held, cot_held, send_sems, recv_sems, own_sems):
    me = lax.axis_index("rep")
    row = lax.axis_index("ty")
    col = lax.axis_index("tx")
    tile = row * col_tiles + col
    barrier = pltpu.get_barrier_semaphore()

    def tile_peer(step):
        peer = lax.rem(tile + step, tile_count)
        return (me, peer // col_tiles, lax.rem(peer, col_tiles))

    @pl.loop(1, tile_count)
    def _(step):
        pl.semaphore_signal(barrier, inc=1, device_id=tile_peer(step),
                            device_id_type=pl.DeviceIdType.MESH)

    pl.semaphore_wait(barrier, tile_count - 1)

    def tile_copies(step):
        peer = lax.rem(tile + step, tile_count)
        return [
            pltpu.make_async_remote_copy(
                src_ref=source.at[0, peer],
                dst_ref=held.at[tile],
                send_sem=send_sems.at[step, index],
                recv_sem=recv_sems.at[step, index],
                device_id=tile_peer(step),
                device_id_type=pl.DeviceIdType.MESH,
            )
            for index, (source, held) in enumerate(((tokens_ref, tokens_held), (cot_ref, cot_held)))
        ]

    own = [
        pltpu.make_async_copy(tokens_ref.at[0, tile], tokens_held.at[tile], own_sems.at[0]),
        pltpu.make_async_copy(cot_ref.at[0, tile], cot_held.at[tile], own_sems.at[1]),
    ]
    for copy in own:
        copy.start()

    @pl.loop(1, tile_count)
    def _(step):
        for copy in tile_copies(step):
            copy.start()

    for copy in own:
        copy.wait()

    @pl.loop(1, tile_count)
    def _(step):
        for copy in tile_copies(step):
            copy.wait()

    tokens_out[...] = tokens_held[...]
    cot_out[...] = cot_held[...]


def exchange(tokens, cotangent):
    col_tiles = lax.axis_size("tx")
    tile_count = lax.axis_size("ty") * col_tiles
    held_shape = (tile_count,) + tokens.shape[2:]
    return pl.pallas_call(
        functools.partial(exchange_kernel, tile_count, col_tiles),
        out_shape=[jax.ShapeDtypeStruct(held_shape, tokens.dtype)] * 2,
        in_specs=[pl.BlockSpec(memory_space=pltpu.VMEM)] * 2,
        out_specs=[pl.BlockSpec(memory_space=pltpu.VMEM)] * 2,
        scratch_shapes=[
            pltpu.VMEM(held_shape, tokens.dtype),
            pltpu.VMEM(held_shape, tokens.dtype),
            pltpu.SemaphoreType.DMA((tile_count, 2)),
            pltpu.SemaphoreType.DMA((tile_count, 2)),
            pltpu.SemaphoreType.DMA((2,)),
        ],
        compiler_params=pltpu.CompilerParams(collective_id=1, has_side_effects=True),
    )(tokens, cotangent)


def shards(tokens, qkv_weight, cotangent):
    rep_count = lax.axis_size("rep")
    row_tiles = lax.axis_size("ty")
    col_tiles = lax.axis_size("tx")
    tile_count = row_tiles * col_tiles
    tile_height = tokens.shape[1]
    tile_width = tokens.shape[2]
    channels = tokens.shape[3]
    stride_rows = row_tiles * tile_height // GRID
    stride_cols = col_tiles * tile_width // GRID
    block_rows = min(tile_height, stride_rows)
    fold_rows = stride_rows // block_rows
    col_groups = tile_width // stride_cols
    outer_rows = tile_height // block_rows
    inner_rows = block_rows // tile_count
    split_shape = (outer_rows, tile_count, inner_rows, tile_width, channels)
    if tile_height == tile_count and outer_rows == 1 and inner_rows == 1:
        grid_x, grid_g = (
            values.reshape(split_shape) for values in exchange(tokens, cotangent)
        )
    else:
        grid_x, grid_g = (
            lax.all_to_all(
                values.reshape(split_shape), ("ty", "tx"), split_axis=1, concat_axis=1, tiled=True
            )
            for values in (tokens, cotangent)
        )
    token_shape = (
        outer_rows,
        row_tiles // fold_rows,
        fold_rows,
        col_tiles,
        inner_rows,
        col_groups,
        stride_cols,
        channels,
    )
    win_count = fold_rows * inner_rows * stride_cols

    def to_windows(values):
        return (
            values.reshape(token_shape)
            .transpose(2, 4, 6, 1, 0, 3, 5, 7)
            .reshape(win_count, GRID * GRID, channels)
        )

    grad_windows, weight_term = window_grads(to_windows(grid_x), to_windows(grid_g), qkv_weight)
    back_shape = (
        fold_rows,
        inner_rows,
        stride_cols,
        row_tiles // fold_rows,
        outer_rows,
        col_tiles,
        col_groups,
        channels,
    )
    spread = grad_windows.reshape(back_shape).transpose(4, 3, 0, 5, 1, 6, 2, 7).reshape(split_shape)
    row_blocks = weight_term.reshape(tile_count, channels // tile_count, weight_term.shape[1])
    if tile_height == tile_count and outer_rows == 1 and inner_rows == 1:
        weight_grad, returned = balanced_sum(
            row_blocks.astype(jnp.bfloat16), spread.reshape((tile_count,) + tokens.shape[2:])
        )
    else:
        returned = lax.all_to_all(spread, ("ty", "tx"), split_axis=1, concat_axis=1, tiled=True)
        gathered = lax.all_to_all(row_blocks.astype(jnp.bfloat16), ("ty", "tx"), 0, 0, tiled=True)
        weight_grad = lax.psum(jnp.sum(gathered.astype(jnp.float32), axis=0), "rep")
    token_grad = returned.reshape(1, tile_height, tile_width, channels)
    weight_grad = weight_grad / (rep_count * tile_count)
    return (token_grad, weight_grad)


def solution(mesh):
    placed = (P("rep", "ty", "tx", None), P(), P("rep", "ty", "tx", None))
    return jax.shard_map(
        shards,
        mesh=mesh,
        in_specs=placed,
        out_specs=(P("rep", "ty", "tx", None), P(("ty", "tx"), None)),
        check_vma=False,
    )
```

```python
import functools

import jax
import jax.numpy as jnp
from jax import lax
from jax.experimental import pallas as pl
from jax.experimental.pallas import tpu as pltpu
from jax.sharding import PartitionSpec as P

HEADS = 16
HEAD_DIM = 32
GRID = 8


eps_norm = 1e-05


def normalize(values):
    center = values - jnp.mean(values, axis=-1, keepdims=True)
    inv_std = lax.rsqrt(jnp.mean(center * center, axis=-1, keepdims=True) + eps_norm)
    return (center * inv_std, inv_std)


def window_grads(window_x, window_g, qkv_weight):
    win_count, win_tokens, channels = window_x.shape
    standard, inv_std = normalize(window_x.astype(jnp.float32))
    normed = standard.astype(jnp.bfloat16).reshape(win_count * win_tokens, channels)
    projection = jnp.dot(normed, qkv_weight, preferred_element_type=jnp.float32)
    flat_shape = (win_count, win_tokens, channels)
    query = (projection[:, :channels] * HEAD_DIM ** (-0.5)).astype(jnp.bfloat16).reshape(flat_shape)
    key = projection[:, channels : 2 * channels].astype(jnp.bfloat16).reshape(flat_shape)
    value = projection[:, 2 * channels :].astype(jnp.bfloat16).reshape(flat_shape)
    grad = window_g.astype(jnp.bfloat16)
    head_mask = (
        lax.broadcasted_iota(jnp.int32, (HEADS, channels), 1) // HEAD_DIM
        == lax.broadcasted_iota(jnp.int32, (HEADS, channels), 0)
    ).astype(jnp.bfloat16)

    def spread(values):
        return values[:, None, :, :] * head_mask[None, :, None, :]

    query_spread = spread(query)
    grad_spread = spread(grad)
    scores = jnp.einsum("wnqc,wkc->wnqk", query_spread, key, preferred_element_type=jnp.float32)
    peak_score = jnp.max(scores, axis=-1, keepdims=True)
    exponent = jnp.exp(scores - peak_score)
    attn_probs = exponent / jnp.sum(exponent, axis=-1, keepdims=True)
    probs_low = attn_probs.astype(jnp.bfloat16)
    attn_grad = jnp.einsum("wnqc,wkc->wnqk", grad_spread, value, preferred_element_type=jnp.float32)
    value_grad = jnp.einsum(
        "wnqk,wnqc->wkc", probs_low, grad_spread, preferred_element_type=jnp.float32
    ).astype(jnp.bfloat16)
    score_grad = (
        attn_probs * (attn_grad - jnp.sum(attn_probs * attn_grad, axis=-1, keepdims=True))
    ).astype(jnp.bfloat16)
    key_grad = jnp.einsum(
        "wnqk,wnqc->wkc", score_grad, query_spread, preferred_element_type=jnp.float32
    ).astype(jnp.bfloat16)
    query_full = jnp.einsum("wnqk,wkc->wnqc", score_grad, key, preferred_element_type=jnp.float32)
    query_grad = (
        jnp.sum(query_full * head_mask[None, :, None, :].astype(jnp.float32), axis=1)
        * HEAD_DIM ** (-0.5)
    ).astype(jnp.bfloat16)
    flat_shape = (win_count * win_tokens, channels)
    proj_grad = jnp.concatenate(
        [
            query_grad.reshape(flat_shape),
            key_grad.reshape(flat_shape),
            value_grad.reshape(flat_shape),
        ],
        axis=1,
    )
    normed_grad = lax.dot_general(
        proj_grad, qkv_weight, (((1,), (1,)), ((), ())), preferred_element_type=jnp.float32
    )
    normed_grad = normed_grad.reshape(win_count, win_tokens, channels)
    weight_term = lax.dot_general(
        normed, proj_grad, (((0,), (0,)), ((), ())), preferred_element_type=jnp.float32
    )
    inner_term = (
        normed_grad
        - jnp.mean(normed_grad, axis=-1, keepdims=True)
        - standard * jnp.mean(normed_grad * standard, axis=-1, keepdims=True)
    )
    token_grad = (window_g.astype(jnp.float32) + inv_std * inner_term).astype(jnp.bfloat16)
    return (token_grad, weight_term)


def weight_sum_kernel(rep_count, tile_count, col_tiles, blocks_ref, spread_ref, out_ref,
                      returned_ref, arrived, partial, held, returned_held, send_sems, recv_sems,
                      rep_send_sems, rep_recv_sems, back_send_sems, back_recv_sems, back_own_sem):
    me = lax.axis_index("rep")
    row = lax.axis_index("ty")
    col = lax.axis_index("tx")
    tile = row * col_tiles + col
    barrier = pltpu.get_barrier_semaphore()

    def tile_peer(step):
        peer = lax.rem(tile + step, tile_count)
        return (me, peer // col_tiles, lax.rem(peer, col_tiles))

    def rep_peer(step):
        return (lax.rem(me + step, rep_count), row, col)

    @pl.loop(1, tile_count)
    def _(step):
        pl.semaphore_signal(barrier, inc=1, device_id=tile_peer(step),
                            device_id_type=pl.DeviceIdType.MESH)

    @pl.loop(1, rep_count)
    def _(step):
        pl.semaphore_signal(barrier, inc=1, device_id=rep_peer(step),
                            device_id_type=pl.DeviceIdType.MESH)

    pl.semaphore_wait(barrier, tile_count + rep_count - 2)

    def back_copy(step):
        peer = lax.rem(tile + step, tile_count)
        return pltpu.make_async_remote_copy(
            src_ref=spread_ref.at[peer],
            dst_ref=returned_held.at[tile],
            send_sem=back_send_sems.at[step],
            recv_sem=back_recv_sems.at[step],
            device_id=tile_peer(step),
            device_id_type=pl.DeviceIdType.MESH,
        )

    back_own = pltpu.make_async_copy(spread_ref.at[tile], returned_held.at[tile], back_own_sem.at[0])
    back_own.start()

    @pl.loop(1, tile_count)
    def _(step):
        back_copy(step).start()

    def tile_copy(step):
        peer = lax.rem(tile + step, tile_count)
        return pltpu.make_async_remote_copy(
            src_ref=blocks_ref.at[peer],
            dst_ref=arrived.at[tile],
            send_sem=send_sems.at[step],
            recv_sem=recv_sems.at[step],
            device_id=tile_peer(step),
            device_id_type=pl.DeviceIdType.MESH,
        )

    own = pltpu.make_async_copy(blocks_ref.at[tile], arrived.at[tile], send_sems.at[0])
    own.start()

    @pl.loop(1, tile_count)
    def _(step):
        tile_copy(step).start()

    own.wait()

    @pl.loop(1, tile_count)
    def _(step):
        tile_copy(step).wait()

    def add_source(source, total):
        return total + arrived[source].astype(jnp.float32)

    partial[...] = lax.fori_loop(
        0, tile_count, add_source, jnp.zeros(partial.shape, jnp.float32)
    )
    held[me] = partial[...]

    def rep_copy(step):
        return pltpu.make_async_remote_copy(
            src_ref=partial,
            dst_ref=held.at[me],
            send_sem=rep_send_sems.at[step],
            recv_sem=rep_recv_sems.at[step],
            device_id=rep_peer(step),
            device_id_type=pl.DeviceIdType.MESH,
        )

    @pl.loop(1, rep_count)
    def _(step):
        rep_copy(step).start()

    @pl.loop(1, rep_count)
    def _(step):
        rep_copy(step).wait()

    back_own.wait()

    @pl.loop(1, tile_count)
    def _(step):
        back_copy(step).wait()

    returned_ref[...] = returned_held[...]
    total = held[0]
    for source in range(1, rep_count):
        total = total + held[source]
    out_ref[...] = total


def weight_sum(row_blocks, spread):
    rep_count = lax.axis_size("rep")
    col_tiles = lax.axis_size("tx")
    tile_count = row_blocks.shape[0]
    block_shape = row_blocks.shape[1:]
    return pl.pallas_call(
        functools.partial(weight_sum_kernel, rep_count, tile_count, col_tiles),
        out_shape=[
            jax.ShapeDtypeStruct(block_shape, jnp.float32),
            jax.ShapeDtypeStruct(spread.shape, spread.dtype),
        ],
        in_specs=[pl.BlockSpec(memory_space=pltpu.VMEM)] * 2,
        out_specs=[pl.BlockSpec(memory_space=pltpu.VMEM)] * 2,
        scratch_shapes=[
            pltpu.VMEM(row_blocks.shape, row_blocks.dtype),
            pltpu.VMEM(block_shape, jnp.float32),
            pltpu.VMEM((rep_count,) + block_shape, jnp.float32),
            pltpu.VMEM(spread.shape, spread.dtype),
            pltpu.SemaphoreType.DMA((tile_count,)),
            pltpu.SemaphoreType.DMA((tile_count,)),
            pltpu.SemaphoreType.DMA((rep_count,)),
            pltpu.SemaphoreType.DMA((rep_count,)),
            pltpu.SemaphoreType.DMA((tile_count,)),
            pltpu.SemaphoreType.DMA((tile_count,)),
            pltpu.SemaphoreType.DMA((1,)),
        ],
        compiler_params=pltpu.CompilerParams(collective_id=0, has_side_effects=True),
    )(row_blocks, spread)


def paired_sum_kernel(rep_count, tile_count, col_tiles, blocks_ref, spread_ref, out_ref,
                      returned_ref, pair_held, pair_sum, arrived, partial, held, final,
                      returned_held, pair_sems, tile_send_sems, tile_recv_sems, zh_send_sems,
                      zh_recv_sems, final_sems, back_send_sems, back_recv_sems, own_sems):
    me = lax.axis_index("rep")
    row = lax.axis_index("ty")
    col = lax.axis_index("tx")
    tile = row * col_tiles + col
    core = lax.rem(me, 2)
    plane = me // 2
    planes = rep_count // 2
    partner = me + 1 - 2 * core
    half = tile_count // 2
    mine_start = core * half
    receiver = tile // half == core
    barrier = pltpu.get_barrier_semaphore()

    def tile_device(peer):
        return (me, peer // col_tiles, lax.rem(peer, col_tiles))

    def tile_peer(step):
        return tile_device(lax.rem(tile + step, tile_count))

    def plane_peer(step):
        return (2 * lax.rem(plane + step, planes) + core, row, col)

    mesh_id = pl.DeviceIdType.MESH
    pl.semaphore_signal(barrier, inc=1, device_id=(partner, row, col), device_id_type=mesh_id)

    @pl.loop(1, tile_count)
    def _(step):
        pl.semaphore_signal(barrier, inc=1, device_id=tile_peer(step), device_id_type=mesh_id)

    @pl.when(receiver)
    def _():
        @pl.loop(1, planes)
        def _(step):
            pl.semaphore_signal(barrier, inc=1, device_id=plane_peer(step), device_id_type=mesh_id)

    pl.semaphore_wait(barrier, tile_count + (planes - 1) * receiver.astype(jnp.int32))

    pair_copy = pltpu.make_async_remote_copy(
        src_ref=blocks_ref.at[pl.ds((1 - core) * half, half)],
        dst_ref=pair_held,
        send_sem=pair_sems.at[0],
        recv_sem=pair_sems.at[1],
        device_id=(partner, row, col),
        device_id_type=mesh_id,
    )
    pair_copy.start()

    def back_copy(step):
        peer = lax.rem(tile + step, tile_count)
        return pltpu.make_async_remote_copy(
            src_ref=spread_ref.at[peer],
            dst_ref=returned_held.at[tile],
            send_sem=back_send_sems.at[step],
            recv_sem=back_recv_sems.at[step],
            device_id=tile_peer(step),
            device_id_type=mesh_id,
        )

    back_own = pltpu.make_async_copy(spread_ref.at[tile], returned_held.at[tile], own_sems.at[0])
    back_own.start()

    @pl.loop(1, tile_count)
    def _(step):
        back_copy(step).start()

    pair_copy.wait()

    def sum_copy(index):
        target = mine_start + index
        step = lax.rem(target - tile + tile_count, tile_count)
        return pltpu.make_async_remote_copy(
            src_ref=pair_sum.at[index],
            dst_ref=arrived.at[tile],
            send_sem=tile_send_sems.at[step],
            recv_sem=tile_recv_sems.at[step],
            device_id=tile_device(target),
            device_id_type=mesh_id,
        )

    @pl.loop(0, half)
    def _(index):
        pair_sum[index] = (
            blocks_ref[mine_start + index].astype(jnp.float32)
            + pair_held[index].astype(jnp.float32)
        ).astype(pair_sum.dtype)

        @pl.when(mine_start + index != tile)
        def _():
            sum_copy(index).start()

    def final_copy():
        return pltpu.make_async_remote_copy(
            src_ref=final,
            dst_ref=final,
            send_sem=final_sems.at[0],
            recv_sem=final_sems.at[1],
            device_id=(partner, row, col),
            device_id_type=mesh_id,
        )

    @pl.when(receiver)
    def _():
        own = pltpu.make_async_copy(
            pair_sum.at[tile - mine_start], arrived.at[tile], own_sems.at[1]
        )
        own.start()
        own.wait()

        def add_arrival(step, total):
            pltpu.make_async_remote_copy(
                src_ref=pair_sum.at[0],
                dst_ref=arrived.at[tile],
                send_sem=tile_send_sems.at[step],
                recv_sem=tile_recv_sems.at[step],
                device_id=tile_peer(step),
                device_id_type=mesh_id,
            ).wait_recv()
            source = lax.rem(tile - step + tile_count, tile_count)
            return total + arrived[source].astype(jnp.float32)

        partial[...] = lax.fori_loop(
            1, tile_count, add_arrival, arrived[tile].astype(jnp.float32)
        )
        held[plane] = partial[...]

        def plane_copy(step):
            return pltpu.make_async_remote_copy(
                src_ref=partial,
                dst_ref=held.at[plane],
                send_sem=zh_send_sems.at[step],
                recv_sem=zh_recv_sems.at[step],
                device_id=plane_peer(step),
                device_id_type=mesh_id,
            )

        @pl.loop(1, planes)
        def _(step):
            plane_copy(step).start()

        @pl.loop(1, planes)
        def _(step):
            plane_copy(step).wait()

        total = held[0]
        for source in range(1, planes):
            total = total + held[source]
        final[...] = total
        copy = final_copy()
        copy.start()
        copy.wait_send()

    @pl.when(jnp.logical_not(receiver))
    def _():
        final_copy().wait_recv()

    @pl.loop(0, half)
    def _(index):
        @pl.when(mine_start + index != tile)
        def _():
            sum_copy(index).wait_send()

    back_own.wait()

    @pl.loop(1, tile_count)
    def _(step):
        back_copy(step).wait()

    returned_ref[...] = returned_held[...]
    out_ref[...] = final[...] * (1.0 / (rep_count * tile_count))


def paired_sum(row_blocks, spread):
    rep_count = lax.axis_size("rep")
    col_tiles = lax.axis_size("tx")
    tile_count = row_blocks.shape[0]
    block_shape = row_blocks.shape[1:]
    half_shape = (tile_count // 2,) + block_shape
    return pl.pallas_call(
        functools.partial(paired_sum_kernel, rep_count, tile_count, col_tiles),
        out_shape=[
            jax.ShapeDtypeStruct(block_shape, jnp.float32),
            jax.ShapeDtypeStruct(spread.shape, spread.dtype),
        ],
        in_specs=[pl.BlockSpec(memory_space=pltpu.VMEM)] * 2,
        out_specs=[pl.BlockSpec(memory_space=pltpu.VMEM)] * 2,
        scratch_shapes=[
            pltpu.VMEM(half_shape, row_blocks.dtype),
            pltpu.VMEM(half_shape, row_blocks.dtype),
            pltpu.VMEM(row_blocks.shape, row_blocks.dtype),
            pltpu.VMEM(block_shape, jnp.float32),
            pltpu.VMEM((rep_count // 2,) + block_shape, jnp.float32),
            pltpu.VMEM(block_shape, jnp.float32),
            pltpu.VMEM(spread.shape, spread.dtype),
            pltpu.SemaphoreType.DMA((2,)),
            pltpu.SemaphoreType.DMA((tile_count,)),
            pltpu.SemaphoreType.DMA((tile_count,)),
            pltpu.SemaphoreType.DMA((rep_count // 2,)),
            pltpu.SemaphoreType.DMA((rep_count // 2,)),
            pltpu.SemaphoreType.DMA((2,)),
            pltpu.SemaphoreType.DMA((tile_count,)),
            pltpu.SemaphoreType.DMA((tile_count,)),
            pltpu.SemaphoreType.DMA((2,)),
        ],
        compiler_params=pltpu.CompilerParams(collective_id=2, has_side_effects=True),
    )(row_blocks, spread)


def exchange_kernel(tile_count, col_tiles, tokens_ref, cot_ref, tokens_out, cot_out,
                    tokens_held, cot_held, send_sems, recv_sems, own_sems):
    me = lax.axis_index("rep")
    row = lax.axis_index("ty")
    col = lax.axis_index("tx")
    tile = row * col_tiles + col
    barrier = pltpu.get_barrier_semaphore()

    def tile_peer(step):
        peer = lax.rem(tile + step, tile_count)
        return (me, peer // col_tiles, lax.rem(peer, col_tiles))

    @pl.loop(1, tile_count)
    def _(step):
        pl.semaphore_signal(barrier, inc=1, device_id=tile_peer(step),
                            device_id_type=pl.DeviceIdType.MESH)

    pl.semaphore_wait(barrier, tile_count - 1)

    def tile_copies(step):
        peer = lax.rem(tile + step, tile_count)
        return [
            pltpu.make_async_remote_copy(
                src_ref=source.at[0, peer],
                dst_ref=held.at[tile],
                send_sem=send_sems.at[step, index],
                recv_sem=recv_sems.at[step, index],
                device_id=tile_peer(step),
                device_id_type=pl.DeviceIdType.MESH,
            )
            for index, (source, held) in enumerate(((tokens_ref, tokens_held), (cot_ref, cot_held)))
        ]

    own = [
        pltpu.make_async_copy(tokens_ref.at[0, tile], tokens_held.at[tile], own_sems.at[0]),
        pltpu.make_async_copy(cot_ref.at[0, tile], cot_held.at[tile], own_sems.at[1]),
    ]
    for copy in own:
        copy.start()

    @pl.loop(1, tile_count)
    def _(step):
        for copy in tile_copies(step):
            copy.start()

    for copy in own:
        copy.wait()

    @pl.loop(1, tile_count)
    def _(step):
        for copy in tile_copies(step):
            copy.wait()

    tokens_out[...] = tokens_held[...]
    cot_out[...] = cot_held[...]


def exchange(tokens, cotangent):
    col_tiles = lax.axis_size("tx")
    tile_count = lax.axis_size("ty") * col_tiles
    held_shape = (tile_count,) + tokens.shape[2:]
    return pl.pallas_call(
        functools.partial(exchange_kernel, tile_count, col_tiles),
        out_shape=[jax.ShapeDtypeStruct(held_shape, tokens.dtype)] * 2,
        in_specs=[pl.BlockSpec(memory_space=pltpu.VMEM)] * 2,
        out_specs=[pl.BlockSpec(memory_space=pltpu.VMEM)] * 2,
        scratch_shapes=[
            pltpu.VMEM(held_shape, tokens.dtype),
            pltpu.VMEM(held_shape, tokens.dtype),
            pltpu.SemaphoreType.DMA((tile_count, 2)),
            pltpu.SemaphoreType.DMA((tile_count, 2)),
            pltpu.SemaphoreType.DMA((2,)),
        ],
        compiler_params=pltpu.CompilerParams(collective_id=1, has_side_effects=True),
    )(tokens, cotangent)


def shards(tokens, qkv_weight, cotangent):
    rep_count = lax.axis_size("rep")
    row_tiles = lax.axis_size("ty")
    col_tiles = lax.axis_size("tx")
    tile_count = row_tiles * col_tiles
    tile_height = tokens.shape[1]
    tile_width = tokens.shape[2]
    channels = tokens.shape[3]
    stride_rows = row_tiles * tile_height // GRID
    stride_cols = col_tiles * tile_width // GRID
    block_rows = min(tile_height, stride_rows)
    fold_rows = stride_rows // block_rows
    col_groups = tile_width // stride_cols
    outer_rows = tile_height // block_rows
    inner_rows = block_rows // tile_count
    split_shape = (outer_rows, tile_count, inner_rows, tile_width, channels)
    if tile_height == tile_count and outer_rows == 1 and inner_rows == 1:
        grid_x, grid_g = (
            values.reshape(split_shape) for values in exchange(tokens, cotangent)
        )
    else:
        grid_x, grid_g = (
            lax.all_to_all(
                values.reshape(split_shape), ("ty", "tx"), split_axis=1, concat_axis=1, tiled=True
            )
            for values in (tokens, cotangent)
        )
    token_shape = (
        outer_rows,
        row_tiles // fold_rows,
        fold_rows,
        col_tiles,
        inner_rows,
        col_groups,
        stride_cols,
        channels,
    )
    win_count = fold_rows * inner_rows * stride_cols

    def to_windows(values):
        return (
            values.reshape(token_shape)
            .transpose(2, 4, 6, 1, 0, 3, 5, 7)
            .reshape(win_count, GRID * GRID, channels)
        )

    grad_windows, weight_term = window_grads(to_windows(grid_x), to_windows(grid_g), qkv_weight)
    back_shape = (
        fold_rows,
        inner_rows,
        stride_cols,
        row_tiles // fold_rows,
        outer_rows,
        col_tiles,
        col_groups,
        channels,
    )
    spread = grad_windows.reshape(back_shape).transpose(4, 3, 0, 5, 1, 6, 2, 7).reshape(split_shape)
    row_blocks = weight_term.reshape(tile_count, channels // tile_count, weight_term.shape[1])
    if tile_height == tile_count and outer_rows == 1 and inner_rows == 1:
        weight_grad, returned = paired_sum(
            row_blocks.astype(jnp.bfloat16), spread.reshape((tile_count,) + tokens.shape[2:])
        )
    else:
        returned = lax.all_to_all(spread, ("ty", "tx"), split_axis=1, concat_axis=1, tiled=True)
        gathered = lax.all_to_all(row_blocks.astype(jnp.bfloat16), ("ty", "tx"), 0, 0, tiled=True)
        weight_grad = lax.psum(jnp.sum(gathered.astype(jnp.float32), axis=0), "rep")
        weight_grad = weight_grad / (rep_count * tile_count)
    token_grad = returned.reshape(1, tile_height, tile_width, channels)
    return (token_grad, weight_grad)


def solution(mesh):
    placed = (P("rep", "ty", "tx", None), P(), P("rep", "ty", "tx", None))
    return jax.shard_map(
        shards,
        mesh=mesh,
        in_specs=placed,
        out_specs=(P("rep", "ty", "tx", None), P(("ty", "tx"), None)),
        check_vma=False,
    )
```

```python
import functools

import jax
import jax.numpy as jnp
from jax import lax
from jax.experimental import pallas as pl
from jax.experimental.pallas import tpu as pltpu
from jax.sharding import PartitionSpec as P

HEADS = 16
HEAD_DIM = 32
GRID = 8


eps_norm = 1e-05


def normalize(values):
    center = values - jnp.mean(values, axis=-1, keepdims=True)
    inv_std = lax.rsqrt(jnp.mean(center * center, axis=-1, keepdims=True) + eps_norm)
    return (center * inv_std, inv_std)


def window_grads(window_x, window_g, qkv_weight):
    win_count, win_tokens, channels = window_x.shape
    standard, inv_std = normalize(window_x.astype(jnp.float32))
    normed = standard.astype(jnp.bfloat16).reshape(win_count * win_tokens, channels)
    projection = jnp.dot(normed, qkv_weight, preferred_element_type=jnp.float32)
    flat_shape = (win_count, win_tokens, channels)
    query = (projection[:, :channels] * HEAD_DIM ** (-0.5)).astype(jnp.bfloat16).reshape(flat_shape)
    key = projection[:, channels : 2 * channels].astype(jnp.bfloat16).reshape(flat_shape)
    value = projection[:, 2 * channels :].astype(jnp.bfloat16).reshape(flat_shape)
    grad = window_g.astype(jnp.bfloat16)
    head_mask = (
        lax.broadcasted_iota(jnp.int32, (HEADS, channels), 1) // HEAD_DIM
        == lax.broadcasted_iota(jnp.int32, (HEADS, channels), 0)
    ).astype(jnp.bfloat16)

    def spread(values):
        return values[:, None, :, :] * head_mask[None, :, None, :]

    query_spread = spread(query)
    grad_spread = spread(grad)
    scores = jnp.einsum("wnqc,wkc->wnqk", query_spread, key, preferred_element_type=jnp.float32)
    peak_score = lax.optimization_barrier(jnp.max(scores, axis=-1, keepdims=True))
    exponent = jnp.exp(scores - peak_score)
    attn_probs = exponent / jnp.sum(exponent, axis=-1, keepdims=True)
    probs_low = attn_probs.astype(jnp.bfloat16)
    attn_grad = jnp.einsum("wnqc,wkc->wnqk", grad_spread, value, preferred_element_type=jnp.float32)
    value_grad = jnp.einsum(
        "wnqk,wnqc->wkc", probs_low, grad_spread, preferred_element_type=jnp.float32
    ).astype(jnp.bfloat16)
    score_grad = (
        attn_probs * (attn_grad - jnp.sum(attn_probs * attn_grad, axis=-1, keepdims=True))
    ).astype(jnp.bfloat16)
    key_grad = jnp.einsum(
        "wnqk,wnqc->wkc", score_grad, query_spread, preferred_element_type=jnp.float32
    ).astype(jnp.bfloat16)
    query_full = jnp.einsum("wnqk,wkc->wnqc", score_grad, key, preferred_element_type=jnp.float32)
    query_grad = (
        jnp.sum(query_full * head_mask[None, :, None, :].astype(jnp.float32), axis=1)
        * HEAD_DIM ** (-0.5)
    ).astype(jnp.bfloat16)
    flat_shape = (win_count * win_tokens, channels)
    proj_grad = jnp.concatenate(
        [
            query_grad.reshape(flat_shape),
            key_grad.reshape(flat_shape),
            value_grad.reshape(flat_shape),
        ],
        axis=1,
    )
    normed_grad = lax.dot_general(
        proj_grad, qkv_weight, (((1,), (1,)), ((), ())), preferred_element_type=jnp.float32
    )
    normed_grad = normed_grad.reshape(win_count, win_tokens, channels)
    weight_term = lax.dot_general(
        normed, proj_grad, (((0,), (0,)), ((), ())), preferred_element_type=jnp.float32
    )
    inner_term = (
        normed_grad
        - jnp.mean(normed_grad, axis=-1, keepdims=True)
        - standard * jnp.mean(normed_grad * standard, axis=-1, keepdims=True)
    )
    token_grad = (window_g.astype(jnp.float32) + inv_std * inner_term).astype(jnp.bfloat16)
    return (token_grad, weight_term)


def weight_sum_kernel(rep_count, tile_count, col_tiles, blocks_ref, spread_ref, out_ref,
                      returned_ref, arrived, partial, held, returned_held, send_sems, recv_sems,
                      rep_send_sems, rep_recv_sems, back_send_sems, back_recv_sems, back_own_sem):
    me = lax.axis_index("rep")
    row = lax.axis_index("ty")
    col = lax.axis_index("tx")
    tile = row * col_tiles + col
    barrier = pltpu.get_barrier_semaphore()

    def tile_peer(step):
        peer = lax.rem(tile + step, tile_count)
        return (me, peer // col_tiles, lax.rem(peer, col_tiles))

    def rep_peer(step):
        return (lax.rem(me + step, rep_count), row, col)

    @pl.loop(1, tile_count)
    def _(step):
        pl.semaphore_signal(barrier, inc=1, device_id=tile_peer(step),
                            device_id_type=pl.DeviceIdType.MESH)

    @pl.loop(1, rep_count)
    def _(step):
        pl.semaphore_signal(barrier, inc=1, device_id=rep_peer(step),
                            device_id_type=pl.DeviceIdType.MESH)

    pl.semaphore_wait(barrier, tile_count + rep_count - 2)

    def back_copy(step):
        peer = lax.rem(tile + step, tile_count)
        return pltpu.make_async_remote_copy(
            src_ref=spread_ref.at[peer],
            dst_ref=returned_held.at[tile],
            send_sem=back_send_sems.at[step],
            recv_sem=back_recv_sems.at[step],
            device_id=tile_peer(step),
            device_id_type=pl.DeviceIdType.MESH,
        )

    back_own = pltpu.make_async_copy(spread_ref.at[tile], returned_held.at[tile], back_own_sem.at[0])
    back_own.start()

    @pl.loop(1, tile_count)
    def _(step):
        back_copy(step).start()

    def tile_copy(step):
        peer = lax.rem(tile + step, tile_count)
        return pltpu.make_async_remote_copy(
            src_ref=blocks_ref.at[peer],
            dst_ref=arrived.at[tile],
            send_sem=send_sems.at[step],
            recv_sem=recv_sems.at[step],
            device_id=tile_peer(step),
            device_id_type=pl.DeviceIdType.MESH,
        )

    own = pltpu.make_async_copy(blocks_ref.at[tile], arrived.at[tile], send_sems.at[0])
    own.start()

    @pl.loop(1, tile_count)
    def _(step):
        tile_copy(step).start()

    own.wait()

    @pl.loop(1, tile_count)
    def _(step):
        tile_copy(step).wait()

    def add_source(source, total):
        return total + arrived[source].astype(jnp.float32)

    partial[...] = lax.fori_loop(
        0, tile_count, add_source, jnp.zeros(partial.shape, jnp.float32)
    )
    held[me] = partial[...]

    def rep_copy(step):
        return pltpu.make_async_remote_copy(
            src_ref=partial,
            dst_ref=held.at[me],
            send_sem=rep_send_sems.at[step],
            recv_sem=rep_recv_sems.at[step],
            device_id=rep_peer(step),
            device_id_type=pl.DeviceIdType.MESH,
        )

    @pl.loop(1, rep_count)
    def _(step):
        rep_copy(step).start()

    @pl.loop(1, rep_count)
    def _(step):
        rep_copy(step).wait()

    back_own.wait()

    @pl.loop(1, tile_count)
    def _(step):
        back_copy(step).wait()

    returned_ref[...] = returned_held[...]
    total = held[0]
    for source in range(1, rep_count):
        total = total + held[source]
    out_ref[...] = total


def weight_sum(row_blocks, spread):
    rep_count = lax.axis_size("rep")
    col_tiles = lax.axis_size("tx")
    tile_count = row_blocks.shape[0]
    block_shape = row_blocks.shape[1:]
    return pl.pallas_call(
        functools.partial(weight_sum_kernel, rep_count, tile_count, col_tiles),
        out_shape=[
            jax.ShapeDtypeStruct(block_shape, jnp.float32),
            jax.ShapeDtypeStruct(spread.shape, spread.dtype),
        ],
        in_specs=[pl.BlockSpec(memory_space=pltpu.VMEM)] * 2,
        out_specs=[pl.BlockSpec(memory_space=pltpu.VMEM)] * 2,
        scratch_shapes=[
            pltpu.VMEM(row_blocks.shape, row_blocks.dtype),
            pltpu.VMEM(block_shape, jnp.float32),
            pltpu.VMEM((rep_count,) + block_shape, jnp.float32),
            pltpu.VMEM(spread.shape, spread.dtype),
            pltpu.SemaphoreType.DMA((tile_count,)),
            pltpu.SemaphoreType.DMA((tile_count,)),
            pltpu.SemaphoreType.DMA((rep_count,)),
            pltpu.SemaphoreType.DMA((rep_count,)),
            pltpu.SemaphoreType.DMA((tile_count,)),
            pltpu.SemaphoreType.DMA((tile_count,)),
            pltpu.SemaphoreType.DMA((1,)),
        ],
        compiler_params=pltpu.CompilerParams(collective_id=0, has_side_effects=True),
    )(row_blocks, spread)


def paired_sum_kernel(rep_count, tile_count, col_tiles, blocks_ref, spread_ref, out_ref,
                      returned_ref, pair_held, pair_sum, arrived, partial, held, final,
                      returned_held, pair_sems, tile_send_sems, tile_recv_sems, zh_send_sems,
                      zh_recv_sems, final_sems, back_send_sems, back_recv_sems, own_sems):
    me = lax.axis_index("rep")
    row = lax.axis_index("ty")
    col = lax.axis_index("tx")
    tile = row * col_tiles + col
    core = lax.rem(me, 2)
    plane = me // 2
    planes = rep_count // 2
    partner = me + 1 - 2 * core
    half = tile_count // 2
    mine_start = core * half
    receiver = tile // half == core
    barrier = pltpu.get_barrier_semaphore()

    def tile_device(peer):
        return (me, peer // col_tiles, lax.rem(peer, col_tiles))

    def tile_peer(step):
        return tile_device(lax.rem(tile + step, tile_count))

    def plane_peer(step):
        return (2 * lax.rem(plane + step, planes) + core, row, col)

    mesh_id = pl.DeviceIdType.MESH
    pl.semaphore_signal(barrier, inc=1, device_id=(partner, row, col), device_id_type=mesh_id)

    @pl.loop(1, tile_count)
    def _(step):
        pl.semaphore_signal(barrier, inc=1, device_id=tile_peer(step), device_id_type=mesh_id)

    @pl.when(receiver)
    def _():
        @pl.loop(1, planes)
        def _(step):
            pl.semaphore_signal(barrier, inc=1, device_id=plane_peer(step), device_id_type=mesh_id)

    pl.semaphore_wait(barrier, tile_count + (planes - 1) * receiver.astype(jnp.int32))

    pair_copy = pltpu.make_async_remote_copy(
        src_ref=blocks_ref.at[pl.ds((1 - core) * half, half)],
        dst_ref=pair_held,
        send_sem=pair_sems.at[0],
        recv_sem=pair_sems.at[1],
        device_id=(partner, row, col),
        device_id_type=mesh_id,
    )
    pair_copy.start()

    def back_copy(step):
        peer = lax.rem(tile + step, tile_count)
        return pltpu.make_async_remote_copy(
            src_ref=spread_ref.at[peer],
            dst_ref=returned_held.at[tile],
            send_sem=back_send_sems.at[step],
            recv_sem=back_recv_sems.at[step],
            device_id=tile_peer(step),
            device_id_type=mesh_id,
        )

    back_own = pltpu.make_async_copy(spread_ref.at[tile], returned_held.at[tile], own_sems.at[0])
    back_own.start()

    @pl.loop(1, tile_count)
    def _(step):
        back_copy(step).start()

    pair_copy.wait()

    @pl.loop(0, half)
    def _(index):
        pair_sum[index] = (
            blocks_ref[mine_start + index].astype(jnp.float32)
            + pair_held[index].astype(jnp.float32)
        ).astype(pair_sum.dtype)

    def sum_copy(index):
        target = mine_start + index
        step = lax.rem(target - tile + tile_count, tile_count)
        return pltpu.make_async_remote_copy(
            src_ref=pair_sum.at[index],
            dst_ref=arrived.at[tile],
            send_sem=tile_send_sems.at[step],
            recv_sem=tile_recv_sems.at[step],
            device_id=tile_device(target),
            device_id_type=mesh_id,
        )

    @pl.loop(0, half)
    def _(index):
        @pl.when(mine_start + index != tile)
        def _():
            sum_copy(index).start()

    def final_copy():
        return pltpu.make_async_remote_copy(
            src_ref=final,
            dst_ref=final,
            send_sem=final_sems.at[0],
            recv_sem=final_sems.at[1],
            device_id=(partner, row, col),
            device_id_type=mesh_id,
        )

    @pl.when(receiver)
    def _():
        own = pltpu.make_async_copy(
            pair_sum.at[tile - mine_start], arrived.at[tile], own_sems.at[1]
        )
        own.start()
        own.wait()

        @pl.loop(1, tile_count)
        def _(step):
            pltpu.make_async_remote_copy(
                src_ref=pair_sum.at[0],
                dst_ref=arrived.at[tile],
                send_sem=tile_send_sems.at[step],
                recv_sem=tile_recv_sems.at[step],
                device_id=tile_peer(step),
                device_id_type=mesh_id,
            ).wait_recv()

        def add_source(source, total):
            return total + arrived[source].astype(jnp.float32)

        partial[...] = lax.fori_loop(
            0, tile_count, add_source, jnp.zeros(partial.shape, jnp.float32)
        )
        held[plane] = partial[...]

        def plane_copy(step):
            return pltpu.make_async_remote_copy(
                src_ref=partial,
                dst_ref=held.at[plane],
                send_sem=zh_send_sems.at[step],
                recv_sem=zh_recv_sems.at[step],
                device_id=plane_peer(step),
                device_id_type=mesh_id,
            )

        @pl.loop(1, planes)
        def _(step):
            plane_copy(step).start()

        @pl.loop(1, planes)
        def _(step):
            plane_copy(step).wait()

        total = held[0]
        for source in range(1, planes):
            total = total + held[source]
        final[...] = total
        copy = final_copy()
        copy.start()
        copy.wait_send()

    @pl.when(jnp.logical_not(receiver))
    def _():
        final_copy().wait_recv()

    @pl.loop(0, half)
    def _(index):
        @pl.when(mine_start + index != tile)
        def _():
            sum_copy(index).wait_send()

    back_own.wait()

    @pl.loop(1, tile_count)
    def _(step):
        back_copy(step).wait()

    returned_ref[...] = returned_held[...]
    out_ref[...] = final[...]


def paired_sum(row_blocks, spread):
    rep_count = lax.axis_size("rep")
    col_tiles = lax.axis_size("tx")
    tile_count = row_blocks.shape[0]
    block_shape = row_blocks.shape[1:]
    half_shape = (tile_count // 2,) + block_shape
    return pl.pallas_call(
        functools.partial(paired_sum_kernel, rep_count, tile_count, col_tiles),
        out_shape=[
            jax.ShapeDtypeStruct(block_shape, jnp.float32),
            jax.ShapeDtypeStruct(spread.shape, spread.dtype),
        ],
        in_specs=[pl.BlockSpec(memory_space=pltpu.VMEM)] * 2,
        out_specs=[pl.BlockSpec(memory_space=pltpu.VMEM)] * 2,
        scratch_shapes=[
            pltpu.VMEM(half_shape, row_blocks.dtype),
            pltpu.VMEM(half_shape, row_blocks.dtype),
            pltpu.VMEM(row_blocks.shape, row_blocks.dtype),
            pltpu.VMEM(block_shape, jnp.float32),
            pltpu.VMEM((rep_count // 2,) + block_shape, jnp.float32),
            pltpu.VMEM(block_shape, jnp.float32),
            pltpu.VMEM(spread.shape, spread.dtype),
            pltpu.SemaphoreType.DMA((2,)),
            pltpu.SemaphoreType.DMA((tile_count,)),
            pltpu.SemaphoreType.DMA((tile_count,)),
            pltpu.SemaphoreType.DMA((rep_count // 2,)),
            pltpu.SemaphoreType.DMA((rep_count // 2,)),
            pltpu.SemaphoreType.DMA((2,)),
            pltpu.SemaphoreType.DMA((tile_count,)),
            pltpu.SemaphoreType.DMA((tile_count,)),
            pltpu.SemaphoreType.DMA((2,)),
        ],
        compiler_params=pltpu.CompilerParams(collective_id=2, has_side_effects=True),
    )(row_blocks, spread)


def exchange_kernel(tile_count, col_tiles, tokens_ref, cot_ref, tokens_out, cot_out,
                    tokens_held, cot_held, send_sems, recv_sems, own_sems):
    me = lax.axis_index("rep")
    row = lax.axis_index("ty")
    col = lax.axis_index("tx")
    tile = row * col_tiles + col
    barrier = pltpu.get_barrier_semaphore()

    def tile_peer(step):
        peer = lax.rem(tile + step, tile_count)
        return (me, peer // col_tiles, lax.rem(peer, col_tiles))

    @pl.loop(1, tile_count)
    def _(step):
        pl.semaphore_signal(barrier, inc=1, device_id=tile_peer(step),
                            device_id_type=pl.DeviceIdType.MESH)

    pl.semaphore_wait(barrier, tile_count - 1)

    def tile_copies(step):
        peer = lax.rem(tile + step, tile_count)
        return [
            pltpu.make_async_remote_copy(
                src_ref=source.at[0, peer],
                dst_ref=held.at[tile],
                send_sem=send_sems.at[step, index],
                recv_sem=recv_sems.at[step, index],
                device_id=tile_peer(step),
                device_id_type=pl.DeviceIdType.MESH,
            )
            for index, (source, held) in enumerate(((tokens_ref, tokens_held), (cot_ref, cot_held)))
        ]

    own = [
        pltpu.make_async_copy(tokens_ref.at[0, tile], tokens_held.at[tile], own_sems.at[0]),
        pltpu.make_async_copy(cot_ref.at[0, tile], cot_held.at[tile], own_sems.at[1]),
    ]
    for copy in own:
        copy.start()

    @pl.loop(1, tile_count)
    def _(step):
        for copy in tile_copies(step):
            copy.start()

    for copy in own:
        copy.wait()

    @pl.loop(1, tile_count)
    def _(step):
        for copy in tile_copies(step):
            copy.wait()

    tokens_out[...] = tokens_held[...]
    cot_out[...] = cot_held[...]


def exchange(tokens, cotangent):
    col_tiles = lax.axis_size("tx")
    tile_count = lax.axis_size("ty") * col_tiles
    held_shape = (tile_count,) + tokens.shape[2:]
    return pl.pallas_call(
        functools.partial(exchange_kernel, tile_count, col_tiles),
        out_shape=[jax.ShapeDtypeStruct(held_shape, tokens.dtype)] * 2,
        in_specs=[pl.BlockSpec(memory_space=pltpu.VMEM)] * 2,
        out_specs=[pl.BlockSpec(memory_space=pltpu.VMEM)] * 2,
        scratch_shapes=[
            pltpu.VMEM(held_shape, tokens.dtype),
            pltpu.VMEM(held_shape, tokens.dtype),
            pltpu.SemaphoreType.DMA((tile_count, 2)),
            pltpu.SemaphoreType.DMA((tile_count, 2)),
            pltpu.SemaphoreType.DMA((2,)),
        ],
        compiler_params=pltpu.CompilerParams(collective_id=1, has_side_effects=True),
    )(tokens, cotangent)


def shards(tokens, qkv_weight, cotangent):
    rep_count = lax.axis_size("rep")
    row_tiles = lax.axis_size("ty")
    col_tiles = lax.axis_size("tx")
    tile_count = row_tiles * col_tiles
    tile_height = tokens.shape[1]
    tile_width = tokens.shape[2]
    channels = tokens.shape[3]
    stride_rows = row_tiles * tile_height // GRID
    stride_cols = col_tiles * tile_width // GRID
    block_rows = min(tile_height, stride_rows)
    fold_rows = stride_rows // block_rows
    col_groups = tile_width // stride_cols
    outer_rows = tile_height // block_rows
    inner_rows = block_rows // tile_count
    split_shape = (outer_rows, tile_count, inner_rows, tile_width, channels)
    if tile_height == tile_count and outer_rows == 1 and inner_rows == 1:
        grid_x, grid_g = (
            values.reshape(split_shape) for values in exchange(tokens, cotangent)
        )
    else:
        grid_x, grid_g = (
            lax.all_to_all(
                values.reshape(split_shape), ("ty", "tx"), split_axis=1, concat_axis=1, tiled=True
            )
            for values in (tokens, cotangent)
        )
    token_shape = (
        outer_rows,
        row_tiles // fold_rows,
        fold_rows,
        col_tiles,
        inner_rows,
        col_groups,
        stride_cols,
        channels,
    )
    win_count = fold_rows * inner_rows * stride_cols

    def to_windows(values):
        return (
            values.reshape(token_shape)
            .transpose(2, 4, 6, 1, 0, 3, 5, 7)
            .reshape(win_count, GRID * GRID, channels)
        )

    grad_windows, weight_term = window_grads(to_windows(grid_x), to_windows(grid_g), qkv_weight)
    back_shape = (
        fold_rows,
        inner_rows,
        stride_cols,
        row_tiles // fold_rows,
        outer_rows,
        col_tiles,
        col_groups,
        channels,
    )
    spread = grad_windows.reshape(back_shape).transpose(4, 3, 0, 5, 1, 6, 2, 7).reshape(split_shape)
    row_blocks = weight_term.reshape(tile_count, channels // tile_count, weight_term.shape[1])
    if tile_height == tile_count and outer_rows == 1 and inner_rows == 1:
        weight_grad, returned = paired_sum(
            row_blocks.astype(jnp.bfloat16), spread.reshape((tile_count,) + tokens.shape[2:])
        )
    else:
        returned = lax.all_to_all(spread, ("ty", "tx"), split_axis=1, concat_axis=1, tiled=True)
        gathered = lax.all_to_all(row_blocks.astype(jnp.bfloat16), ("ty", "tx"), 0, 0, tiled=True)
        weight_grad = lax.psum(jnp.sum(gathered.astype(jnp.float32), axis=0), "rep")
    token_grad = returned.reshape(1, tile_height, tile_width, channels)
    weight_grad = weight_grad / (rep_count * tile_count)
    return (token_grad, weight_grad)


def solution(mesh):
    placed = (P("rep", "ty", "tx", None), P(), P("rep", "ty", "tx", None))
    return jax.shard_map(
        shards,
        mesh=mesh,
        in_specs=placed,
        out_specs=(P("rep", "ty", "tx", None), P(("ty", "tx"), None)),
        check_vma=False,
    )
```

```python
import functools

import jax
import jax.numpy as jnp
from jax import lax
from jax.experimental import pallas as pl
from jax.experimental.pallas import tpu as pltpu
from jax.sharding import PartitionSpec as P

HEADS = 16
HEAD_DIM = 32
GRID = 8


eps_norm = 1e-05


def normalize(values):
    center = values - jnp.mean(values, axis=-1, keepdims=True)
    inv_std = lax.rsqrt(jnp.mean(center * center, axis=-1, keepdims=True) + eps_norm)
    return (center * inv_std, inv_std)


def window_grads(window_x, window_g, qkv_weight):
    win_count, win_tokens, channels = window_x.shape
    standard, inv_std = lax.optimization_barrier(normalize(window_x.astype(jnp.float32)))
    normed = standard.astype(jnp.bfloat16).reshape(win_count * win_tokens, channels)
    projection = jnp.dot(normed, qkv_weight, preferred_element_type=jnp.float32)
    flat_shape = (win_count, win_tokens, channels)
    query = (projection[:, :channels] * HEAD_DIM ** (-0.5)).astype(jnp.bfloat16).reshape(flat_shape)
    key = projection[:, channels : 2 * channels].astype(jnp.bfloat16).reshape(flat_shape)
    value = projection[:, 2 * channels :].astype(jnp.bfloat16).reshape(flat_shape)
    grad = window_g.astype(jnp.bfloat16)
    head_mask = (
        lax.broadcasted_iota(jnp.int32, (HEADS, channels), 1) // HEAD_DIM
        == lax.broadcasted_iota(jnp.int32, (HEADS, channels), 0)
    ).astype(jnp.bfloat16)

    def spread(values):
        return values[:, None, :, :] * head_mask[None, :, None, :]

    query_spread = spread(query)
    grad_spread = spread(grad)
    scores = jnp.einsum("wnqc,wkc->wnqk", query_spread, key, preferred_element_type=jnp.float32)
    peak_score = lax.optimization_barrier(jnp.max(scores, axis=-1, keepdims=True))
    exponent = jnp.exp(scores - peak_score)
    attn_probs = exponent / jnp.sum(exponent, axis=-1, keepdims=True)
    probs_low = attn_probs.astype(jnp.bfloat16)
    attn_grad = jnp.einsum("wnqc,wkc->wnqk", grad_spread, value, preferred_element_type=jnp.float32)
    value_grad = jnp.einsum(
        "wnqk,wnqc->wkc", probs_low, grad_spread, preferred_element_type=jnp.float32
    ).astype(jnp.bfloat16)
    score_grad = (
        attn_probs * (attn_grad - jnp.sum(attn_probs * attn_grad, axis=-1, keepdims=True))
    ).astype(jnp.bfloat16)
    key_grad = jnp.einsum(
        "wnqk,wnqc->wkc", score_grad, query_spread, preferred_element_type=jnp.float32
    ).astype(jnp.bfloat16)
    query_full = jnp.einsum("wnqk,wkc->wnqc", score_grad, key, preferred_element_type=jnp.float32)
    query_grad = (
        jnp.sum(query_full * head_mask[None, :, None, :].astype(jnp.float32), axis=1)
        * HEAD_DIM ** (-0.5)
    ).astype(jnp.bfloat16)
    flat_shape = (win_count * win_tokens, channels)
    proj_grad = jnp.concatenate(
        [
            query_grad.reshape(flat_shape),
            key_grad.reshape(flat_shape),
            value_grad.reshape(flat_shape),
        ],
        axis=1,
    )
    normed_grad = lax.dot_general(
        proj_grad, qkv_weight, (((1,), (1,)), ((), ())), preferred_element_type=jnp.float32
    )
    normed_grad = normed_grad.reshape(win_count, win_tokens, channels)
    weight_term = lax.dot_general(
        normed, proj_grad, (((0,), (0,)), ((), ())), preferred_element_type=jnp.float32
    )
    inner_term = (
        normed_grad
        - jnp.mean(normed_grad, axis=-1, keepdims=True)
        - standard * jnp.mean(normed_grad * standard, axis=-1, keepdims=True)
    )
    token_grad = (window_g.astype(jnp.float32) + inv_std * inner_term).astype(jnp.bfloat16)
    return (token_grad, weight_term)


def weight_sum_kernel(rep_count, tile_count, col_tiles, blocks_ref, spread_ref, out_ref,
                      returned_ref, arrived, partial, held, returned_held, send_sems, recv_sems,
                      rep_send_sems, rep_recv_sems, back_send_sems, back_recv_sems, back_own_sem):
    me = lax.axis_index("rep")
    row = lax.axis_index("ty")
    col = lax.axis_index("tx")
    tile = row * col_tiles + col
    barrier = pltpu.get_barrier_semaphore()

    def tile_peer(step):
        peer = lax.rem(tile + step, tile_count)
        return (me, peer // col_tiles, lax.rem(peer, col_tiles))

    def rep_peer(step):
        return (lax.rem(me + step, rep_count), row, col)

    @pl.loop(1, tile_count)
    def _(step):
        pl.semaphore_signal(barrier, inc=1, device_id=tile_peer(step),
                            device_id_type=pl.DeviceIdType.MESH)

    @pl.loop(1, rep_count)
    def _(step):
        pl.semaphore_signal(barrier, inc=1, device_id=rep_peer(step),
                            device_id_type=pl.DeviceIdType.MESH)

    pl.semaphore_wait(barrier, tile_count + rep_count - 2)

    def back_copy(step):
        peer = lax.rem(tile + step, tile_count)
        return pltpu.make_async_remote_copy(
            src_ref=spread_ref.at[peer],
            dst_ref=returned_held.at[tile],
            send_sem=back_send_sems.at[step],
            recv_sem=back_recv_sems.at[step],
            device_id=tile_peer(step),
            device_id_type=pl.DeviceIdType.MESH,
        )

    back_own = pltpu.make_async_copy(spread_ref.at[tile], returned_held.at[tile], back_own_sem.at[0])
    back_own.start()

    @pl.loop(1, tile_count)
    def _(step):
        back_copy(step).start()

    def tile_copy(step):
        peer = lax.rem(tile + step, tile_count)
        return pltpu.make_async_remote_copy(
            src_ref=blocks_ref.at[peer],
            dst_ref=arrived.at[tile],
            send_sem=send_sems.at[step],
            recv_sem=recv_sems.at[step],
            device_id=tile_peer(step),
            device_id_type=pl.DeviceIdType.MESH,
        )

    own = pltpu.make_async_copy(blocks_ref.at[tile], arrived.at[tile], send_sems.at[0])
    own.start()

    @pl.loop(1, tile_count)
    def _(step):
        tile_copy(step).start()

    own.wait()

    @pl.loop(1, tile_count)
    def _(step):
        tile_copy(step).wait()

    def add_source(source, total):
        return total + arrived[source].astype(jnp.float32)

    partial[...] = lax.fori_loop(
        0, tile_count, add_source, jnp.zeros(partial.shape, jnp.float32)
    )
    held[me] = partial[...]

    def rep_copy(step):
        return pltpu.make_async_remote_copy(
            src_ref=partial,
            dst_ref=held.at[me],
            send_sem=rep_send_sems.at[step],
            recv_sem=rep_recv_sems.at[step],
            device_id=rep_peer(step),
            device_id_type=pl.DeviceIdType.MESH,
        )

    @pl.loop(1, rep_count)
    def _(step):
        rep_copy(step).start()

    @pl.loop(1, rep_count)
    def _(step):
        rep_copy(step).wait()

    back_own.wait()

    @pl.loop(1, tile_count)
    def _(step):
        back_copy(step).wait()

    returned_ref[...] = returned_held[...]
    total = held[0]
    for source in range(1, rep_count):
        total = total + held[source]
    out_ref[...] = total


def weight_sum(row_blocks, spread):
    rep_count = lax.axis_size("rep")
    col_tiles = lax.axis_size("tx")
    tile_count = row_blocks.shape[0]
    block_shape = row_blocks.shape[1:]
    return pl.pallas_call(
        functools.partial(weight_sum_kernel, rep_count, tile_count, col_tiles),
        out_shape=[
            jax.ShapeDtypeStruct(block_shape, jnp.float32),
            jax.ShapeDtypeStruct(spread.shape, spread.dtype),
        ],
        in_specs=[pl.BlockSpec(memory_space=pltpu.VMEM)] * 2,
        out_specs=[pl.BlockSpec(memory_space=pltpu.VMEM)] * 2,
        scratch_shapes=[
            pltpu.VMEM(row_blocks.shape, row_blocks.dtype),
            pltpu.VMEM(block_shape, jnp.float32),
            pltpu.VMEM((rep_count,) + block_shape, jnp.float32),
            pltpu.VMEM(spread.shape, spread.dtype),
            pltpu.SemaphoreType.DMA((tile_count,)),
            pltpu.SemaphoreType.DMA((tile_count,)),
            pltpu.SemaphoreType.DMA((rep_count,)),
            pltpu.SemaphoreType.DMA((rep_count,)),
            pltpu.SemaphoreType.DMA((tile_count,)),
            pltpu.SemaphoreType.DMA((tile_count,)),
            pltpu.SemaphoreType.DMA((1,)),
        ],
        compiler_params=pltpu.CompilerParams(collective_id=0, has_side_effects=True),
    )(row_blocks, spread)


def paired_sum_kernel(rep_count, tile_count, col_tiles, blocks_ref, spread_ref, out_ref,
                      returned_ref, pair_held, pair_sum, arrived, partial, held, final,
                      returned_held, pair_sems, tile_send_sems, tile_recv_sems, zh_send_sems,
                      zh_recv_sems, final_sems, back_send_sems, back_recv_sems, own_sems):
    me = lax.axis_index("rep")
    row = lax.axis_index("ty")
    col = lax.axis_index("tx")
    tile = row * col_tiles + col
    core = lax.rem(me, 2)
    plane = me // 2
    planes = rep_count // 2
    partner = me + 1 - 2 * core
    half = tile_count // 2
    mine_start = core * half
    receiver = tile // half == core
    barrier = pltpu.get_barrier_semaphore()

    def tile_device(peer):
        return (me, peer // col_tiles, lax.rem(peer, col_tiles))

    def tile_peer(step):
        return tile_device(lax.rem(tile + step, tile_count))

    def plane_peer(step):
        return (2 * lax.rem(plane + step, planes) + core, row, col)

    mesh_id = pl.DeviceIdType.MESH
    pl.semaphore_signal(barrier, inc=1, device_id=(partner, row, col), device_id_type=mesh_id)

    @pl.loop(1, tile_count)
    def _(step):
        pl.semaphore_signal(barrier, inc=1, device_id=tile_peer(step), device_id_type=mesh_id)

    @pl.when(receiver)
    def _():
        @pl.loop(1, planes)
        def _(step):
            pl.semaphore_signal(barrier, inc=1, device_id=plane_peer(step), device_id_type=mesh_id)

    pl.semaphore_wait(barrier, tile_count + (planes - 1) * receiver.astype(jnp.int32))

    pair_copy = pltpu.make_async_remote_copy(
        src_ref=blocks_ref.at[pl.ds((1 - core) * half, half)],
        dst_ref=pair_held,
        send_sem=pair_sems.at[0],
        recv_sem=pair_sems.at[1],
        device_id=(partner, row, col),
        device_id_type=mesh_id,
    )
    pair_copy.start()

    def back_copy(step):
        peer = lax.rem(tile + step, tile_count)
        return pltpu.make_async_remote_copy(
            src_ref=spread_ref.at[peer],
            dst_ref=returned_held.at[tile],
            send_sem=back_send_sems.at[step],
            recv_sem=back_recv_sems.at[step],
            device_id=tile_peer(step),
            device_id_type=mesh_id,
        )

    back_own = pltpu.make_async_copy(spread_ref.at[tile], returned_held.at[tile], own_sems.at[0])
    back_own.start()

    @pl.loop(1, tile_count)
    def _(step):
        back_copy(step).start()

    pair_copy.wait()

    @pl.loop(0, half)
    def _(index):
        pair_sum[index] = (
            blocks_ref[mine_start + index].astype(jnp.float32)
            + pair_held[index].astype(jnp.float32)
        ).astype(pair_sum.dtype)

    def sum_copy(index):
        target = mine_start + index
        step = lax.rem(target - tile + tile_count, tile_count)
        return pltpu.make_async_remote_copy(
            src_ref=pair_sum.at[index],
            dst_ref=arrived.at[tile],
            send_sem=tile_send_sems.at[step],
            recv_sem=tile_recv_sems.at[step],
            device_id=tile_device(target),
            device_id_type=mesh_id,
        )

    @pl.loop(0, half)
    def _(index):
        @pl.when(mine_start + index != tile)
        def _():
            sum_copy(index).start()

    def final_copy():
        return pltpu.make_async_remote_copy(
            src_ref=final,
            dst_ref=final,
            send_sem=final_sems.at[0],
            recv_sem=final_sems.at[1],
            device_id=(partner, row, col),
            device_id_type=mesh_id,
        )

    @pl.when(receiver)
    def _():
        own = pltpu.make_async_copy(
            pair_sum.at[tile - mine_start], arrived.at[tile], own_sems.at[1]
        )
        own.start()
        own.wait()

        @pl.loop(1, tile_count)
        def _(step):
            pltpu.make_async_remote_copy(
                src_ref=pair_sum.at[0],
                dst_ref=arrived.at[tile],
                send_sem=tile_send_sems.at[step],
                recv_sem=tile_recv_sems.at[step],
                device_id=tile_peer(step),
                device_id_type=mesh_id,
            ).wait_recv()

        def add_source(source, total):
            return total + arrived[source].astype(jnp.float32)

        partial[...] = lax.fori_loop(
            0, tile_count, add_source, jnp.zeros(partial.shape, jnp.float32)
        )
        held[plane] = partial[...]

        def plane_copy(step):
            return pltpu.make_async_remote_copy(
                src_ref=partial,
                dst_ref=held.at[plane],
                send_sem=zh_send_sems.at[step],
                recv_sem=zh_recv_sems.at[step],
                device_id=plane_peer(step),
                device_id_type=mesh_id,
            )

        @pl.loop(1, planes)
        def _(step):
            plane_copy(step).start()

        @pl.loop(1, planes)
        def _(step):
            plane_copy(step).wait()

        total = held[0]
        for source in range(1, planes):
            total = total + held[source]
        final[...] = total
        copy = final_copy()
        copy.start()
        copy.wait_send()

    @pl.when(jnp.logical_not(receiver))
    def _():
        final_copy().wait_recv()

    @pl.loop(0, half)
    def _(index):
        @pl.when(mine_start + index != tile)
        def _():
            sum_copy(index).wait_send()

    back_own.wait()

    @pl.loop(1, tile_count)
    def _(step):
        back_copy(step).wait()

    returned_ref[...] = returned_held[...]
    out_ref[...] = final[...]


def paired_sum(row_blocks, spread):
    rep_count = lax.axis_size("rep")
    col_tiles = lax.axis_size("tx")
    tile_count = row_blocks.shape[0]
    block_shape = row_blocks.shape[1:]
    half_shape = (tile_count // 2,) + block_shape
    return pl.pallas_call(
        functools.partial(paired_sum_kernel, rep_count, tile_count, col_tiles),
        out_shape=[
            jax.ShapeDtypeStruct(block_shape, jnp.float32),
            jax.ShapeDtypeStruct(spread.shape, spread.dtype),
        ],
        in_specs=[pl.BlockSpec(memory_space=pltpu.VMEM)] * 2,
        out_specs=[pl.BlockSpec(memory_space=pltpu.VMEM)] * 2,
        scratch_shapes=[
            pltpu.VMEM(half_shape, row_blocks.dtype),
            pltpu.VMEM(half_shape, row_blocks.dtype),
            pltpu.VMEM(row_blocks.shape, row_blocks.dtype),
            pltpu.VMEM(block_shape, jnp.float32),
            pltpu.VMEM((rep_count // 2,) + block_shape, jnp.float32),
            pltpu.VMEM(block_shape, jnp.float32),
            pltpu.VMEM(spread.shape, spread.dtype),
            pltpu.SemaphoreType.DMA((2,)),
            pltpu.SemaphoreType.DMA((tile_count,)),
            pltpu.SemaphoreType.DMA((tile_count,)),
            pltpu.SemaphoreType.DMA((rep_count // 2,)),
            pltpu.SemaphoreType.DMA((rep_count // 2,)),
            pltpu.SemaphoreType.DMA((2,)),
            pltpu.SemaphoreType.DMA((tile_count,)),
            pltpu.SemaphoreType.DMA((tile_count,)),
            pltpu.SemaphoreType.DMA((2,)),
        ],
        compiler_params=pltpu.CompilerParams(collective_id=2, has_side_effects=True),
    )(row_blocks, spread)


def exchange_kernel(tile_count, col_tiles, tokens_ref, cot_ref, tokens_out, cot_out,
                    tokens_held, cot_held, send_sems, recv_sems, own_sems):
    me = lax.axis_index("rep")
    row = lax.axis_index("ty")
    col = lax.axis_index("tx")
    tile = row * col_tiles + col
    barrier = pltpu.get_barrier_semaphore()

    def tile_peer(step):
        peer = lax.rem(tile + step, tile_count)
        return (me, peer // col_tiles, lax.rem(peer, col_tiles))

    @pl.loop(1, tile_count)
    def _(step):
        pl.semaphore_signal(barrier, inc=1, device_id=tile_peer(step),
                            device_id_type=pl.DeviceIdType.MESH)

    pl.semaphore_wait(barrier, tile_count - 1)

    def tile_copies(step):
        peer = lax.rem(tile + step, tile_count)
        return [
            pltpu.make_async_remote_copy(
                src_ref=source.at[0, peer],
                dst_ref=held.at[tile],
                send_sem=send_sems.at[step, index],
                recv_sem=recv_sems.at[step, index],
                device_id=tile_peer(step),
                device_id_type=pl.DeviceIdType.MESH,
            )
            for index, (source, held) in enumerate(((tokens_ref, tokens_held), (cot_ref, cot_held)))
        ]

    own = [
        pltpu.make_async_copy(tokens_ref.at[0, tile], tokens_held.at[tile], own_sems.at[0]),
        pltpu.make_async_copy(cot_ref.at[0, tile], cot_held.at[tile], own_sems.at[1]),
    ]
    for copy in own:
        copy.start()

    @pl.loop(1, tile_count)
    def _(step):
        for copy in tile_copies(step):
            copy.start()

    for copy in own:
        copy.wait()

    @pl.loop(1, tile_count)
    def _(step):
        for copy in tile_copies(step):
            copy.wait()

    tokens_out[...] = tokens_held[...]
    cot_out[...] = cot_held[...]


def exchange(tokens, cotangent):
    col_tiles = lax.axis_size("tx")
    tile_count = lax.axis_size("ty") * col_tiles
    held_shape = (tile_count,) + tokens.shape[2:]
    return pl.pallas_call(
        functools.partial(exchange_kernel, tile_count, col_tiles),
        out_shape=[jax.ShapeDtypeStruct(held_shape, tokens.dtype)] * 2,
        in_specs=[pl.BlockSpec(memory_space=pltpu.VMEM)] * 2,
        out_specs=[pl.BlockSpec(memory_space=pltpu.VMEM)] * 2,
        scratch_shapes=[
            pltpu.VMEM(held_shape, tokens.dtype),
            pltpu.VMEM(held_shape, tokens.dtype),
            pltpu.SemaphoreType.DMA((tile_count, 2)),
            pltpu.SemaphoreType.DMA((tile_count, 2)),
            pltpu.SemaphoreType.DMA((2,)),
        ],
        compiler_params=pltpu.CompilerParams(collective_id=1, has_side_effects=True),
    )(tokens, cotangent)


def shards(tokens, qkv_weight, cotangent):
    rep_count = lax.axis_size("rep")
    row_tiles = lax.axis_size("ty")
    col_tiles = lax.axis_size("tx")
    tile_count = row_tiles * col_tiles
    tile_height = tokens.shape[1]
    tile_width = tokens.shape[2]
    channels = tokens.shape[3]
    stride_rows = row_tiles * tile_height // GRID
    stride_cols = col_tiles * tile_width // GRID
    block_rows = min(tile_height, stride_rows)
    fold_rows = stride_rows // block_rows
    col_groups = tile_width // stride_cols
    outer_rows = tile_height // block_rows
    inner_rows = block_rows // tile_count
    split_shape = (outer_rows, tile_count, inner_rows, tile_width, channels)
    if tile_height == tile_count and outer_rows == 1 and inner_rows == 1:
        grid_x, grid_g = (
            values.reshape(split_shape) for values in exchange(tokens, cotangent)
        )
    else:
        grid_x, grid_g = (
            lax.all_to_all(
                values.reshape(split_shape), ("ty", "tx"), split_axis=1, concat_axis=1, tiled=True
            )
            for values in (tokens, cotangent)
        )
    token_shape = (
        outer_rows,
        row_tiles // fold_rows,
        fold_rows,
        col_tiles,
        inner_rows,
        col_groups,
        stride_cols,
        channels,
    )
    win_count = fold_rows * inner_rows * stride_cols

    def to_windows(values):
        return (
            values.reshape(token_shape)
            .transpose(2, 4, 6, 1, 0, 3, 5, 7)
            .reshape(win_count, GRID * GRID, channels)
        )

    window_x, window_g = lax.optimization_barrier((to_windows(grid_x), to_windows(grid_g)))
    grad_windows, weight_term = window_grads(window_x, window_g, qkv_weight)
    back_shape = (
        fold_rows,
        inner_rows,
        stride_cols,
        row_tiles // fold_rows,
        outer_rows,
        col_tiles,
        col_groups,
        channels,
    )
    spread = grad_windows.reshape(back_shape).transpose(4, 3, 0, 5, 1, 6, 2, 7).reshape(split_shape)
    row_blocks = weight_term.reshape(tile_count, channels // tile_count, weight_term.shape[1])
    if tile_height == tile_count and outer_rows == 1 and inner_rows == 1:
        weight_grad, returned = paired_sum(
            row_blocks.astype(jnp.bfloat16), spread.reshape((tile_count,) + tokens.shape[2:])
        )
    else:
        returned = lax.all_to_all(spread, ("ty", "tx"), split_axis=1, concat_axis=1, tiled=True)
        gathered = lax.all_to_all(row_blocks.astype(jnp.bfloat16), ("ty", "tx"), 0, 0, tiled=True)
        weight_grad = lax.psum(jnp.sum(gathered.astype(jnp.float32), axis=0), "rep")
    token_grad = returned.reshape(1, tile_height, tile_width, channels)
    weight_grad = weight_grad / (rep_count * tile_count)
    return (token_grad, weight_grad)


def solution(mesh):
    placed = (P("rep", "ty", "tx", None), P(), P("rep", "ty", "tx", None))
    return jax.shard_map(
        shards,
        mesh=mesh,
        in_specs=placed,
        out_specs=(P("rep", "ty", "tx", None), P(("ty", "tx"), None)),
        check_vma=False,
    )
```
